256 devices in a mesh: space: 64 (over y, x, z_hi, core), batch: 4 (over z_lo).
Axes of the slice: x: 4, y: 4, z: 8 (z_hi: 2, z_lo: 4; z = z_hi * 4 + z_lo), core: 2. Of those that a mesh axis runs over, the one named last changes fastest.
Arguments:
- fields: bfloat16 [4, 64, 32, 32, 256], P('batch', 'space'), may hold values from -6 to 6
- cotangent: bfloat16 [4, 64, 32, 32, 256], P('batch', 'space'), may hold values from -6 to 6
- dw_kernel: float32 [9, 256], replicated, may hold values from -2 to 2
- dw_bias: float32 [256], replicated, may hold values from -3 to 3
- ln_gain: float32 [256], replicated, may hold values from 0.1 to 1.9
- ln_shift: float32 [256], replicated, may hold values from -1.8 to 1.8
- w_in: bfloat16 [256, 1024], replicated, may hold values from -0.375 to 0.375
- b_in: float32 [1024], replicated, may hold values from -3 to 3
- w_out: bfloat16 [1024, 256], replicated, may hold values from -0.1875 to 0.1875
- b_out: float32 [256], replicated, may hold values from -3 to 3
- seam_links: int32 [64, 4], replicated, may hold values from 0 to 511, as said below
- corner_links: int32 [64, 4], replicated, may hold values from 0 to 255, as said below
Outputs:
- blocks: bfloat16 [4, 64, 32, 32, 256], P('batch', 'space')
- grad_fields: bfloat16 [4, 64, 32, 32, 256], P('batch', 'space')
- grad_kernel: float32 [9, 256], replicated
- grad_channels: float32 [4, 256], replicated
- grad_w_in: float32 [256, 1024], replicated
- grad_b_in: float32 [1024], replicated
- grad_w_out: float32 [1024, 256], replicated
The draws below stay inside these ranges and needn't reach their ends.
Inputs may be any that keep to these rules, and one draw needn't show every extreme that they name: seam_links[t, e] = 8 p + 2 f + r: edge e of tile t meets edge f of tile p, reversed if r = 1. The relation is symmetric: seam_links[p, f] = 8 t + 2 e + r. The four edges of a tile meet four different tiles, none of them the tile itself. corner_links[t, k] = 4 p + j: the cell beyond corner k of tile t is corner cell j of tile p, and corner_links[p, j] = 4 t + k.
All inputs are finite; a program needn't handle non-finite values.
Results may differ from the reference program's by a relative error of at most 0.006.
Values may be sent and summed in bfloat16 or wider, within the bound.
No kernel may reach another device: no remote copies, remote signals or barrier semaphores. Data moves between devices by JAX's collectives and lax.ppermute only.
A program may use at most 64 MiB of HBM per device.

```python
import jax
import jax.numpy as jnp
from jax import lax

C = 256
H = 1024
S = 32
TILES = 64
SAMPLES = 4


def tile_torus(key):
    base = jax.random.fold_in(key, 4242)
    keys = jax.random.split(base, 4)
    placement = jax.random.permutation(keys[0], TILES).astype(jnp.int32)
    stride = jax.random.randint(keys[1], (), 3, TILES // 2).astype(jnp.int32)
    vertical = jax.random.randint(keys[2], (TILES,), 0, 2).astype(jnp.int32)
    across = jax.random.randint(keys[3], (TILES,), 0, 2).astype(jnp.int32)
    position = jnp.arange(TILES, dtype=jnp.int32)
    lower_owner = placement[(position + stride) % TILES]
    vertical = jnp.where(lower_owner == 0, 0, vertical).astype(jnp.int32)
    across = jnp.where(placement == TILES - 1, 1, across).astype(jnp.int32)
    return (placement, stride, vertical, across)


def draw_seam_links(key, part):
    placement, stride, vertical, across = tile_torus(key)
    position = jnp.arange(TILES, dtype=jnp.int32)
    upper = (position - stride) % TILES
    lower = (position + stride) % TILES
    before = (position - 1) % TILES
    after = (position + 1) % TILES
    table_rows = jnp.stack([placement[upper] * 8 + 2 + vertical[upper], placement[lower] * 8 + vertical, placement[before] * 8 + 6 + across[before], placement[after] * 8 + 4 + across], axis=1)
    return jnp.zeros((TILES, 4), jnp.int32).at[placement].set(table_rows)


def draw_corner_links(key, part):
    placement, stride, vertical, across = tile_torus(key)
    position = jnp.arange(TILES, dtype=jnp.int32)
    table_rows = jnp.stack([placement[(position - stride - 1) % TILES] * 4 + 3, placement[(position - stride + 1) % TILES] * 4 + 2, placement[(position + stride - 1) % TILES] * 4 + 1, placement[(position + stride + 1) % TILES] * 4], axis=1)
    return jnp.zeros((TILES, 4), jnp.int32).at[placement].set(table_rows)


def level_of(rng, shape, shards, least, high):
    factor_of = 1.0
    for dim, shards_of in shards:
        draws = jax.random.uniform(jax.random.fold_in(jax.random.fold_in(rng, 6), dim), (shards_of,), jnp.float32, least / len(shards), high / len(shards))
        factor_of = factor_of * jnp.repeat(jnp.exp(draws), shape[dim] // shards_of).reshape((-1,) + (1,) * (len(shape) - 1 - dim))
    return factor_of


def scatter_about(stream_key, dims, spread, limit, cuts=(), kind=jnp.bfloat16):
    values = spread * jax.random.normal(stream_key, dims, jnp.float32)
    if cuts:
        values = values * level_of(stream_key, dims, cuts, -0.22, 0.18)
    return jnp.clip(values, -limit, limit).astype(kind)


def setup_inputs(seed: int = 0) -> dict:
    arg_keys = jax.random.split(jax.random.key(seed), 13)
    return {
        "fields": scatter_about(arg_keys[0], (SAMPLES, TILES, S, S, C), 1.0, 6.0, ((0, 4), (1, 64))),
        "cotangent": scatter_about(arg_keys[1], (SAMPLES, TILES, S, S, C), 1.0, 6.0, ((0, 4), (1, 64))),
        "dw_kernel": scatter_about(arg_keys[2], (9, C), 0.33, 2.0, (), jnp.float32),
        "dw_bias": scatter_about(arg_keys[3], (C,), 0.5, 3.0, (), jnp.float32),
        "ln_gain": jnp.clip(1.0 + 0.18 * jax.random.normal(arg_keys[4], (C,), jnp.float32), 0.1, 1.9),
        "ln_shift": scatter_about(arg_keys[5], (C,), 0.3, 1.8, (), jnp.float32),
        "w_in": scatter_about(arg_keys[6], (C, H), C ** -0.5, 0.375),
        "b_in": scatter_about(arg_keys[7], (H,), 0.5, 3.0, (), jnp.float32),
        "w_out": scatter_about(arg_keys[8], (H, C), H ** -0.5, 0.1875),
        "b_out": scatter_about(arg_keys[9], (C,), 0.5, 3.0, (), jnp.float32),
        "seam_links": draw_seam_links(jax.random.fold_in(arg_keys[12], 71), 0),
        "corner_links": draw_corner_links(jax.random.fold_in(arg_keys[12], 71), 0),
    }


def edge_parts(tile_fields):
    strips = jnp.stack([tile_fields[:, 0], tile_fields[:, -1], tile_fields[:, :, 0], tile_fields[:, :, -1]], axis=1)
    corner_cells = jnp.stack([tile_fields[:, 0, 0], tile_fields[:, 0, -1], tile_fields[:, -1, 0], tile_fields[:, -1, -1]], axis=1)
    return (strips, corner_cells)

def assemble(center, halo_strips, halo_cells):
    top_line = jnp.concatenate([halo_cells[0][None], halo_strips[0], halo_cells[1][None]], axis=0)
    bottom_line = jnp.concatenate([halo_cells[2][None], halo_strips[1], halo_cells[3][None]], axis=0)
    middle = jnp.concatenate([halo_strips[2][:, None], center, halo_strips[3][:, None]], axis=1)
    return jnp.concatenate([top_line[None], middle, bottom_line[None]], axis=0)

def halo_pad(tile_fields, seam_links, corner_links):
    strips, corner_cells = edge_parts(tile_fields)
    owners = seam_links // 8
    partner_edge = seam_links // 2 % 4
    reverse = seam_links % 2
    picked = strips[owners, partner_edge]
    picked = jnp.where((reverse == 1)[:, :, None, None], picked[:, :, ::-1], picked)
    picked_cells = corner_cells[corner_links // 4, corner_links % 4]
    return jax.vmap(assemble)(tile_fields, picked, picked_cells)

def tile_step(padded, tile_field, tile_cot, dw_kernel, dw_bias, ln_gain, ln_shift, w_in, b_in, w_out, b_out):
    extent = tile_field.shape[0]
    channels = tile_field.shape[2]
    conv_out = jnp.zeros((extent, extent, channels), jnp.float32) + dw_bias
    for k in range(9):
        conv_out = conv_out + padded[k // 3:k // 3 + extent, k % 3:k % 3 + extent] * dw_kernel[k]
    conv_rows = conv_out.reshape(extent * extent, channels)
    centred = conv_rows - lax.optimization_barrier(jnp.mean(conv_rows, axis=1, keepdims=True))
    inv_std = 1.0 / jnp.sqrt(lax.optimization_barrier(jnp.mean(centred * centred, axis=1, keepdims=True)) + 1e-06)
    x_hat = centred * inv_std
    normed = (x_hat * ln_gain + ln_shift).astype(jnp.bfloat16)
    hidden = jnp.dot(normed, w_in, preferred_element_type=jnp.float32) + b_in
    active = jax.nn.gelu(hidden).astype(jnp.bfloat16)
    field_rows = tile_field.reshape(extent * extent, channels).astype(jnp.float32)
    blocks_out = (field_rows + jnp.dot(active, w_out, preferred_element_type=jnp.float32) + b_out).astype(jnp.bfloat16)
    cot_rows = tile_cot.reshape(extent * extent, channels)
    g_b_out = lax.optimization_barrier(jnp.sum(cot_rows.astype(jnp.float32), axis=0))
    g_w_out = lax.dot_general(active, cot_rows, (((0,), (0,)), ((), ())), preferred_element_type=jnp.float32)
    d_act = lax.dot_general(cot_rows, w_out, (((1,), (1,)), ((), ())), preferred_element_type=jnp.float32)
    d_hidden = jax.vjp(jax.nn.gelu, hidden)[1](d_act)[0].astype(jnp.bfloat16)
    g_b_in = lax.optimization_barrier(jnp.sum(d_hidden.astype(jnp.float32), axis=0))
    g_w_in = lax.dot_general(normed, d_hidden, (((0,), (0,)), ((), ())), preferred_element_type=jnp.float32)
    d_normed = lax.dot_general(d_hidden, w_in, (((1,), (1,)), ((), ())), preferred_element_type=jnp.float32)
    g_gain = lax.optimization_barrier(jnp.sum(d_normed * x_hat, axis=0))
    g_shift = lax.optimization_barrier(jnp.sum(d_normed, axis=0))
    d_unit = d_normed * ln_gain
    d_conv = inv_std * (d_unit - lax.optimization_barrier(jnp.mean(d_unit, axis=1, keepdims=True)) - x_hat * lax.optimization_barrier(jnp.mean(d_unit * x_hat, axis=1, keepdims=True)))
    d_conv_wide = d_conv.astype(jnp.bfloat16).astype(jnp.float32).reshape(extent, extent, channels)
    g_bias = lax.optimization_barrier(jnp.sum(d_conv_wide, axis=(0, 1)))
    kernel_rows = []
    d_padded = jnp.zeros((extent + 2, extent + 2, channels), jnp.float32)
    for k in range(9):
        window = padded[k // 3:k // 3 + extent, k % 3:k % 3 + extent].astype(jnp.float32)
        kernel_rows.append(lax.optimization_barrier(jnp.sum(window * d_conv_wide, axis=(0, 1))))
        d_padded = d_padded.at[k // 3:k // 3 + extent, k % 3:k % 3 + extent].add(dw_kernel[k] * d_conv_wide)
    grads = (jnp.stack(kernel_rows), jnp.stack([g_bias, g_gain, g_shift, g_b_out]), g_w_in, g_b_in, g_w_out)
    return (blocks_out.reshape(extent, extent, channels), d_padded, grads)

def reference(fields, cotangent, dw_kernel, dw_bias, ln_gain, ln_shift, w_in, b_in, w_out, b_out, seam_links, corner_links):
    initial = (jnp.zeros((9, C), jnp.float32), jnp.zeros((4, C), jnp.float32), jnp.zeros((C, H), jnp.float32), jnp.zeros((H,), jnp.float32), jnp.zeros((H, C), jnp.float32))

    def one_sample(carry, inputs):
        sample_fields, sample_cot = inputs
        wide = sample_fields.astype(jnp.float32)
        padded = halo_pad(wide, seam_links, corner_links)

        def one_tile(inner, item):
            tile_pad, tile_field, tile_cot = item
            blocks_out, d_padded, grads = tile_step(tile_pad, tile_field, tile_cot, dw_kernel, dw_bias, ln_gain, ln_shift, w_in, b_in, w_out, b_out)
            return (jax.tree.map(lambda a, b: a + b, inner, grads), (blocks_out, d_padded))
        carry, (outs, d_pads) = lax.scan(one_tile, carry, (padded, sample_fields, sample_cot))
        interior = d_pads[:, 1:-1, 1:-1]
        rim_part = d_pads.at[:, 1:-1, 1:-1].set(0.0)
        rim_part = lax.optimization_barrier(rim_part.astype(jnp.bfloat16)).astype(jnp.float32)
        pulled = jax.vjp(lambda f: halo_pad(f, seam_links, corner_links), wide)[1](rim_part)[0]
        grad_out = (sample_cot.astype(jnp.float32) + interior + pulled).astype(jnp.bfloat16)
        return (carry, (outs, grad_out))
    grads, (blocks, grad_fields) = lax.scan(one_sample, initial, (fields, cotangent))
    squares = jnp.float32(0.0)
    entries = 0
    for piece in grads:
        squares = squares + jnp.sum(piece * piece)
        entries = entries + piece.size
    scale = 1.0 / jnp.sqrt(squares / entries + 1e-06)
    return (blocks, grad_fields, grads[0] * scale, grads[1] * scale, grads[2] * scale, grads[3] * scale, grads[4] * scale)
```

```python
import functools

import jax
import jax.numpy as jnp
from jax import lax
from jax.experimental import pallas as pl
from jax.experimental.pallas import tpu as pltpu
from jax.sharding import PartitionSpec as P

S = 32
C = 256
H = 1024
SLOT = 40
CHUNK = 72
BF = jnp.bfloat16
F32 = jnp.float32
GELU_C = 0.7978845608028654
VMEM = functools.partial(pl.BlockSpec, memory_space=pltpu.VMEM)
SMEM = functools.partial(pl.BlockSpec, memory_space=pltpu.SMEM)


def params(mib):
    return pltpu.CompilerParams(vmem_limit_bytes=mib * 1024 * 1024)


def fill_slots(out_ref, strips, cells, pos, seam_ref):
    cells8 = jnp.concatenate([c.reshape(1, C) for c in cells] + [jnp.zeros((4, C), F32)], axis=0)
    cells8 = cells8.astype(BF)

    def put(p, carry):
        out_ref[p, pl.ds(S, SLOT - S), :] = cells8
        return carry

    lax.fori_loop(0, 64, put, 0)
    for e in range(4):
        out_ref[seam_ref[pos, e] // 8, pl.ds(0, S), :] = strips[e].astype(BF)


def take_slots(recv_ref, pos, seam_ref, corner_ref):
    rows = lax.broadcasted_iota(jnp.int32, (S, S), 0)
    cols = lax.broadcasted_iota(jnp.int32, (S, S), 1)
    strips = []
    for e in range(4):
        code = seam_ref[pos, e]
        target = jnp.where(code % 2 == 1, S - 1 - rows, rows)
        turn = (cols == target).astype(F32).astype(BF)
        strip = recv_ref[code // 8, pl.ds(0, S), :]
        strips.append(jnp.dot(turn, strip, preferred_element_type=F32))
    cells = []
    row8 = lax.broadcasted_iota(jnp.int32, (SLOT - S, C), 0)
    for k in range(4):
        code = corner_ref[pos, k]
        block = recv_ref[code // 4, pl.ds(S, SLOT - S), :].astype(F32)
        cells.append(jnp.sum(jnp.where(row8 == code % 4, block, 0.0), axis=0, keepdims=True))
    return strips, cells


def pack_kernel(pos_ref, seam_ref, field_ref, out_ref, wide_ref):
    wide_ref[...] = field_ref[...].astype(F32)
    strips = [wide_ref[0], wide_ref[S - 1], wide_ref[:, 0, :], wide_ref[:, S - 1, :]]
    cells = [wide_ref[i, pl.ds(j, 1), :] for i in (0, S - 1) for j in (0, S - 1)]
    fill_slots(out_ref, strips, cells, pos_ref[0], seam_ref)


def tile_kernel(
    pos_ref,
    seam_ref,
    corner_ref,
    field_ref,
    cot_ref,
    recv_ref,
    kern_ref,
    vec_ref,
    w_in_ref,
    b_in_ref,
    w_out_ref,
    blocks_ref,
    inner_ref,
    rim_ref,
    own_ref,
    send_ref,
    pad_ref,
    xhat_ref,
    istd_ref,
    normed_ref,
    active_ref,
    dhid_ref,
    dnorm_ref,
    dconv_ref,
):
    pos = pos_ref[0]
    core = pos_ref[1]
    strips, cells = take_slots(recv_ref, pos, seam_ref, corner_ref)
    center = field_ref[...].astype(F32)
    pad_ref[1, pl.ds(1, S)] = center
    pad_ref[1, 0] = strips[0]
    pad_ref[1, S + 1] = strips[1]
    pad_ref[0, pl.ds(1, S)] = pltpu.roll(center, 1, 1)
    pad_ref[2, pl.ds(1, S)] = pltpu.roll(center, S - 1, 1)
    pad_ref[0, 0] = pltpu.roll(strips[0], 1, 0)
    pad_ref[2, 0] = pltpu.roll(strips[0], S - 1, 0)
    pad_ref[0, S + 1] = pltpu.roll(strips[1], 1, 0)
    pad_ref[2, S + 1] = pltpu.roll(strips[1], S - 1, 0)
    pad_ref[0, pl.ds(1, S), 0, :] = strips[2]
    pad_ref[2, pl.ds(1, S), S - 1, :] = strips[3]
    pad_ref[0, 0, pl.ds(0, 1), :] = cells[0]
    pad_ref[2, 0, pl.ds(S - 1, 1), :] = cells[1]
    pad_ref[0, S + 1, pl.ds(0, 1), :] = cells[2]
    pad_ref[2, S + 1, pl.ds(S - 1, 1), :] = cells[3]

    bias = vec_ref[0:1, :]
    gain = vec_ref[1:2, :]
    shift = vec_ref[2:3, :]
    b_out = vec_ref[3:4, :]

    def forward_rows(b, carry):
        r0 = b * 8
        acc = jnp.zeros((8, S, C), F32) + bias.reshape(1, 1, C)
        for u in range(3):
            for v in range(3):
                k = 3 * u + v
                acc = acc + pad_ref[v, pl.ds(r0 + u, 8)] * kern_ref[k : k + 1, :].reshape(1, 1, C)
        rows = acc.reshape(8 * S, C)
        centred = rows - jnp.mean(rows, axis=1, keepdims=True)
        istd = 1.0 / jnp.sqrt(jnp.mean(centred * centred, axis=1, keepdims=True) + 1e-06)
        xhat = centred * istd
        q = pl.ds(pl.multiple_of(b * 256, 256), 256)
        xhat_ref[q, :] = xhat
        istd_ref[q, :] = jnp.broadcast_to(istd, (256, 128))
        normed_ref[q, :] = (xhat * gain + shift).astype(BF)
        return carry

    lax.fori_loop(0, 4, forward_rows, 0)

    def block_rows(b, carry):
        q = pl.ds(pl.multiple_of(b * 256, 256), 256)
        normed = normed_ref[q, :]
        cot = cot_ref[q, :]
        out = field_ref[pl.ds(b * 8, 8)].reshape(256, C).astype(F32) + b_out
        dnorm = jnp.zeros((256, C), F32)
        sums = []
        for n in range(4):
            h = slice(256 * n, 256 * n + 256)
            z = jnp.dot(normed, w_in_ref[:, h], preferred_element_type=F32) + b_in_ref[:, h]
            dact = lax.dot_general(
                cot, w_out_ref[h, :], (((1,), (1,)), ((), ())), preferred_element_type=F32
            )
            z2 = z * z
            half = 0.5 + 0.5 * jnp.tanh(z * (GELU_C + (GELU_C * 0.044715) * z2))
            act = z * half
            slope = half + act * (1.0 - half) * (2 * GELU_C + (6 * GELU_C * 0.044715) * z2)
            act = act.astype(BF)
            dhid = (dact * slope).astype(BF)
            active_ref[q, h] = act
            dhid_ref[q, h] = dhid
            sums.append(jnp.sum(dhid.astype(F32), axis=0, keepdims=True))
            out = out + jnp.dot(act, w_out_ref[h, :], preferred_element_type=F32)
            dnorm = dnorm + lax.dot_general(
                dhid, w_in_ref[:, h], (((1,), (1,)), ((), ())), preferred_element_type=F32
            )
        blocks_ref[q, :] = out.astype(BF)
        xhat = xhat_ref[q, :]
        dunit = dnorm * gain
        dconv = istd_ref[q, 0:1] * (
            dunit
            - jnp.mean(dunit, axis=1, keepdims=True)
            - xhat * jnp.mean(dunit * xhat, axis=1, keepdims=True)
        )
        dconv_ref[pl.ds(b * 8, 8)] = dconv.astype(BF).astype(F32).reshape(8, S, C)
        g_gain = jnp.sum(dnorm * xhat, axis=0, keepdims=True)
        g_shift = jnp.sum(dnorm, axis=0, keepdims=True)
        g_bout = jnp.sum(cot.astype(F32), axis=0, keepdims=True)
        return tuple(a + x for a, x in zip(carry, sums + [g_gain, g_shift, g_bout]))

    zero = jnp.zeros((1, C), F32)
    *g_bin, g_gain, g_shift, g_bout = lax.fori_loop(0, 4, block_rows, (zero,) * 7)

    def put_rows(first, value):
        mine = core == first // 16
        base = first % 16

        @pl.when(mine)
        def _():
            own_ref[pl.ds(base, 4), pl.ds(0, 64), :] = value.reshape(4, 64, C)

        @pl.when(jnp.logical_not(mine))
        def _():
            send_ref[pl.ds(base, 4), pl.ds(0, 64), :] = value.reshape(4, 64, C).astype(BF)

    for n in range(4):
        h = slice(256 * n, 256 * n + 256)
        over_rows = (((0,), (0,)), ((), ()))
        put_rows(
            4 * n,
            lax.dot_general(normed_ref[...], dhid_ref[:, h], over_rows, preferred_element_type=F32),
        )
        put_rows(
            16 + 4 * n,
            lax.dot_general(active_ref[:, h], cot_ref[...], over_rows, preferred_element_type=F32),
        )

    taps = [kern_ref[k : k + 1, :].reshape(1, 1, C) for k in range(9)]
    g_kernel = []
    for u in range(3):
        for v in range(3):

            def tap_rows(b, acc, u=u, v=v):
                part = pad_ref[v, pl.ds(b * 4 + u, 4)] * dconv_ref[pl.ds(b * 4, 4)]
                return acc + jnp.sum(part.reshape(4 * S // 8, 8, C), axis=0)

            acc = lax.fori_loop(0, 8, tap_rows, jnp.zeros((8, C), F32))
            g_kernel.append(jnp.sum(acc, axis=0, keepdims=True))

    def bias_rows(b, acc):
        return acc + jnp.sum(dconv_ref[pl.ds(b * 4, 4)].reshape(4 * S // 8, 8, C), axis=0)

    g_bias = jnp.sum(lax.fori_loop(0, 8, bias_rows, jnp.zeros((8, C), F32)), axis=0, keepdims=True)

    small = g_kernel + [g_bias, g_gain, g_shift, g_bout] + g_bin + [zero] * 15
    row8 = lax.broadcasted_iota(jnp.int32, (CHUNK - 64, C), 0)
    for j in range(32):
        row = jnp.where(row8 == 0, small[j], 0.0)

        @pl.when(core == j // 16)
        def _(row=row, j=j):
            own_ref[j % 16, pl.ds(64, CHUNK - 64), :] = row

        @pl.when(core != j // 16)
        def _(row=row, j=j):
            send_ref[j % 16, pl.ds(64, CHUNK - 64), :] = row.astype(BF)

    pad_ref[:, 0] = jnp.zeros((3, S, C), F32)
    pad_ref[:, S + 1] = jnp.zeros((3, S, C), F32)
    col = lax.broadcasted_iota(jnp.int32, (S, C), 0)

    def shift_rows(i, carry):
        row = dconv_ref[i]
        pad_ref[1, i + 1] = row
        pad_ref[0, i + 1] = jnp.where(col == S - 1, 0.0, pltpu.roll(row, S - 1, 0))
        pad_ref[2, i + 1] = jnp.where(col == 0, 0.0, pltpu.roll(row, 1, 0))
        return carry

    lax.fori_loop(0, S, shift_rows, 0)

    def inner_rows(b, carry):
        acc = jnp.zeros((4, S, C), F32)
        for u in range(3):
            for v in range(3):
                acc = acc + pad_ref[v, pl.ds(b * 4 + 2 - u, 4)] * taps[3 * u + v]
        inner_ref[pl.ds(b * 4, 4)] = acc
        return carry

    lax.fori_loop(0, 8, inner_rows, 0)

    def flat(k):
        return kern_ref[k : k + 1, :]

    top = sum(pad_ref[v, 1] * flat(v) for v in range(3))
    bottom = sum(pad_ref[v, S] * flat(6 + v) for v in range(3))
    left_col = dconv_ref[:, 0, :]
    right_col = dconv_ref[:, S - 1, :]

    def side(column, v):
        below = jnp.where(col == S - 1, 0.0, pltpu.roll(column, S - 1, 0))
        above = jnp.where(col == 0, 0.0, pltpu.roll(column, 1, 0))
        return below * flat(v) + column * flat(3 + v) + above * flat(6 + v)

    corners = [
        dconv_ref[0, pl.ds(0, 1), :] * flat(0),
        dconv_ref[0, pl.ds(S - 1, 1), :] * flat(2),
        dconv_ref[S - 1, pl.ds(0, 1), :] * flat(6),
        dconv_ref[S - 1, pl.ds(S - 1, 1), :] * flat(8),
    ]
    fill_slots(rim_ref, [top, bottom, side(left_col, 0), side(right_col, 2)], corners, pos, seam_ref)


def join_kernel(pos_ref, seam_ref, corner_ref, cot_ref, inner_ref, recv_ref, out_ref, acc_ref):
    strips, cells = take_slots(recv_ref, pos_ref[0], seam_ref, corner_ref)
    acc_ref[...] = cot_ref[...].astype(F32) + inner_ref[...]
    acc_ref[0] = acc_ref[0] + strips[0]
    acc_ref[S - 1] = acc_ref[S - 1] + strips[1]
    acc_ref[:, 0, :] = acc_ref[:, 0, :] + strips[2]
    acc_ref[:, S - 1, :] = acc_ref[:, S - 1, :] + strips[3]
    for n, (i, j) in enumerate(((0, 0), (0, S - 1), (S - 1, 0), (S - 1, S - 1))):
        acc_ref[i, pl.ds(j, 1), :] = acc_ref[i, pl.ds(j, 1), :] + cells[n]
    out_ref[...] = acc_ref[...].astype(BF)


def scale_kernel(
    at_ref, own_ref, other_ref, kern_ref, chan_ref, w_in_ref, b_in_ref, w_out_ref, entries
):
    core, x0, y0 = at_ref[1], at_ref[2], at_ref[3]
    halves = (own_ref, other_ref)
    sums = []
    for half in range(2):
        def one_half(j, acc, half=half):
            a = own_ref[j].astype(F32)
            b = other_ref[j].astype(F32)
            v = jnp.where(core == half, a, b)
            return acc + jnp.sum((v * v).reshape(CHUNK // 8, 8, C), axis=0)

        def ordered(j, acc, one_half=one_half):
            k = ((j // 4 - x0 + 4) % 4) * 4 + (j % 4 - y0 + 4) % 4
            return one_half(k, acc)

        sums.append(lax.fori_loop(0, 16, ordered, jnp.zeros((8, C), F32)))
    total = jnp.sum(jnp.sum(sums[0] + sums[1], axis=0, keepdims=True), axis=1, keepdims=True)
    scale = 1.0 / jnp.sqrt(total / entries + 1e-06)

    for j in range(32):
        c, x, y = j // 16, (j // 4) % 4, j % 4
        k = ((x - x0 + 4) % 4) * 4 + (y - y0 + 4) % 4

        def emit(ref, j=j, k=k):
            rows = ref[k, pl.ds(0, 64), :].astype(F32) * scale
            if j < 16:
                w_in_ref[64 * (j % 4) : 64 * (j % 4) + 64, 256 * (j // 4) : 256 * (j // 4) + 256] = rows
            else:
                w_out_ref[64 * (j - 16) : 64 * (j - 16) + 64, :] = rows
            row = ref[k, pl.ds(64, 8), :].astype(F32)[0:1] * scale
            if j < 9:
                kern_ref[j : j + 1, :] = row
            elif j < 13:
                chan_ref[j - 9 : j - 8, :] = row
            elif j < 17:
                b_in_ref[:, 256 * (j - 13) : 256 * (j - 13) + 256] = row

        for near in range(2):

            @pl.when((core == c) == (near == 1))
            def _(emit=emit, near=near):
                emit(halves[1 - near])


def at(y, x, h, c):
    return ((y * 4 + x) * 2 + h) * 2 + c


def moves(axis, d):
    pairs = []
    for y in range(4):
        for x in range(4):
            for h in range(2):
                for c in range(2):
                    to = {
                        "y": ((y + d) % 4, x, h, c),
                        "x": (y, (x + d) % 4, h, c),
                        "h": (y, x, 1 - h, c),
                        "c": (y, x, h, 1 - c),
                    }[axis]
                    pairs.append((at(y, x, h, c), at(*to)))
    return pairs


def sum_over_devices(own, send, x, y):
    rest = own + lax.ppermute(send, "space", moves("c", 1)).astype(F32)
    for axis, place, n in (("x", x, 4), ("y", y, 1)):
        parts = rest.reshape(4, n, CHUNK, C)
        pick = lambda d: lax.dynamic_slice(
            parts, ((place + jnp.uint32(d)) & jnp.uint32(3),) + (jnp.uint32(0),) * 3, (1, n, CHUNK, C)
        )[0]
        got = [lax.ppermute(pick(d).astype(BF), "space", moves(axis, d)) for d in (1, 2, 3)]
        rest = pick(0) + (got[0].astype(F32) + got[1].astype(F32) + got[2].astype(F32))
    piece = rest.reshape(CHUNK, C)
    piece = piece + lax.ppermute(piece, "space", moves("h", 1))
    ring = lambda d: [(i, (i + d) % 4) for i in range(4)]
    got = [lax.ppermute(piece, "batch", ring(d)) for d in (1, 2, 3)]
    piece = (piece + got[1]) + (got[0] + got[2])
    full = piece.astype(BF)[None]
    for axis in ("y", "x"):
        got = [lax.ppermute(full, "space", moves(axis, -d)) for d in (1, 2, 3)]
        full = jnp.stack([full] + got).reshape(-1, CHUNK, C)
    return full, lax.ppermute(full, "space", moves("c", 1))


def shards(
    fields,
    cotangent,
    dw_kernel,
    dw_bias,
    ln_gain,
    ln_shift,
    w_in,
    b_in,
    w_out,
    b_out,
    seam_links,
    corner_links,
):
    pos = lax.axis_index("space")
    core = pos & 1
    x = (pos >> 2) & 3
    y = pos >> 4
    here = jnp.stack([pos, core, x, y])
    field = fields[0, 0]
    cot = cotangent[0, 0]
    sds = jax.ShapeDtypeStruct
    slots = sds((64, SLOT, C), BF)

    out_slots = pl.pallas_call(
        pack_kernel,
        out_shape=slots,
        in_specs=[SMEM(), SMEM(), VMEM()],
        out_specs=VMEM(),
        scratch_shapes=[pltpu.VMEM((S, S, C), F32)],
        compiler_params=params(8),
        name="pack",
    )(here, seam_links, field)
    halo = lax.all_to_all(out_slots, "space", 0, 0, tiled=True)

    vectors = jnp.stack([dw_bias, ln_gain, ln_shift, b_out])
    cells = S * S
    blocks, inner, rim_slots, own, send = pl.pallas_call(
        tile_kernel,
        out_shape=(
            sds((cells, C), BF),
            sds((S, S, C), F32),
            slots,
            sds((16, CHUNK, C), F32),
            sds((16, CHUNK, C), BF),
        ),
        in_specs=[SMEM()] * 3 + [VMEM()] * 8,
        out_specs=(VMEM(),) * 5,
        scratch_shapes=[
            pltpu.VMEM((3, S + 2, S, C), F32),
            pltpu.VMEM((cells, C), F32),
            pltpu.VMEM((cells, 128), F32),
            pltpu.VMEM((cells, C), BF),
            pltpu.VMEM((cells, H), BF),
            pltpu.VMEM((cells, H), BF),
            pltpu.VMEM((8, C), F32),
            pltpu.VMEM((S, S, C), F32),
        ],
        compiler_params=params(28),
        name="tile",
    )(
        here,
        seam_links,
        corner_links,
        field,
        cot.reshape(cells, C),
        halo,
        dw_kernel,
        vectors,
        w_in,
        b_in.reshape(1, H),
        w_out,
    )
    back = lax.all_to_all(rim_slots, "space", 0, 0, tiled=True)
    near, far = sum_over_devices(own, send, x.astype(jnp.uint32), y.astype(jnp.uint32))
    grad_tile = pl.pallas_call(
        join_kernel,
        out_shape=sds((S, S, C), BF),
        in_specs=[SMEM()] * 3 + [VMEM()] * 3,
        out_specs=VMEM(),
        scratch_shapes=[pltpu.VMEM((S, S, C), F32)],
        compiler_params=params(10),
        name="join",
    )(here, seam_links, corner_links, cot, inner, back)

    entries = 13 * C + 2 * C * H + H
    grad_kernel, grad_channels, grad_w_in, grad_b_in, grad_w_out = pl.pallas_call(
        functools.partial(scale_kernel, entries=entries),
        out_shape=(
            sds((9, C), F32),
            sds((4, C), F32),
            sds((C, H), F32),
            sds((1, H), F32),
            sds((H, C), F32),
        ),
        in_specs=[SMEM(), VMEM(), VMEM()],
        out_specs=(VMEM(),) * 5,
        compiler_params=params(10),
        name="scale",
    )(here, near, far)
    return (
        blocks.reshape(1, 1, S, S, C),
        grad_tile[None, None],
        grad_kernel,
        grad_channels,
        grad_w_in,
        grad_b_in.reshape(H),
        grad_w_out,
    )


def solution(mesh):
    tile = P("batch", "space", None, None, None)
    return jax.shard_map(
        shards,
        mesh=mesh,
        in_specs=(tile, tile) + (P(),) * 10,
        out_specs=(tile, tile) + (P(),) * 5,
        check_vma=False,
    )
```

```python
import functools

import jax
import jax.numpy as jnp
from jax import lax
from jax.experimental import pallas as pl
from jax.experimental.pallas import tpu as pltpu
from jax.sharding import PartitionSpec as P

S = 32
C = 256
H = 1024
SLOT = 40
CHUNK = 72
BF = jnp.bfloat16
F32 = jnp.float32
GELU_C = 0.7978845608028654
VMEM = functools.partial(pl.BlockSpec, memory_space=pltpu.VMEM)
SMEM = functools.partial(pl.BlockSpec, memory_space=pltpu.SMEM)


def params(mib):
    return pltpu.CompilerParams(vmem_limit_bytes=mib * 1024 * 1024)


def fill_slots(out_ref, strips, cells, pos, seam_ref):
    cells8 = jnp.concatenate([c.reshape(1, C) for c in cells] + [jnp.zeros((4, C), F32)], axis=0)
    cells8 = cells8.astype(BF)

    def put(p, carry):
        out_ref[p, pl.ds(S, SLOT - S), :] = cells8
        return carry

    lax.fori_loop(0, 64, put, 0)
    for e in range(4):
        out_ref[seam_ref[pos, e] // 8, pl.ds(0, S), :] = strips[e].astype(BF)


def take_slots(recv_ref, pos, seam_ref, corner_ref):
    rows = lax.broadcasted_iota(jnp.int32, (S, S), 0)
    cols = lax.broadcasted_iota(jnp.int32, (S, S), 1)
    strips = []
    for e in range(4):
        code = seam_ref[pos, e]
        target = jnp.where(code % 2 == 1, S - 1 - rows, rows)
        turn = (cols == target).astype(F32).astype(BF)
        strip = recv_ref[code // 8, pl.ds(0, S), :]
        strips.append(jnp.dot(turn, strip, preferred_element_type=F32))
    cells = []
    row8 = lax.broadcasted_iota(jnp.int32, (SLOT - S, C), 0)
    for k in range(4):
        code = corner_ref[pos, k]
        block = recv_ref[code // 4, pl.ds(S, SLOT - S), :].astype(F32)
        cells.append(jnp.sum(jnp.where(row8 == code % 4, block, 0.0), axis=0, keepdims=True))
    return strips, cells


def pack_kernel(pos_ref, seam_ref, field_ref, out_ref, wide_ref):
    wide_ref[...] = field_ref[...].astype(F32)
    strips = [wide_ref[0], wide_ref[S - 1], wide_ref[:, 0, :], wide_ref[:, S - 1, :]]
    cells = [wide_ref[i, pl.ds(j, 1), :] for i in (0, S - 1) for j in (0, S - 1)]
    fill_slots(out_ref, strips, cells, pos_ref[0], seam_ref)


def tile_kernel(
    pos_ref,
    seam_ref,
    corner_ref,
    field_ref,
    cot_ref,
    recv_ref,
    kern_ref,
    vec_ref,
    w_in_ref,
    b_in_ref,
    w_out_ref,
    blocks_ref,
    inner_ref,
    rim_ref,
    own_ref,
    send_ref,
    pad_ref,
    xhat_ref,
    istd_ref,
    normed_ref,
    active_ref,
    dhid_ref,
    dnorm_ref,
    dconv_ref,
):
    pos = pos_ref[0]
    core = pos_ref[1]
    strips, cells = take_slots(recv_ref, pos, seam_ref, corner_ref)
    center = field_ref[...].astype(F32)
    pad_ref[1, pl.ds(1, S)] = center
    pad_ref[1, 0] = strips[0]
    pad_ref[1, S + 1] = strips[1]
    pad_ref[0, pl.ds(1, S)] = pltpu.roll(center, 1, 1)
    pad_ref[2, pl.ds(1, S)] = pltpu.roll(center, S - 1, 1)
    pad_ref[0, 0] = pltpu.roll(strips[0], 1, 0)
    pad_ref[2, 0] = pltpu.roll(strips[0], S - 1, 0)
    pad_ref[0, S + 1] = pltpu.roll(strips[1], 1, 0)
    pad_ref[2, S + 1] = pltpu.roll(strips[1], S - 1, 0)
    pad_ref[0, pl.ds(1, S), 0, :] = strips[2]
    pad_ref[2, pl.ds(1, S), S - 1, :] = strips[3]
    pad_ref[0, 0, pl.ds(0, 1), :] = cells[0]
    pad_ref[2, 0, pl.ds(S - 1, 1), :] = cells[1]
    pad_ref[0, S + 1, pl.ds(0, 1), :] = cells[2]
    pad_ref[2, S + 1, pl.ds(S - 1, 1), :] = cells[3]

    bias = vec_ref[0:1, :]
    gain = vec_ref[1:2, :]
    shift = vec_ref[2:3, :]
    b_out = vec_ref[3:4, :]

    def forward_rows(b, carry):
        r0 = b * 8
        acc = jnp.zeros((8, S, C), F32) + bias.reshape(1, 1, C)
        for u in range(3):
            for v in range(3):
                k = 3 * u + v
                acc = acc + pad_ref[v, pl.ds(r0 + u, 8)] * kern_ref[k : k + 1, :].reshape(1, 1, C)
        rows = acc.reshape(8 * S, C)
        centred = rows - jnp.mean(rows, axis=1, keepdims=True)
        istd = 1.0 / jnp.sqrt(jnp.mean(centred * centred, axis=1, keepdims=True) + 1e-06)
        xhat = centred * istd
        q = pl.ds(pl.multiple_of(b * 256, 256), 256)
        xhat_ref[q, :] = xhat
        istd_ref[q, :] = jnp.broadcast_to(istd, (256, 128))
        normed_ref[q, :] = (xhat * gain + shift).astype(BF)
        return carry

    lax.fori_loop(0, 4, forward_rows, 0)

    def block_rows(b, carry):
        q = pl.ds(pl.multiple_of(b * 256, 256), 256)
        normed = normed_ref[q, :]
        cot = cot_ref[q, :]
        out = field_ref[pl.ds(b * 8, 8)].reshape(256, C).astype(F32) + b_out
        dnorm = jnp.zeros((256, C), F32)
        sums = []
        for n in range(4):
            h = slice(256 * n, 256 * n + 256)
            z = jnp.dot(normed, w_in_ref[:, h], preferred_element_type=F32) + b_in_ref[:, h]
            dact = lax.dot_general(
                cot, w_out_ref[h, :], (((1,), (1,)), ((), ())), preferred_element_type=F32
            )
            z2 = z * z
            half = 0.5 + 0.5 * jnp.tanh(z * (GELU_C + (GELU_C * 0.044715) * z2))
            act = z * half
            slope = half + act * (1.0 - half) * (2 * GELU_C + (6 * GELU_C * 0.044715) * z2)
            act = act.astype(BF)
            dhid = (dact * slope).astype(BF)
            active_ref[q, h] = act
            dhid_ref[q, h] = dhid
            sums.append(jnp.sum(dhid.astype(F32), axis=0, keepdims=True))
            out = out + jnp.dot(act, w_out_ref[h, :], preferred_element_type=F32)
            dnorm = dnorm + lax.dot_general(
                dhid, w_in_ref[:, h], (((1,), (1,)), ((), ())), preferred_element_type=F32
            )
        blocks_ref[q, :] = out.astype(BF)
        xhat = xhat_ref[q, :]
        dunit = dnorm * gain
        dconv = istd_ref[q, 0:1] * (
            dunit
            - jnp.mean(dunit, axis=1, keepdims=True)
            - xhat * jnp.mean(dunit * xhat, axis=1, keepdims=True)
        )
        dconv_ref[pl.ds(b * 8, 8)] = dconv.astype(BF).astype(F32).reshape(8, S, C)
        g_gain = jnp.sum(dnorm * xhat, axis=0, keepdims=True)
        g_shift = jnp.sum(dnorm, axis=0, keepdims=True)
        g_bout = jnp.sum(cot.astype(F32), axis=0, keepdims=True)
        return tuple(a + x for a, x in zip(carry, sums + [g_gain, g_shift, g_bout]))

    zero = jnp.zeros((1, C), F32)
    *g_bin, g_gain, g_shift, g_bout = lax.fori_loop(0, 4, block_rows, (zero,) * 7)

    def put_rows(first, value):
        mine = core == first // 16
        base = first % 16

        @pl.when(mine)
        def _():
            own_ref[pl.ds(base, 4), pl.ds(0, 64), :] = value.reshape(4, 64, C)

        @pl.when(jnp.logical_not(mine))
        def _():
            send_ref[pl.ds(base, 4), pl.ds(0, 64), :] = value.reshape(4, 64, C).astype(BF)

    for n in range(4):
        h = slice(256 * n, 256 * n + 256)
        over_rows = (((0,), (0,)), ((), ()))
        put_rows(
            4 * n,
            lax.dot_general(normed_ref[...], dhid_ref[:, h], over_rows, preferred_element_type=F32),
        )
        put_rows(
            16 + 4 * n,
            lax.dot_general(active_ref[:, h], cot_ref[...], over_rows, preferred_element_type=F32),
        )

    taps = [kern_ref[k : k + 1, :].reshape(1, 1, C) for k in range(9)]
    g_kernel = []
    for u in range(3):
        for v in range(3):

            def tap_rows(b, acc, u=u, v=v):
                part = pad_ref[v, pl.ds(b * 4 + u, 4)] * dconv_ref[pl.ds(b * 4, 4)]
                return acc + jnp.sum(part.reshape(4 * S // 8, 8, C), axis=0)

            acc = lax.fori_loop(0, 8, tap_rows, jnp.zeros((8, C), F32))
            g_kernel.append(jnp.sum(acc, axis=0, keepdims=True))

    def bias_rows(b, acc):
        return acc + jnp.sum(dconv_ref[pl.ds(b * 4, 4)].reshape(4 * S // 8, 8, C), axis=0)

    g_bias = jnp.sum(lax.fori_loop(0, 8, bias_rows, jnp.zeros((8, C), F32)), axis=0, keepdims=True)

    small = g_kernel + [g_bias, g_gain, g_shift, g_bout] + g_bin + [zero] * 15
    row8 = lax.broadcasted_iota(jnp.int32, (CHUNK - 64, C), 0)
    for j in range(32):
        row = jnp.where(row8 == 0, small[j], 0.0)

        @pl.when(core == j // 16)
        def _(row=row, j=j):
            own_ref[j % 16, pl.ds(64, CHUNK - 64), :] = row

        @pl.when(core != j // 16)
        def _(row=row, j=j):
            send_ref[j % 16, pl.ds(64, CHUNK - 64), :] = row.astype(BF)

    pad_ref[:, 0] = jnp.zeros((3, S, C), F32)
    pad_ref[:, S + 1] = jnp.zeros((3, S, C), F32)
    col = lax.broadcasted_iota(jnp.int32, (S, C), 0)

    def shift_rows(i, carry):
        row = dconv_ref[i]
        pad_ref[1, i + 1] = row
        pad_ref[0, i + 1] = jnp.where(col == S - 1, 0.0, pltpu.roll(row, S - 1, 0))
        pad_ref[2, i + 1] = jnp.where(col == 0, 0.0, pltpu.roll(row, 1, 0))
        return carry

    lax.fori_loop(0, S, shift_rows, 0)

    def inner_rows(b, carry):
        acc = jnp.zeros((4, S, C), F32)
        for u in range(3):
            for v in range(3):
                acc = acc + pad_ref[v, pl.ds(b * 4 + 2 - u, 4)] * taps[3 * u + v]
        inner_ref[pl.ds(b * 4, 4)] = acc
        return carry

    lax.fori_loop(0, 8, inner_rows, 0)

    def flat(k):
        return kern_ref[k : k + 1, :]

    top = sum(pad_ref[v, 1] * flat(v) for v in range(3))
    bottom = sum(pad_ref[v, S] * flat(6 + v) for v in range(3))
    left_col = dconv_ref[:, 0, :]
    right_col = dconv_ref[:, S - 1, :]

    def side(column, v):
        below = jnp.where(col == S - 1, 0.0, pltpu.roll(column, S - 1, 0))
        above = jnp.where(col == 0, 0.0, pltpu.roll(column, 1, 0))
        return below * flat(v) + column * flat(3 + v) + above * flat(6 + v)

    corners = [
        dconv_ref[0, pl.ds(0, 1), :] * flat(0),
        dconv_ref[0, pl.ds(S - 1, 1), :] * flat(2),
        dconv_ref[S - 1, pl.ds(0, 1), :] * flat(6),
        dconv_ref[S - 1, pl.ds(S - 1, 1), :] * flat(8),
    ]
    fill_slots(rim_ref, [top, bottom, side(left_col, 0), side(right_col, 2)], corners, pos, seam_ref)


def join_kernel(pos_ref, seam_ref, corner_ref, cot_ref, inner_ref, recv_ref, out_ref, acc_ref):
    strips, cells = take_slots(recv_ref, pos_ref[0], seam_ref, corner_ref)
    acc_ref[...] = cot_ref[...].astype(F32) + inner_ref[...]
    acc_ref[0] = acc_ref[0] + strips[0]
    acc_ref[S - 1] = acc_ref[S - 1] + strips[1]
    acc_ref[:, 0, :] = acc_ref[:, 0, :] + strips[2]
    acc_ref[:, S - 1, :] = acc_ref[:, S - 1, :] + strips[3]
    for n, (i, j) in enumerate(((0, 0), (0, S - 1), (S - 1, 0), (S - 1, S - 1))):
        acc_ref[i, pl.ds(j, 1), :] = acc_ref[i, pl.ds(j, 1), :] + cells[n]
    out_ref[...] = acc_ref[...].astype(BF)


def scale_kernel(
    at_ref, own_ref, other_ref, kern_ref, chan_ref, w_in_ref, b_in_ref, w_out_ref, entries
):
    core, x0, y0 = at_ref[1], at_ref[2], at_ref[3]
    halves = (own_ref, other_ref)
    sums = []
    for half in range(2):
        def one_half(j, acc, half=half):
            a = own_ref[j].astype(F32)
            b = other_ref[j].astype(F32)
            v = jnp.where(core == half, a, b)
            return acc + jnp.sum((v * v).reshape(CHUNK // 8, 8, C), axis=0)

        def ordered(j, acc, one_half=one_half):
            k = ((j // 4 - x0 + 4) % 4) * 4 + (j % 4 - y0 + 4) % 4
            return one_half(k, acc)

        sums.append(lax.fori_loop(0, 16, ordered, jnp.zeros((8, C), F32)))
    total = jnp.sum(jnp.sum(sums[0] + sums[1], axis=0, keepdims=True), axis=1, keepdims=True)
    scale = 1.0 / jnp.sqrt(total / entries + 1e-06)

    for j in range(32):
        c, x, y = j // 16, (j // 4) % 4, j % 4
        k = ((x - x0 + 4) % 4) * 4 + (y - y0 + 4) % 4

        def emit(ref, j=j, k=k):
            rows = ref[k, pl.ds(0, 64), :].astype(F32) * scale
            if j < 16:
                w_in_ref[64 * (j % 4) : 64 * (j % 4) + 64, 256 * (j // 4) : 256 * (j // 4) + 256] = rows
            else:
                w_out_ref[64 * (j - 16) : 64 * (j - 16) + 64, :] = rows
            row = ref[k, pl.ds(64, 8), :].astype(F32)[0:1] * scale
            if j < 9:
                kern_ref[j : j + 1, :] = row
            elif j < 13:
                chan_ref[j - 9 : j - 8, :] = row
            elif j < 17:
                b_in_ref[:, 256 * (j - 13) : 256 * (j - 13) + 256] = row

        for near in range(2):

            @pl.when((core == c) == (near == 1))
            def _(emit=emit, near=near):
                emit(halves[1 - near])


def at(y, x, h, c):
    return ((y * 4 + x) * 2 + h) * 2 + c


def moves(axis, d):
    pairs = []
    for y in range(4):
        for x in range(4):
            for h in range(2):
                for c in range(2):
                    to = {
                        "y": ((y + d) % 4, x, h, c),
                        "x": (y, (x + d) % 4, h, c),
                        "h": (y, x, 1 - h, c),
                        "c": (y, x, h, 1 - c),
                    }[axis]
                    pairs.append((at(y, x, h, c), at(*to)))
    return pairs


def z_moves(d):
    pairs = []
    for y in range(4):
        for x in range(4):
            for c in range(2):
                for z in range(8):
                    to = (z + d) % 8
                    pairs.append((at(y, x, z // 4, c) * 4 + z % 4, at(y, x, to // 4, c) * 4 + to % 4))
    return pairs


def sum_over_devices(own, send, x, y, later):
    rest = own + lax.ppermute(send, "space", moves("c", 1)).astype(F32)
    for axis, place, n in (("x", x, 4), ("y", y, 1)):
        parts = rest.reshape(4, n, CHUNK, C)
        pick = lambda d: lax.dynamic_slice(
            parts, ((place + jnp.uint32(d)) & jnp.uint32(3),) + (jnp.uint32(0),) * 3, (1, n, CHUNK, C)
        )[0]
        got = [lax.ppermute(pick(d).astype(BF), "space", moves(axis, d)) for d in (1, 2, 3)]
        rest = pick(0) + (got[0].astype(F32) + got[1].astype(F32) + got[2].astype(F32))
        if axis == "x":
            rest, later = lax.optimization_barrier((rest, later))
    piece = rest.reshape(CHUNK, C).astype(BF)
    got = [lax.ppermute(piece, ("space", "batch"), z_moves(d)) for d in range(1, 8)]
    v = [p.astype(F32) for p in [piece] + got]
    piece = ((v[0] + v[4]) + (v[2] + v[6])) + ((v[1] + v[5]) + (v[3] + v[7]))
    full = piece.astype(BF)[None]
    for axis in ("y", "x"):
        got = [lax.ppermute(full, "space", moves(axis, -d)) for d in (1, 2, 3)]
        full = jnp.stack([full] + got).reshape(-1, CHUNK, C)
    return full, lax.ppermute(full, "space", moves("c", 1)), later


def shards(
    fields,
    cotangent,
    dw_kernel,
    dw_bias,
    ln_gain,
    ln_shift,
    w_in,
    b_in,
    w_out,
    b_out,
    seam_links,
    corner_links,
):
    pos = lax.axis_index("space")
    core = pos & 1
    x = (pos >> 2) & 3
    y = pos >> 4
    here = jnp.stack([pos, core, x, y])
    field = fields[0, 0]
    cot = cotangent[0, 0]
    sds = jax.ShapeDtypeStruct
    slots = sds((64, SLOT, C), BF)

    out_slots = pl.pallas_call(
        pack_kernel,
        out_shape=slots,
        in_specs=[SMEM(), SMEM(), VMEM()],
        out_specs=VMEM(),
        scratch_shapes=[pltpu.VMEM((S, S, C), F32)],
        compiler_params=params(8),
        name="pack",
    )(here, seam_links, field)
    halo = lax.all_to_all(out_slots, "space", 0, 0, tiled=True)

    vectors = jnp.stack([dw_bias, ln_gain, ln_shift, b_out])
    cells = S * S
    blocks, inner, rim_slots, own, send = pl.pallas_call(
        tile_kernel,
        out_shape=(
            sds((cells, C), BF),
            sds((S, S, C), F32),
            slots,
            sds((16, CHUNK, C), F32),
            sds((16, CHUNK, C), BF),
        ),
        in_specs=[SMEM()] * 3 + [VMEM()] * 8,
        out_specs=(VMEM(),) * 5,
        scratch_shapes=[
            pltpu.VMEM((3, S + 2, S, C), F32),
            pltpu.VMEM((cells, C), F32),
            pltpu.VMEM((cells, 128), F32),
            pltpu.VMEM((cells, C), BF),
            pltpu.VMEM((cells, H), BF),
            pltpu.VMEM((cells, H), BF),
            pltpu.VMEM((8, C), F32),
            pltpu.VMEM((S, S, C), F32),
        ],
        compiler_params=params(28),
        name="tile",
    )(
        here,
        seam_links,
        corner_links,
        field,
        cot.reshape(cells, C),
        halo,
        dw_kernel,
        vectors,
        w_in,
        b_in.reshape(1, H),
        w_out,
    )
    near, far, rim_slots = sum_over_devices(
        own, send, x.astype(jnp.uint32), y.astype(jnp.uint32), rim_slots
    )
    back = lax.all_to_all(rim_slots, "space", 0, 0, tiled=True)
    grad_tile = pl.pallas_call(
        join_kernel,
        out_shape=sds((S, S, C), BF),
        in_specs=[SMEM()] * 3 + [VMEM()] * 3,
        out_specs=VMEM(),
        scratch_shapes=[pltpu.VMEM((S, S, C), F32)],
        compiler_params=params(10),
        name="join",
    )(here, seam_links, corner_links, cot, inner, back)

    entries = 13 * C + 2 * C * H + H
    grad_kernel, grad_channels, grad_w_in, grad_b_in, grad_w_out = pl.pallas_call(
        functools.partial(scale_kernel, entries=entries),
        out_shape=(
            sds((9, C), F32),
            sds((4, C), F32),
            sds((C, H), F32),
            sds((1, H), F32),
            sds((H, C), F32),
        ),
        in_specs=[SMEM(), VMEM(), VMEM()],
        out_specs=(VMEM(),) * 5,
        compiler_params=params(10),
        name="scale",
    )(here, near, far)
    return (
        blocks.reshape(1, 1, S, S, C),
        grad_tile[None, None],
        grad_kernel,
        grad_channels,
        grad_w_in,
        grad_b_in.reshape(H),
        grad_w_out,
    )


def solution(mesh):
    tile = P("batch", "space", None, None, None)
    return jax.shard_map(
        shards,
        mesh=mesh,
        in_specs=(tile, tile) + (P(),) * 10,
        out_specs=(tile, tile) + (P(),) * 5,
        check_vma=False,
    )
```

```python
import functools

import jax
import jax.numpy as jnp
from jax import lax
from jax.experimental import pallas as pl
from jax.experimental.pallas import tpu as pltpu
from jax.sharding import PartitionSpec as P

S = 32
C = 256
H = 1024
SLOT = 72
EDGE = 136
CHUNK = 72
BF = jnp.bfloat16
F32 = jnp.float32
GELU_C = 0.7978845608028654
VMEM = functools.partial(pl.BlockSpec, memory_space=pltpu.VMEM)
SMEM = functools.partial(pl.BlockSpec, memory_space=pltpu.SMEM)


def params(mib):
    return pltpu.CompilerParams(vmem_limit_bytes=mib * 1024 * 1024)


def put_edges(out_ref, strips, cells):
    for e in range(4):
        out_ref[pl.ds(S * e, S), :] = strips[e].astype(BF)
    cells8 = jnp.concatenate([c.reshape(1, C) for c in cells] + [jnp.zeros((4, C), F32)], axis=0)
    out_ref[pl.ds(4 * S, 8), :] = cells8.astype(BF)


def half_of(tile):
    return (tile // 2) % 2


def place_of(tile):
    return (tile // 4) * 2 + tile % 2


def take_slots(recv_ref, pos, seam_ref, corner_ref):
    rows = lax.broadcasted_iota(jnp.int32, (S, S), 0)
    cols = lax.broadcasted_iota(jnp.int32, (S, S), 1)
    strips = []
    for e in range(4):
        code = seam_ref[pos, e]
        tile = code // 8
        target = jnp.where(code % 2 == 1, S - 1 - rows, rows)
        turn = (cols == target).astype(F32).astype(BF)
        strip = recv_ref[place_of(tile), pl.ds(pl.multiple_of(S * half_of(tile), S), S), :]
        strips.append(jnp.dot(turn, strip, preferred_element_type=F32))
    cells = []
    row8 = lax.broadcasted_iota(jnp.int32, (SLOT - 2 * S, C), 0)
    for k in range(4):
        code = corner_ref[pos, k]
        tile = code // 4
        block = recv_ref[place_of(tile), pl.ds(2 * S, SLOT - 2 * S), :].astype(F32)
        row = 4 * half_of(tile) + code % 4
        cells.append(jnp.sum(jnp.where(row8 == row, block, 0.0), axis=0, keepdims=True))
    return strips, cells


def edge_kernel(field_ref, out_ref, wide_ref):
    wide_ref[...] = field_ref[...].astype(F32)
    strips = [wide_ref[0], wide_ref[S - 1], wide_ref[:, 0, :], wide_ref[:, S - 1, :]]
    cells = [wide_ref[i, pl.ds(j, 1), :] for i in (0, S - 1) for j in (0, S - 1)]
    put_edges(out_ref, strips, cells)


def slot_kernel(pos_ref, seam_ref, own_ref, other_ref, out_ref):
    pos = pos_ref[0]
    half = half_of(pos)
    mine = own_ref[pl.ds(4 * S, 8), :].astype(F32)
    other = other_ref[pl.ds(4 * S, 8), :].astype(F32)
    row8 = lax.broadcasted_iota(jnp.int32, (8, C), 0)
    first = jnp.where(half == 0, mine, other)
    second = jnp.where(half == 0, other, mine)
    cells8 = jnp.where(row8 < 4, first, pltpu.roll(second, 4, 0)).astype(BF)

    def put(p, carry):
        out_ref[p, pl.ds(2 * S, SLOT - 2 * S), :] = cells8
        return carry

    lax.fori_loop(0, 32, put, 0)
    for source, edges, at_half in ((pos, own_ref, half), (pos ^ 2, other_ref, 1 - half)):
        for e in range(4):
            tile = seam_ref[source, e] // 8

            @pl.when(half_of(tile) == half)
            def _(tile=tile, edges=edges, at_half=at_half, e=e):
                rows = pl.ds(pl.multiple_of(S * at_half, S), S)
                out_ref[place_of(tile), rows, :] = edges[pl.ds(S * e, S), :]


def tile_kernel(
    pos_ref,
    seam_ref,
    corner_ref,
    field_ref,
    cot_ref,
    recv_ref,
    kern_ref,
    vec_ref,
    w_in_ref,
    b_in_ref,
    w_out_ref,
    blocks_ref,
    inner_ref,
    rim_ref,
    own_ref,
    send_ref,
    pad_ref,
    xhat_ref,
    istd_ref,
    normed_ref,
    active_ref,
    dhid_ref,
    dnorm_ref,
    dconv_ref,
):
    pos = pos_ref[0]
    core = pos_ref[1]
    strips, cells = take_slots(recv_ref, pos, seam_ref, corner_ref)
    center = field_ref[...].astype(F32)
    pad_ref[1, pl.ds(1, S)] = center
    pad_ref[1, 0] = strips[0]
    pad_ref[1, S + 1] = strips[1]
    pad_ref[0, pl.ds(1, S)] = pltpu.roll(center, 1, 1)
    pad_ref[2, pl.ds(1, S)] = pltpu.roll(center, S - 1, 1)
    pad_ref[0, 0] = pltpu.roll(strips[0], 1, 0)
    pad_ref[2, 0] = pltpu.roll(strips[0], S - 1, 0)
    pad_ref[0, S + 1] = pltpu.roll(strips[1], 1, 0)
    pad_ref[2, S + 1] = pltpu.roll(strips[1], S - 1, 0)
    pad_ref[0, pl.ds(1, S), 0, :] = strips[2]
    pad_ref[2, pl.ds(1, S), S - 1, :] = strips[3]
    pad_ref[0, 0, pl.ds(0, 1), :] = cells[0]
    pad_ref[2, 0, pl.ds(S - 1, 1), :] = cells[1]
    pad_ref[0, S + 1, pl.ds(0, 1), :] = cells[2]
    pad_ref[2, S + 1, pl.ds(S - 1, 1), :] = cells[3]

    bias = vec_ref[0:1, :]
    gain = vec_ref[1:2, :]
    shift = vec_ref[2:3, :]
    b_out = vec_ref[3:4, :]

    def forward_rows(b, carry):
        r0 = b * 8
        acc = jnp.zeros((8, S, C), F32) + bias.reshape(1, 1, C)
        for u in range(3):
            for v in range(3):
                k = 3 * u + v
                acc = acc + pad_ref[v, pl.ds(r0 + u, 8)] * kern_ref[k : k + 1, :].reshape(1, 1, C)
        rows = acc.reshape(8 * S, C)
        centred = rows - jnp.mean(rows, axis=1, keepdims=True)
        istd = 1.0 / jnp.sqrt(jnp.mean(centred * centred, axis=1, keepdims=True) + 1e-06)
        xhat = centred * istd
        q = pl.ds(pl.multiple_of(b * 256, 256), 256)
        xhat_ref[q, :] = xhat
        istd_ref[q, :] = jnp.broadcast_to(istd, (256, 128))
        normed_ref[q, :] = (xhat * gain + shift).astype(BF)
        return carry

    lax.fori_loop(0, 4, forward_rows, 0)

    def block_rows(b, carry):
        q = pl.ds(pl.multiple_of(b * 256, 256), 256)
        normed = normed_ref[q, :]
        cot = cot_ref[q, :]
        out = field_ref[pl.ds(b * 8, 8)].reshape(256, C).astype(F32) + b_out
        dnorm = jnp.zeros((256, C), F32)
        sums = []
        for n in range(4):
            h = slice(256 * n, 256 * n + 256)
            z = jnp.dot(normed, w_in_ref[:, h], preferred_element_type=F32) + b_in_ref[:, h]
            dact = lax.dot_general(
                cot, w_out_ref[h, :], (((1,), (1,)), ((), ())), preferred_element_type=F32
            )
            z2 = z * z
            half = 0.5 + 0.5 * jnp.tanh(z * (GELU_C + (GELU_C * 0.044715) * z2))
            act = z * half
            slope = half + act * (1.0 - half) * (2 * GELU_C + (6 * GELU_C * 0.044715) * z2)
            act = act.astype(BF)
            dhid = (dact * slope).astype(BF)
            active_ref[q, h] = act
            dhid_ref[q, h] = dhid
            sums.append(jnp.sum(dhid.astype(F32), axis=0, keepdims=True))
            out = out + jnp.dot(act, w_out_ref[h, :], preferred_element_type=F32)
            dnorm = dnorm + lax.dot_general(
                dhid, w_in_ref[:, h], (((1,), (1,)), ((), ())), preferred_element_type=F32
            )
        blocks_ref[q, :] = out.astype(BF)
        xhat = xhat_ref[q, :]
        dunit = dnorm * gain
        dconv = istd_ref[q, 0:1] * (
            dunit
            - jnp.mean(dunit, axis=1, keepdims=True)
            - xhat * jnp.mean(dunit * xhat, axis=1, keepdims=True)
        )
        dconv_ref[pl.ds(b * 8, 8)] = dconv.astype(BF).astype(F32).reshape(8, S, C)
        g_gain = jnp.sum(dnorm * xhat, axis=0, keepdims=True)
        g_shift = jnp.sum(dnorm, axis=0, keepdims=True)
        g_bout = jnp.sum(cot.astype(F32), axis=0, keepdims=True)
        return tuple(a + x for a, x in zip(carry, sums + [g_gain, g_shift, g_bout]))

    zero = jnp.zeros((1, C), F32)
    *g_bin, g_gain, g_shift, g_bout = lax.fori_loop(0, 4, block_rows, (zero,) * 7)

    def put_rows(first, value):
        mine = core == first // 16
        base = first % 16

        @pl.when(mine)
        def _():
            own_ref[pl.ds(base, 4), pl.ds(0, 64), :] = value.reshape(4, 64, C)

        @pl.when(jnp.logical_not(mine))
        def _():
            send_ref[pl.ds(base, 4), pl.ds(0, 64), :] = value.reshape(4, 64, C).astype(BF)

    for n in range(4):
        h = slice(256 * n, 256 * n + 256)
        over_rows = (((0,), (0,)), ((), ()))
        put_rows(
            4 * n,
            lax.dot_general(normed_ref[...], dhid_ref[:, h], over_rows, preferred_element_type=F32),
        )
        put_rows(
            16 + 4 * n,
            lax.dot_general(active_ref[:, h], cot_ref[...], over_rows, preferred_element_type=F32),
        )

    taps = [kern_ref[k : k + 1, :].reshape(1, 1, C) for k in range(9)]
    g_kernel = []
    for u in range(3):
        for v in range(3):

            def tap_rows(b, acc, u=u, v=v):
                part = pad_ref[v, pl.ds(b * 4 + u, 4)] * dconv_ref[pl.ds(b * 4, 4)]
                return acc + jnp.sum(part.reshape(4 * S // 8, 8, C), axis=0)

            acc = lax.fori_loop(0, 8, tap_rows, jnp.zeros((8, C), F32))
            g_kernel.append(jnp.sum(acc, axis=0, keepdims=True))

    def bias_rows(b, acc):
        return acc + jnp.sum(dconv_ref[pl.ds(b * 4, 4)].reshape(4 * S // 8, 8, C), axis=0)

    g_bias = jnp.sum(lax.fori_loop(0, 8, bias_rows, jnp.zeros((8, C), F32)), axis=0, keepdims=True)

    small = g_kernel + [g_bias, g_gain, g_shift, g_bout] + g_bin + [zero] * 15
    row8 = lax.broadcasted_iota(jnp.int32, (CHUNK - 64, C), 0)
    for j in range(32):
        row = jnp.where(row8 == 0, small[j], 0.0)

        @pl.when(core == j // 16)
        def _(row=row, j=j):
            own_ref[j % 16, pl.ds(64, CHUNK - 64), :] = row

        @pl.when(core != j // 16)
        def _(row=row, j=j):
            send_ref[j % 16, pl.ds(64, CHUNK - 64), :] = row.astype(BF)

    pad_ref[:, 0] = jnp.zeros((3, S, C), F32)
    pad_ref[:, S + 1] = jnp.zeros((3, S, C), F32)
    col = lax.broadcasted_iota(jnp.int32, (S, C), 0)

    def shift_rows(i, carry):
        row = dconv_ref[i]
        pad_ref[1, i + 1] = row
        pad_ref[0, i + 1] = jnp.where(col == S - 1, 0.0, pltpu.roll(row, S - 1, 0))
        pad_ref[2, i + 1] = jnp.where(col == 0, 0.0, pltpu.roll(row, 1, 0))
        return carry

    lax.fori_loop(0, S, shift_rows, 0)

    def inner_rows(b, carry):
        acc = jnp.zeros((4, S, C), F32)
        for u in range(3):
            for v in range(3):
                acc = acc + pad_ref[v, pl.ds(b * 4 + 2 - u, 4)] * taps[3 * u + v]
        inner_ref[pl.ds(b * 4, 4)] = acc
        return carry

    lax.fori_loop(0, 8, inner_rows, 0)

    def flat(k):
        return kern_ref[k : k + 1, :]

    top = sum(pad_ref[v, 1] * flat(v) for v in range(3))
    bottom = sum(pad_ref[v, S] * flat(6 + v) for v in range(3))
    left_col = dconv_ref[:, 0, :]
    right_col = dconv_ref[:, S - 1, :]

    def side(column, v):
        below = jnp.where(col == S - 1, 0.0, pltpu.roll(column, S - 1, 0))
        above = jnp.where(col == 0, 0.0, pltpu.roll(column, 1, 0))
        return below * flat(v) + column * flat(3 + v) + above * flat(6 + v)

    corners = [
        dconv_ref[0, pl.ds(0, 1), :] * flat(0),
        dconv_ref[0, pl.ds(S - 1, 1), :] * flat(2),
        dconv_ref[S - 1, pl.ds(0, 1), :] * flat(6),
        dconv_ref[S - 1, pl.ds(S - 1, 1), :] * flat(8),
    ]
    put_edges(rim_ref, [top, bottom, side(left_col, 0), side(right_col, 2)], corners)


def join_kernel(pos_ref, seam_ref, corner_ref, cot_ref, inner_ref, recv_ref, out_ref, acc_ref):
    strips, cells = take_slots(recv_ref, pos_ref[0], seam_ref, corner_ref)
    acc_ref[...] = cot_ref[...].astype(F32) + inner_ref[...]
    acc_ref[0] = acc_ref[0] + strips[0]
    acc_ref[S - 1] = acc_ref[S - 1] + strips[1]
    acc_ref[:, 0, :] = acc_ref[:, 0, :] + strips[2]
    acc_ref[:, S - 1, :] = acc_ref[:, S - 1, :] + strips[3]
    for n, (i, j) in enumerate(((0, 0), (0, S - 1), (S - 1, 0), (S - 1, S - 1))):
        acc_ref[i, pl.ds(j, 1), :] = acc_ref[i, pl.ds(j, 1), :] + cells[n]
    out_ref[...] = acc_ref[...].astype(BF)


def scale_kernel(
    at_ref, own_ref, other_ref, kern_ref, chan_ref, w_in_ref, b_in_ref, w_out_ref, entries
):
    core, x0, y0 = at_ref[1], at_ref[2], at_ref[3]
    halves = (own_ref, other_ref)
    sums = []
    for half in range(2):
        def one_half(j, acc, half=half):
            a = own_ref[j].astype(F32)
            b = other_ref[j].astype(F32)
            v = jnp.where(core == half, a, b)
            return acc + jnp.sum((v * v).reshape(CHUNK // 8, 8, C), axis=0)

        def ordered(j, acc, one_half=one_half):
            k = ((j // 4 - x0 + 4) % 4) * 4 + (j % 4 - y0 + 4) % 4
            return one_half(k, acc)

        sums.append(lax.fori_loop(0, 16, ordered, jnp.zeros((8, C), F32)))
    total = jnp.sum(jnp.sum(sums[0] + sums[1], axis=0, keepdims=True), axis=1, keepdims=True)
    scale = 1.0 / jnp.sqrt(total / entries + 1e-06)

    for j in range(32):
        c, x, y = j // 16, (j // 4) % 4, j % 4
        k = ((x - x0 + 4) % 4) * 4 + (y - y0 + 4) % 4

        def emit(ref, j=j, k=k):
            rows = ref[k, pl.ds(0, 64), :].astype(F32) * scale
            if j < 16:
                w_in_ref[64 * (j % 4) : 64 * (j % 4) + 64, 256 * (j // 4) : 256 * (j // 4) + 256] = rows
            else:
                w_out_ref[64 * (j - 16) : 64 * (j - 16) + 64, :] = rows
            row = ref[k, pl.ds(64, 8), :].astype(F32)[0:1] * scale
            if j < 9:
                kern_ref[j : j + 1, :] = row
            elif j < 13:
                chan_ref[j - 9 : j - 8, :] = row
            elif j < 17:
                b_in_ref[:, 256 * (j - 13) : 256 * (j - 13) + 256] = row

        for near in range(2):

            @pl.when((core == c) == (near == 1))
            def _(emit=emit, near=near):
                emit(halves[1 - near])


def at(y, x, h, c):
    return ((y * 4 + x) * 2 + h) * 2 + c


def moves(axis, d):
    pairs = []
    for y in range(4):
        for x in range(4):
            for h in range(2):
                for c in range(2):
                    to = {
                        "y": ((y + d) % 4, x, h, c),
                        "x": (y, (x + d) % 4, h, c),
                        "h": (y, x, 1 - h, c),
                        "c": (y, x, h, 1 - c),
                    }[axis]
                    pairs.append((at(y, x, h, c), at(*to)))
    return pairs


def exchange(slots):
    halves = [[at(p // 8, p // 2 % 4, h, p % 2) for p in range(32)] for h in range(2)]
    return lax.all_to_all(slots, "space", 0, 0, axis_index_groups=halves, tiled=True)


def z_moves(d):
    pairs = []
    for y in range(4):
        for x in range(4):
            for c in range(2):
                for z in range(8):
                    to = (z + d) % 8
                    pairs.append((at(y, x, z // 4, c) * 4 + z % 4, at(y, x, to // 4, c) * 4 + to % 4))
    return pairs


def sum_over_devices(own, send, x, y, later):
    rest = own + lax.ppermute(send, "space", moves("c", 1)).astype(F32)
    for axis, place, n in (("x", x, 4), ("y", y, 1)):
        parts = rest.reshape(4, n, CHUNK, C)
        pick = lambda d: lax.dynamic_slice(
            parts, ((place + jnp.uint32(d)) & jnp.uint32(3),) + (jnp.uint32(0),) * 3, (1, n, CHUNK, C)
        )[0]
        got = [lax.ppermute(pick(d).astype(BF), "space", moves(axis, d)) for d in (1, 2, 3)]
        rest = pick(0) + (got[0].astype(F32) + got[1].astype(F32) + got[2].astype(F32))
        if axis == "y":
            rest, later = lax.optimization_barrier((rest, later))
    piece = rest.reshape(CHUNK, C).astype(BF)
    got = [lax.ppermute(piece, ("space", "batch"), z_moves(d)) for d in range(1, 8)]
    v = [p.astype(F32) for p in [piece] + got]
    piece = ((v[0] + v[4]) + (v[2] + v[6])) + ((v[1] + v[5]) + (v[3] + v[7]))
    full = piece.astype(BF)[None]
    for axis in ("y", "x"):
        got = [lax.ppermute(full, "space", moves(axis, -d)) for d in (1, 2, 3)]
        full = jnp.stack([full] + got).reshape(-1, CHUNK, C)
    return full, lax.ppermute(full, "space", moves("c", 1)), later


def shards(
    fields,
    cotangent,
    dw_kernel,
    dw_bias,
    ln_gain,
    ln_shift,
    w_in,
    b_in,
    w_out,
    b_out,
    seam_links,
    corner_links,
):
    pos = lax.axis_index("space")
    core = pos & 1
    x = (pos >> 2) & 3
    y = pos >> 4
    here = jnp.stack([pos, core, x, y])
    field = fields[0, 0]
    cot = cotangent[0, 0]
    sds = jax.ShapeDtypeStruct
    edges = sds((EDGE, C), BF)

    def to_slots(mine):
        return pl.pallas_call(
            slot_kernel,
            out_shape=sds((32, SLOT, C), BF),
            in_specs=[SMEM(), SMEM(), VMEM(), VMEM()],
            out_specs=VMEM(),
            compiler_params=params(6),
            name="slots",
        )(here, seam_links, mine, lax.ppermute(mine, "space", moves("h", 1)))

    field_edges = pl.pallas_call(
        edge_kernel,
        out_shape=edges,
        in_specs=[VMEM()],
        out_specs=VMEM(),
        scratch_shapes=[pltpu.VMEM((S, S, C), F32)],
        compiler_params=params(8),
        name="edges",
    )(field)
    halo = exchange(to_slots(field_edges))

    vectors = jnp.stack([dw_bias, ln_gain, ln_shift, b_out])
    cells = S * S
    blocks, inner, rim, own, send = pl.pallas_call(
        tile_kernel,
        out_shape=(
            sds((cells, C), BF),
            sds((S, S, C), F32),
            edges,
            sds((16, CHUNK, C), F32),
            sds((16, CHUNK, C), BF),
        ),
        in_specs=[SMEM()] * 3 + [VMEM()] * 8,
        out_specs=(VMEM(),) * 5,
        scratch_shapes=[
            pltpu.VMEM((3, S + 2, S, C), F32),
            pltpu.VMEM((cells, C), F32),
            pltpu.VMEM((cells, 128), F32),
            pltpu.VMEM((cells, C), BF),
            pltpu.VMEM((cells, H), BF),
            pltpu.VMEM((cells, H), BF),
            pltpu.VMEM((8, C), F32),
            pltpu.VMEM((S, S, C), F32),
        ],
        compiler_params=params(28),
        name="tile",
    )(
        here,
        seam_links,
        corner_links,
        field,
        cot.reshape(cells, C),
        halo,
        dw_kernel,
        vectors,
        w_in,
        b_in.reshape(1, H),
        w_out,
    )
    near, far, rim_slots = sum_over_devices(
        own, send, x.astype(jnp.uint32), y.astype(jnp.uint32), to_slots(rim)
    )
    back = exchange(rim_slots)
    grad_tile = pl.pallas_call(
        join_kernel,
        out_shape=sds((S, S, C), BF),
        in_specs=[SMEM()] * 3 + [VMEM()] * 3,
        out_specs=VMEM(),
        scratch_shapes=[pltpu.VMEM((S, S, C), F32)],
        compiler_params=params(10),
        name="join",
    )(here, seam_links, corner_links, cot, inner, back)

    entries = 13 * C + 2 * C * H + H
    grad_kernel, grad_channels, grad_w_in, grad_b_in, grad_w_out = pl.pallas_call(
        functools.partial(scale_kernel, entries=entries),
        out_shape=(
            sds((9, C), F32),
            sds((4, C), F32),
            sds((C, H), F32),
            sds((1, H), F32),
            sds((H, C), F32),
        ),
        in_specs=[SMEM(), VMEM(), VMEM()],
        out_specs=(VMEM(),) * 5,
        compiler_params=params(10),
        name="scale",
    )(here, near, far)
    return (
        blocks.reshape(1, 1, S, S, C),
        grad_tile[None, None],
        grad_kernel,
        grad_channels,
        grad_w_in,
        grad_b_in.reshape(H),
        grad_w_out,
    )


def solution(mesh):
    tile = P("batch", "space", None, None, None)
    return jax.shard_map(
        shards,
        mesh=mesh,
        in_specs=(tile, tile) + (P(),) * 10,
        out_specs=(tile, tile) + (P(),) * 5,
        check_vma=False,
    )
```

```python
import functools

import jax
import jax.numpy as jnp
from jax import lax
from jax.experimental import pallas as pl
from jax.experimental.pallas import tpu as pltpu
from jax.sharding import PartitionSpec as P

S = 32
C = 256
H = 1024
SLOT = 72
EDGE = 136
CHUNK = 72
BF = jnp.bfloat16
F32 = jnp.float32
GELU_C = 0.7978845608028654
VMEM = functools.partial(pl.BlockSpec, memory_space=pltpu.VMEM)
SMEM = functools.partial(pl.BlockSpec, memory_space=pltpu.SMEM)


def params(mib):
    return pltpu.CompilerParams(vmem_limit_bytes=mib * 1024 * 1024)


def put_edges(out_ref, strips, cells):
    for e in range(4):
        out_ref[pl.ds(S * e, S), :] = strips[e].astype(BF)
    cells8 = jnp.concatenate([c.reshape(1, C) for c in cells] + [jnp.zeros((4, C), F32)], axis=0)
    out_ref[pl.ds(4 * S, 8), :] = cells8.astype(BF)


def half_of(tile):
    return (tile // 2) % 2


def place_of(tile):
    return (tile // 4) * 2 + tile % 2


def take_slots(recv_ref, pos, seam_ref, corner_ref):
    rows = lax.broadcasted_iota(jnp.int32, (S, S), 0)
    cols = lax.broadcasted_iota(jnp.int32, (S, S), 1)
    strips = []
    for e in range(4):
        code = seam_ref[pos, e]
        tile = code // 8
        target = jnp.where(code % 2 == 1, S - 1 - rows, rows)
        turn = (cols == target).astype(F32).astype(BF)
        strip = recv_ref[place_of(tile), pl.ds(pl.multiple_of(S * half_of(tile), S), S), :]
        strips.append(jnp.dot(turn, strip, preferred_element_type=F32))
    cells = []
    row8 = lax.broadcasted_iota(jnp.int32, (SLOT - 2 * S, C), 0)
    for k in range(4):
        code = corner_ref[pos, k]
        tile = code // 4
        block = recv_ref[place_of(tile), pl.ds(2 * S, SLOT - 2 * S), :].astype(F32)
        row = 4 * half_of(tile) + code % 4
        cells.append(jnp.sum(jnp.where(row8 == row, block, 0.0), axis=0, keepdims=True))
    return strips, cells


def edge_kernel(field_ref, out_ref, wide_ref):
    wide_ref[...] = field_ref[...].astype(F32)
    strips = [wide_ref[0], wide_ref[S - 1], wide_ref[:, 0, :], wide_ref[:, S - 1, :]]
    cells = [wide_ref[i, pl.ds(j, 1), :] for i in (0, S - 1) for j in (0, S - 1)]
    put_edges(out_ref, strips, cells)


def slot_kernel(pos_ref, seam_ref, own_ref, other_ref, out_ref):
    pos = pos_ref[0]
    half = half_of(pos)
    mine = own_ref[pl.ds(4 * S, 8), :].astype(F32)
    other = other_ref[pl.ds(4 * S, 8), :].astype(F32)
    row8 = lax.broadcasted_iota(jnp.int32, (8, C), 0)
    first = jnp.where(half == 0, mine, other)
    second = jnp.where(half == 0, other, mine)
    cells8 = jnp.where(row8 < 4, first, pltpu.roll(second, 4, 0)).astype(BF)

    def put(p, carry):
        out_ref[p, pl.ds(2 * S, SLOT - 2 * S), :] = cells8
        return carry

    lax.fori_loop(0, 32, put, 0)
    for source, edges, at_half in ((pos, own_ref, half), (pos ^ 2, other_ref, 1 - half)):
        for e in range(4):
            tile = seam_ref[source, e] // 8

            @pl.when(half_of(tile) == half)
            def _(tile=tile, edges=edges, at_half=at_half, e=e):
                rows = pl.ds(pl.multiple_of(S * at_half, S), S)
                out_ref[place_of(tile), rows, :] = edges[pl.ds(S * e, S), :]


def tile_kernel(
    pos_ref,
    seam_ref,
    corner_ref,
    field_ref,
    cot_ref,
    recv_ref,
    kern_ref,
    vec_ref,
    w_in_ref,
    b_in_ref,
    w_out_ref,
    blocks_ref,
    inner_ref,
    rim_ref,
    own_ref,
    send_ref,
    pad_ref,
    xhat_ref,
    istd_ref,
    normed_ref,
    active_ref,
    dhid_ref,
    dnorm_ref,
    dconv_ref,
):
    pos = pos_ref[0]
    core = pos_ref[1]
    strips, cells = take_slots(recv_ref, pos, seam_ref, corner_ref)
    center = field_ref[...].astype(F32)
    pad_ref[1, pl.ds(1, S)] = center
    pad_ref[1, 0] = strips[0]
    pad_ref[1, S + 1] = strips[1]
    pad_ref[0, pl.ds(1, S)] = pltpu.roll(center, 1, 1)
    pad_ref[2, pl.ds(1, S)] = pltpu.roll(center, S - 1, 1)
    pad_ref[0, 0] = pltpu.roll(strips[0], 1, 0)
    pad_ref[2, 0] = pltpu.roll(strips[0], S - 1, 0)
    pad_ref[0, S + 1] = pltpu.roll(strips[1], 1, 0)
    pad_ref[2, S + 1] = pltpu.roll(strips[1], S - 1, 0)
    pad_ref[0, pl.ds(1, S), 0, :] = strips[2]
    pad_ref[2, pl.ds(1, S), S - 1, :] = strips[3]
    pad_ref[0, 0, pl.ds(0, 1), :] = cells[0]
    pad_ref[2, 0, pl.ds(S - 1, 1), :] = cells[1]
    pad_ref[0, S + 1, pl.ds(0, 1), :] = cells[2]
    pad_ref[2, S + 1, pl.ds(S - 1, 1), :] = cells[3]

    bias = vec_ref[0:1, :]
    gain = vec_ref[1:2, :]
    shift = vec_ref[2:3, :]
    b_out = vec_ref[3:4, :]

    def forward_rows(b, carry):
        r0 = b * 8
        acc = jnp.zeros((8, S, C), F32) + bias.reshape(1, 1, C)
        for u in range(3):
            for v in range(3):
                k = 3 * u + v
                acc = acc + pad_ref[v, pl.ds(r0 + u, 8)] * kern_ref[k : k + 1, :].reshape(1, 1, C)
        rows = acc.reshape(8 * S, C)
        centred = rows - jnp.mean(rows, axis=1, keepdims=True)
        istd = 1.0 / jnp.sqrt(jnp.mean(centred * centred, axis=1, keepdims=True) + 1e-06)
        xhat = centred * istd
        q = pl.ds(pl.multiple_of(b * 256, 256), 256)
        xhat_ref[q, :] = xhat
        istd_ref[q, :] = jnp.broadcast_to(istd, (256, 128))
        normed_ref[q, :] = (xhat * gain + shift).astype(BF)
        return carry

    lax.fori_loop(0, 4, forward_rows, 0)

    def block_rows(b, carry):
        q = pl.ds(pl.multiple_of(b * 256, 256), 256)
        normed = normed_ref[q, :]
        cot = cot_ref[q, :]
        out = field_ref[pl.ds(b * 8, 8)].reshape(256, C).astype(F32) + b_out
        dnorm = jnp.zeros((256, C), F32)
        sums = []
        for n in range(4):
            h = slice(256 * n, 256 * n + 256)
            z = jnp.dot(normed, w_in_ref[:, h], preferred_element_type=F32) + b_in_ref[:, h]
            dact = lax.dot_general(
                cot, w_out_ref[h, :], (((1,), (1,)), ((), ())), preferred_element_type=F32
            )
            z2 = z * z
            half = 0.5 + 0.5 * jnp.tanh(z * (GELU_C + (GELU_C * 0.044715) * z2))
            act = z * half
            slope = half + act * (1.0 - half) * (2 * GELU_C + (6 * GELU_C * 0.044715) * z2)
            act = act.astype(BF)
            dhid = (dact * slope).astype(BF)
            active_ref[q, h] = act
            dhid_ref[q, h] = dhid
            sums.append(jnp.sum(dhid.astype(F32), axis=0, keepdims=True))
            out = out + jnp.dot(act, w_out_ref[h, :], preferred_element_type=F32)
            dnorm = dnorm + lax.dot_general(
                dhid, w_in_ref[:, h], (((1,), (1,)), ((), ())), preferred_element_type=F32
            )
        blocks_ref[q, :] = out.astype(BF)
        xhat = xhat_ref[q, :]
        dunit = dnorm * gain
        dconv = istd_ref[q, 0:1] * (
            dunit
            - jnp.mean(dunit, axis=1, keepdims=True)
            - xhat * jnp.mean(dunit * xhat, axis=1, keepdims=True)
        )
        dconv_ref[pl.ds(b * 8, 8)] = dconv.astype(BF).astype(F32).reshape(8, S, C)
        g_gain = jnp.sum(dnorm * xhat, axis=0, keepdims=True)
        g_shift = jnp.sum(dnorm, axis=0, keepdims=True)
        g_bout = jnp.sum(cot.astype(F32), axis=0, keepdims=True)
        return tuple(a + x for a, x in zip(carry, sums + [g_gain, g_shift, g_bout]))

    zero = jnp.zeros((1, C), F32)
    *g_bin, g_gain, g_shift, g_bout = lax.fori_loop(0, 4, block_rows, (zero,) * 7)

    def put_rows(first, value):
        mine = core == first // 16
        base = first % 16

        @pl.when(mine)
        def _():
            own_ref[pl.ds(base, 4), pl.ds(0, 64), :] = value.reshape(4, 64, C)

        @pl.when(jnp.logical_not(mine))
        def _():
            send_ref[pl.ds(base, 4), pl.ds(0, 64), :] = value.reshape(4, 64, C).astype(BF)

    for n in range(4):
        h = slice(256 * n, 256 * n + 256)
        over_rows = (((0,), (0,)), ((), ()))
        put_rows(
            4 * n,
            lax.dot_general(normed_ref[...], dhid_ref[:, h], over_rows, preferred_element_type=F32),
        )
        put_rows(
            16 + 4 * n,
            lax.dot_general(active_ref[:, h], cot_ref[...], over_rows, preferred_element_type=F32),
        )

    taps = [kern_ref[k : k + 1, :].reshape(1, 1, C) for k in range(9)]
    g_kernel = []
    for u in range(3):
        for v in range(3):

            def tap_rows(b, acc, u=u, v=v):
                part = pad_ref[v, pl.ds(b * 4 + u, 4)] * dconv_ref[pl.ds(b * 4, 4)]
                return acc + jnp.sum(part.reshape(4 * S // 8, 8, C), axis=0)

            acc = lax.fori_loop(0, 8, tap_rows, jnp.zeros((8, C), F32))
            g_kernel.append(jnp.sum(acc, axis=0, keepdims=True))

    def bias_rows(b, acc):
        return acc + jnp.sum(dconv_ref[pl.ds(b * 4, 4)].reshape(4 * S // 8, 8, C), axis=0)

    g_bias = jnp.sum(lax.fori_loop(0, 8, bias_rows, jnp.zeros((8, C), F32)), axis=0, keepdims=True)

    small = g_kernel + [g_bias, g_gain, g_shift, g_bout] + g_bin + [zero] * 15
    row8 = lax.broadcasted_iota(jnp.int32, (CHUNK - 64, C), 0)
    for j in range(32):
        row = jnp.where(row8 == 0, small[j], 0.0)

        @pl.when(core == j // 16)
        def _(row=row, j=j):
            own_ref[j % 16, pl.ds(64, CHUNK - 64), :] = row

        @pl.when(core != j // 16)
        def _(row=row, j=j):
            send_ref[j % 16, pl.ds(64, CHUNK - 64), :] = row.astype(BF)

    pad_ref[:, 0] = jnp.zeros((3, S, C), F32)
    pad_ref[:, S + 1] = jnp.zeros((3, S, C), F32)
    col = lax.broadcasted_iota(jnp.int32, (S, C), 0)

    def shift_rows(i, carry):
        row = dconv_ref[i]
        pad_ref[1, i + 1] = row
        pad_ref[0, i + 1] = jnp.where(col == S - 1, 0.0, pltpu.roll(row, S - 1, 0))
        pad_ref[2, i + 1] = jnp.where(col == 0, 0.0, pltpu.roll(row, 1, 0))
        return carry

    lax.fori_loop(0, S, shift_rows, 0)

    def inner_rows(b, carry):
        acc = jnp.zeros((4, S, C), F32)
        for u in range(3):
            for v in range(3):
                acc = acc + pad_ref[v, pl.ds(b * 4 + 2 - u, 4)] * taps[3 * u + v]
        inner_ref[pl.ds(b * 4, 4)] = acc
        return carry

    lax.fori_loop(0, 8, inner_rows, 0)

    def flat(k):
        return kern_ref[k : k + 1, :]

    top = sum(pad_ref[v, 1] * flat(v) for v in range(3))
    bottom = sum(pad_ref[v, S] * flat(6 + v) for v in range(3))
    left_col = dconv_ref[:, 0, :]
    right_col = dconv_ref[:, S - 1, :]

    def side(column, v):
        below = jnp.where(col == S - 1, 0.0, pltpu.roll(column, S - 1, 0))
        above = jnp.where(col == 0, 0.0, pltpu.roll(column, 1, 0))
        return below * flat(v) + column * flat(3 + v) + above * flat(6 + v)

    corners = [
        dconv_ref[0, pl.ds(0, 1), :] * flat(0),
        dconv_ref[0, pl.ds(S - 1, 1), :] * flat(2),
        dconv_ref[S - 1, pl.ds(0, 1), :] * flat(6),
        dconv_ref[S - 1, pl.ds(S - 1, 1), :] * flat(8),
    ]
    put_edges(rim_ref, [top, bottom, side(left_col, 0), side(right_col, 2)], corners)


def join_kernel(pos_ref, seam_ref, corner_ref, cot_ref, inner_ref, recv_ref, out_ref, acc_ref):
    strips, cells = take_slots(recv_ref, pos_ref[0], seam_ref, corner_ref)
    acc_ref[...] = cot_ref[...].astype(F32) + inner_ref[...]
    acc_ref[0] = acc_ref[0] + strips[0]
    acc_ref[S - 1] = acc_ref[S - 1] + strips[1]
    acc_ref[:, 0, :] = acc_ref[:, 0, :] + strips[2]
    acc_ref[:, S - 1, :] = acc_ref[:, S - 1, :] + strips[3]
    for n, (i, j) in enumerate(((0, 0), (0, S - 1), (S - 1, 0), (S - 1, S - 1))):
        acc_ref[i, pl.ds(j, 1), :] = acc_ref[i, pl.ds(j, 1), :] + cells[n]
    out_ref[...] = acc_ref[...].astype(BF)


def scale_kernel(
    at_ref, own_ref, other_ref, kern_ref, chan_ref, w_in_ref, b_in_ref, w_out_ref, entries
):
    core = at_ref[1]
    halves = (own_ref, other_ref)
    sums = []
    for half in range(2):
        def one_half(j, acc, half=half):
            v = jnp.where(core == half, own_ref[j].astype(F32), other_ref[j].astype(F32))
            return acc + jnp.sum((v * v).reshape(CHUNK // 8, 8, C), axis=0)

        sums.append(lax.fori_loop(0, 16, one_half, jnp.zeros((8, C), F32)))
    total = jnp.sum(jnp.sum(sums[0] + sums[1], axis=0, keepdims=True), axis=1, keepdims=True)
    scale = 1.0 / jnp.sqrt(total / entries + 1e-06)

    for j in range(32):
        c, k = j // 16, j % 16

        def emit(ref, j=j, k=k):
            rows = ref[k, pl.ds(0, 64), :].astype(F32) * scale
            if j < 16:
                w_in_ref[64 * (j % 4) : 64 * (j % 4) + 64, 256 * (j // 4) : 256 * (j // 4) + 256] = rows
            else:
                w_out_ref[64 * (j - 16) : 64 * (j - 16) + 64, :] = rows
            row = ref[k, pl.ds(64, 8), :].astype(F32)[0:1] * scale
            if j < 9:
                kern_ref[j : j + 1, :] = row
            elif j < 13:
                chan_ref[j - 9 : j - 8, :] = row
            elif j < 17:
                b_in_ref[:, 256 * (j - 13) : 256 * (j - 13) + 256] = row

        for near in range(2):

            @pl.when((core == c) == (near == 1))
            def _(emit=emit, near=near):
                emit(halves[1 - near])


def at(y, x, h, c):
    return ((y * 4 + x) * 2 + h) * 2 + c


def moves(axis, d):
    pairs = []
    for y in range(4):
        for x in range(4):
            for h in range(2):
                for c in range(2):
                    to = {
                        "y": ((y + d) % 4, x, h, c),
                        "x": (y, (x + d) % 4, h, c),
                        "h": (y, x, 1 - h, c),
                        "c": (y, x, h, 1 - c),
                    }[axis]
                    pairs.append((at(y, x, h, c), at(*to)))
    return pairs


def exchange(slots):
    halves = [[at(p // 8, p // 2 % 4, h, p % 2) for p in range(32)] for h in range(2)]
    return lax.all_to_all(slots, "space", 0, 0, axis_index_groups=halves, tiled=True)


def plane(slots):
    planes = [
        [at(p % 4, p // 4, h, c) for p in range(16)] for h in range(2) for c in range(2)
    ]
    return lax.all_to_all(slots, "space", 0, 0, axis_index_groups=planes, tiled=True)


def sum_over_devices(own, send, slots):
    rest = own + lax.ppermute(send, "space", moves("c", 1)).astype(F32)
    parts = plane(rest.astype(BF))
    piece = jnp.sum(parts.astype(F32), axis=0)
    piece, slots = lax.optimization_barrier((piece, slots))
    back = exchange(slots)
    piece = piece + lax.ppermute(piece, "space", moves("h", 1))
    turn = lambda d: [(i, (i + d) % 4) for i in range(4)]
    mine = piece.astype(BF)
    got = [mine] + [lax.ppermute(mine, "batch", turn(d)) for d in (1, 2, 3)]
    got = [g.astype(F32) for g in got]
    piece = (got[0] + got[2]) + (got[1] + got[3])
    piece, back = lax.optimization_barrier((piece.astype(BF), back))
    full = plane(jnp.broadcast_to(piece[None], (16, CHUNK, C)))
    return full, lax.ppermute(full, "space", moves("c", 1)), back


def shards(
    fields,
    cotangent,
    dw_kernel,
    dw_bias,
    ln_gain,
    ln_shift,
    w_in,
    b_in,
    w_out,
    b_out,
    seam_links,
    corner_links,
):
    pos = lax.axis_index("space")
    here = jnp.stack([pos, pos & 1])
    field = fields[0, 0]
    cot = cotangent[0, 0]
    sds = jax.ShapeDtypeStruct
    edges = sds((EDGE, C), BF)

    def to_slots(mine):
        return pl.pallas_call(
            slot_kernel,
            out_shape=sds((32, SLOT, C), BF),
            in_specs=[SMEM(), SMEM(), VMEM(), VMEM()],
            out_specs=VMEM(),
            compiler_params=params(6),
            name="slots",
        )(here, seam_links, mine, lax.ppermute(mine, "space", moves("h", 1)))

    field_edges = pl.pallas_call(
        edge_kernel,
        out_shape=edges,
        in_specs=[VMEM()],
        out_specs=VMEM(),
        scratch_shapes=[pltpu.VMEM((S, S, C), F32)],
        compiler_params=params(8),
        name="edges",
    )(field)
    halo = exchange(to_slots(field_edges))

    vectors = jnp.stack([dw_bias, ln_gain, ln_shift, b_out])
    cells = S * S
    blocks, inner, rim, own, send = pl.pallas_call(
        tile_kernel,
        out_shape=(
            sds((cells, C), BF),
            sds((S, S, C), F32),
            edges,
            sds((16, CHUNK, C), F32),
            sds((16, CHUNK, C), BF),
        ),
        in_specs=[SMEM()] * 3 + [VMEM()] * 8,
        out_specs=(VMEM(),) * 5,
        scratch_shapes=[
            pltpu.VMEM((3, S + 2, S, C), F32),
            pltpu.VMEM((cells, C), F32),
            pltpu.VMEM((cells, 128), F32),
            pltpu.VMEM((cells, C), BF),
            pltpu.VMEM((cells, H), BF),
            pltpu.VMEM((cells, H), BF),
            pltpu.VMEM((8, C), F32),
            pltpu.VMEM((S, S, C), F32),
        ],
        compiler_params=params(28),
        name="tile",
    )(
        here,
        seam_links,
        corner_links,
        field,
        cot.reshape(cells, C),
        halo,
        dw_kernel,
        vectors,
        w_in,
        b_in.reshape(1, H),
        w_out,
    )
    near, far, back = sum_over_devices(own, send, to_slots(rim))
    grad_tile = pl.pallas_call(
        join_kernel,
        out_shape=sds((S, S, C), BF),
        in_specs=[SMEM()] * 3 + [VMEM()] * 3,
        out_specs=VMEM(),
        scratch_shapes=[pltpu.VMEM((S, S, C), F32)],
        compiler_params=params(10),
        name="join",
    )(here, seam_links, corner_links, cot, inner, back)

    entries = 13 * C + 2 * C * H + H
    grad_kernel, grad_channels, grad_w_in, grad_b_in, grad_w_out = pl.pallas_call(
        functools.partial(scale_kernel, entries=entries),
        out_shape=(
            sds((9, C), F32),
            sds((4, C), F32),
            sds((C, H), F32),
            sds((1, H), F32),
            sds((H, C), F32),
        ),
        in_specs=[SMEM(), VMEM(), VMEM()],
        out_specs=(VMEM(),) * 5,
        compiler_params=params(10),
        name="scale",
    )(here, near, far)
    return (
        blocks.reshape(1, 1, S, S, C),
        grad_tile[None, None],
        grad_kernel,
        grad_channels,
        grad_w_in,
        grad_b_in.reshape(H),
        grad_w_out,
    )


def solution(mesh):
    tile = P("batch", "space", None, None, None)
    return jax.shard_map(
        shards,
        mesh=mesh,
        in_specs=(tile, tile) + (P(),) * 10,
        out_specs=(tile, tile) + (P(),) * 5,
        check_vma=False,
    )
```

```python
import functools

import jax
import jax.numpy as jnp
from jax import lax
from jax.experimental import pallas as pl
from jax.experimental.pallas import tpu as pltpu
from jax.sharding import PartitionSpec as P

S = 32
C = 256
H = 1024
SLOT = 72
EDGE = 136
CHUNK = 72
BF = jnp.bfloat16
F32 = jnp.float32
GELU_C = 0.7978845608028654
VMEM = functools.partial(pl.BlockSpec, memory_space=pltpu.VMEM)


def staged_call(kernel, ins, outs, scratch, mib, name, cost=None):
    n_in, n_out = len(ins), len(outs)
    space = {"vmem": pltpu.VMEM, "smem": pltpu.SMEM}
    in_bufs = [space[w](a.shape, a.dtype) for a, w, _ in ins if w != "here"]
    out_bufs = [pltpu.VMEM(o.shape, o.dtype) for o, to_hbm in outs if to_hbm]
    hbm = pl.BlockSpec(memory_space=pltpu.HBM)

    def body(*refs):
        given, results = refs[:n_in], refs[n_in : n_in + n_out]
        rest = list(refs[n_in + n_out :])
        sems = rest.pop(0)
        stages = [rest.pop(0) for _ in in_bufs]
        drains = [rest.pop(0) for _ in out_bufs]
        args, waits, soon, n = [], {}, [], 0
        for i, (ref, (_, where, late)) in enumerate(zip(given, ins)):
            if where == "here":
                args.append(ref)
                continue
            copy = pltpu.make_async_copy(ref, stages[n], sems.at[n])
            copy.start()
            args.append(stages[n])
            n += 1
            if late:
                waits[i] = copy.wait
            else:
                soon.append(copy)
        for copy in soon:
            copy.wait()
        writes = []
        for ref, (_, to_hbm) in zip(results, outs):
            if to_hbm:
                drain = drains.pop(0)
                writes.append(pltpu.make_async_copy(drain, ref, sems.at[n]))
                args.append(drain)
                n += 1
            else:
                args.append(ref)
        kernel(waits, *args, *rest)
        for copy in writes:
            copy.start()
        for copy in writes:
            copy.wait()

    return pl.pallas_call(
        body,
        out_shape=tuple(o for o, _ in outs),
        in_specs=[VMEM() if w == "here" else hbm for _, w, _ in ins],
        out_specs=tuple(hbm if to_hbm else VMEM() for _, to_hbm in outs),
        scratch_shapes=[pltpu.SemaphoreType.DMA((len(in_bufs) + len(out_bufs) + 1,))]
        + in_bufs
        + out_bufs
        + scratch,
        compiler_params=pltpu.CompilerParams(vmem_limit_bytes=mib * 1024 * 1024),
        cost_estimate=cost,
        name=name,
    )(*(a for a, _, _ in ins))


def put_edges(out_ref, strips, cells):
    for e in range(4):
        out_ref[pl.ds(S * e, S), :] = strips[e].astype(BF)
    cells8 = jnp.concatenate([c.reshape(1, C) for c in cells] + [jnp.zeros((4, C), F32)], axis=0)
    out_ref[pl.ds(4 * S, 8), :] = cells8.astype(BF)


def half_of(tile):
    return (tile // 2) % 2


def place_of(tile):
    return (tile // 4) * 2 + tile % 2


def take_slots(recv_ref, pos, seam_ref, corner_ref):
    rows = lax.broadcasted_iota(jnp.int32, (S, S), 0)
    cols = lax.broadcasted_iota(jnp.int32, (S, S), 1)
    strips = []
    for e in range(4):
        code = seam_ref[e, pos]
        tile = code // 8
        target = jnp.where(code % 2 == 1, S - 1 - rows, rows)
        turn = (cols == target).astype(F32).astype(BF)
        strip = recv_ref[place_of(tile), pl.ds(pl.multiple_of(S * half_of(tile), S), S), :]
        strips.append(jnp.dot(turn, strip, preferred_element_type=F32))
    cells = []
    row8 = lax.broadcasted_iota(jnp.int32, (SLOT - 2 * S, C), 0)
    for k in range(4):
        code = corner_ref[k, pos]
        tile = code // 4
        block = recv_ref[place_of(tile), pl.ds(2 * S, SLOT - 2 * S), :].astype(F32)
        row = 4 * half_of(tile) + code % 4
        cells.append(jnp.sum(jnp.where(row8 == row, block, 0.0), axis=0, keepdims=True))
    return strips, cells


def edge_kernel(waits, field_ref, out_ref, wide_ref):
    wide_ref[...] = field_ref[...].astype(F32)
    strips = [wide_ref[0], wide_ref[S - 1], wide_ref[:, 0, :], wide_ref[:, S - 1, :]]
    cells = [wide_ref[i, pl.ds(j, 1), :] for i in (0, S - 1) for j in (0, S - 1)]
    put_edges(out_ref, strips, cells)


def slot_kernel(waits, pos_ref, seam_ref, own_ref, other_ref, out_ref):
    pos = pos_ref[0]
    half = half_of(pos)
    mine = own_ref[pl.ds(4 * S, 8), :].astype(F32)
    other = other_ref[pl.ds(4 * S, 8), :].astype(F32)
    row8 = lax.broadcasted_iota(jnp.int32, (8, C), 0)
    first = jnp.where(half == 0, mine, other)
    second = jnp.where(half == 0, other, mine)
    cells8 = jnp.where(row8 < 4, first, pltpu.roll(second, 4, 0)).astype(BF)

    def put(p, carry):
        out_ref[p, pl.ds(2 * S, SLOT - 2 * S), :] = cells8
        return carry

    lax.fori_loop(0, 32, put, 0)
    for source, edges, at_half in ((pos, own_ref, half), (pos ^ 2, other_ref, 1 - half)):
        for e in range(4):
            tile = seam_ref[e, source] // 8

            @pl.when(half_of(tile) == half)
            def _(tile=tile, edges=edges, at_half=at_half, e=e):
                rows = pl.ds(pl.multiple_of(S * at_half, S), S)
                out_ref[place_of(tile), rows, :] = edges[pl.ds(S * e, S), :]


def mlp_rows(normed, cot, out, gain_parts, w_in_ref, b_in_ref, w_out_ref, keep):
    gain, xhat, istd = gain_parts
    dnorm = jnp.zeros(out.shape, F32)
    sums = []
    for n in range(4):
        h = slice(256 * n, 256 * n + 256)
        z = jnp.dot(normed, w_in_ref[:, h], preferred_element_type=F32) + b_in_ref[:, h]
        dact = lax.dot_general(
            cot, w_out_ref[h, :], (((1,), (1,)), ((), ())), preferred_element_type=F32
        )
        z2 = z * z
        half = 0.5 + 0.5 * jnp.tanh(z * (GELU_C + (GELU_C * 0.044715) * z2))
        act = z * half
        slope = half + act * (1.0 - half) * (2 * GELU_C + (6 * GELU_C * 0.044715) * z2)
        act = act.astype(BF)
        dhid = (dact * slope).astype(BF)
        keep(n, act, dhid)
        sums.append(jnp.sum(dhid.astype(F32), axis=0, keepdims=True))
        out = out + jnp.dot(act, w_out_ref[h, :], preferred_element_type=F32)
        dnorm = dnorm + lax.dot_general(
            dhid, w_in_ref[:, h], (((1,), (1,)), ((), ())), preferred_element_type=F32
        )
    dunit = dnorm * gain
    dconv = istd * (
        dunit
        - jnp.mean(dunit, axis=1, keepdims=True)
        - xhat * jnp.mean(dunit * xhat, axis=1, keepdims=True)
    )
    sums.append(jnp.sum(dnorm * xhat, axis=0, keepdims=True))
    sums.append(jnp.sum(dnorm, axis=0, keepdims=True))
    return out.astype(BF), dconv.astype(BF).astype(F32), sums


def norm_rows(rows):
    centred = rows - jnp.mean(rows, axis=1, keepdims=True)
    istd = 1.0 / jnp.sqrt(jnp.mean(centred * centred, axis=1, keepdims=True) + 1e-06)
    return centred * istd, istd


OVER_ROWS = (((0,), (0,)), ((), ()))


def inside_kernel(
    waits,
    field_ref,
    cot_ref,
    kern_ref,
    bias_ref,
    gain_ref,
    shift_ref,
    b_out_ref,
    w_in_ref,
    b_in_ref,
    w_out_ref,
    blocks_ref,
    base_ref,
    grad_ref,
    pad_ref,
    xhat_ref,
    istd_ref,
    normed_ref,
    active_ref,
    dhid_ref,
    keep_ref,
    dconv_ref,
):
    center = field_ref[...].astype(F32)
    pad_ref[:, 0] = jnp.zeros((3, S, C), F32)
    pad_ref[:, S + 1] = jnp.zeros((3, S, C), F32)
    pad_ref[1, pl.ds(1, S)] = center
    pad_ref[0, pl.ds(1, S)] = pltpu.roll(center, 1, 1)
    pad_ref[2, pl.ds(1, S)] = pltpu.roll(center, S - 1, 1)

    bias = bias_ref[...]
    gain = gain_ref[...]
    shift = shift_ref[...]
    b_out = b_out_ref[...]
    rowid = lax.broadcasted_iota(jnp.int32, (256, C), 0)
    col = rowid & (S - 1)

    def forward_rows(b, carry):
        r0 = b * 8
        acc = jnp.zeros((8, S, C), F32) + bias.reshape(1, 1, C)
        for u in range(3):
            for v in range(3):
                k = 3 * u + v
                acc = acc + pad_ref[v, pl.ds(r0 + u, 8)] * kern_ref[k : k + 1, :].reshape(1, 1, C)
        xhat, istd = norm_rows(acc.reshape(8 * S, C))
        q = pl.ds(pl.multiple_of(b * 256, 256), 256)
        xhat_ref[q, :] = xhat
        istd_ref[q, :] = jnp.broadcast_to(istd, (256, 128))
        normed_ref[q, :] = (xhat * gain + shift).astype(BF)
        row = r0 + (rowid >> 5)
        kept = (col > 0) & (col < S - 1) & (row > 0) & (row < S - 1)
        keep_ref[q, :] = jnp.where(kept, cot_ref[q, :].astype(F32), 0.0).astype(BF)
        return carry

    lax.fori_loop(0, 4, forward_rows, 0)
    waits[7]()
    waits[9]()

    def block_rows(b, carry):
        q = pl.ds(pl.multiple_of(b * 256, 256), 256)

        def keep(n, act, dhid):
            active_ref[q, 256 * n : 256 * n + 256] = act
            dhid_ref[q, 256 * n : 256 * n + 256] = dhid

        out = field_ref[pl.ds(b * 8, 8)].reshape(256, C).astype(F32) + b_out
        parts = (gain, xhat_ref[q, :], istd_ref[q, 0:1])
        out, dconv, sums = mlp_rows(
            normed_ref[q, :], keep_ref[q, :], out, parts, w_in_ref, b_in_ref, w_out_ref, keep
        )
        blocks_ref[q, :] = out
        dconv_ref[pl.ds(b * 8, 8)] = dconv.reshape(8, S, C)
        sums.append(jnp.sum(cot_ref[q, :].astype(F32), axis=0, keepdims=True))
        return tuple(a + x for a, x in zip(carry, sums))

    zero = jnp.zeros((1, C), F32)
    *g_bin, g_gain, g_shift, g_bout = lax.fori_loop(0, 4, block_rows, (zero,) * 7)

    for n in range(4):
        h = slice(256 * n, 256 * n + 256)
        dot = functools.partial(lax.dot_general, dimension_numbers=OVER_ROWS, preferred_element_type=F32)
        g = dot(normed_ref[...], dhid_ref[:, h])
        grad_ref[4 * n : 4 * n + 4, pl.ds(0, 64), :] = g.reshape(4, 64, C)
        g = dot(active_ref[:, h], keep_ref[...])
        grad_ref[16 + 4 * n : 20 + 4 * n, pl.ds(0, 64), :] = g.reshape(4, 64, C)

    g_kernel = []
    for u in range(3):
        for v in range(3):

            def tap_rows(b, acc, u=u, v=v):
                part = pad_ref[v, pl.ds(b * 4 + u, 4)] * dconv_ref[pl.ds(b * 4, 4)]
                return acc + jnp.sum(part.reshape(4 * S // 8, 8, C), axis=0)

            acc = lax.fori_loop(0, 8, tap_rows, jnp.zeros((8, C), F32))
            g_kernel.append(jnp.sum(acc, axis=0, keepdims=True))

    def bias_rows(b, acc):
        return acc + jnp.sum(dconv_ref[pl.ds(b * 4, 4)].reshape(4 * S // 8, 8, C), axis=0)

    g_bias = jnp.sum(lax.fori_loop(0, 8, bias_rows, jnp.zeros((8, C), F32)), axis=0, keepdims=True)

    small = g_kernel + [g_bias, g_gain, g_shift, g_bout] + g_bin + [zero] * 15
    row8 = lax.broadcasted_iota(jnp.int32, (CHUNK - 64, C), 0)
    for j in range(32):
        grad_ref[j, pl.ds(64, CHUNK - 64), :] = jnp.where(row8 == 0, small[j], 0.0)

    def shift_rows(i, carry):
        row = dconv_ref[i]
        pad_ref[1, i + 1] = row
        pad_ref[0, i + 1] = pltpu.roll(row, S - 1, 0)
        pad_ref[2, i + 1] = pltpu.roll(row, 1, 0)
        return carry

    lax.fori_loop(0, S, shift_rows, 0)
    taps = [kern_ref[k : k + 1, :].reshape(1, 1, C) for k in range(9)]

    def inner_rows(b, carry):
        q = pl.ds(pl.multiple_of(b * 4 * S, 4 * S), 4 * S)
        acc = cot_ref[q, :].astype(F32).reshape(4, S, C)
        for u in range(3):
            for v in range(3):
                acc = acc + pad_ref[v, pl.ds(b * 4 + 2 - u, 4)] * taps[3 * u + v]
        base_ref[pl.ds(b * 4, 4)] = acc
        return carry

    lax.fori_loop(0, 8, inner_rows, 0)


def border_kernel(
    waits,
    pos_ref,
    seam_ref,
    corner_ref,
    field_ref,
    cot_ref,
    recv_ref,
    kern_ref,
    bias_ref,
    gain_ref,
    shift_ref,
    b_out_ref,
    w_in_ref,
    b_in_ref,
    w_out_ref,
    part_ref,
    grad_ref,
    blocks_ref,
    lines_ref,
    rim_ref,
    own_ref,
    send_ref,
    wide_ref,
):
    pos = pos_ref[0]
    core = pos % 2
    strips, cells = take_slots(recv_ref, pos, seam_ref, corner_ref)
    top, bottom, left, right = strips
    last = S - 1
    wide_ref[...] = field_ref[...].astype(F32)
    at_row = lambda i: wide_ref[i]
    at_col = lambda j: wide_ref[:, j, :]
    spot = lambda line, i: line[i : i + 1]
    place = lax.broadcasted_iota(jnp.int32, (S, C), 0)
    flat = lambda k: kern_ref[k : k + 1, :]

    bands = [
        (
            (top, at_row(0), at_row(1)),
            ((cells[0], cells[1]), (spot(left, 0), spot(right, 0)), (spot(left, 1), spot(right, 1))),
            lambda a, s: 3 * a + s,
        ),
        (
            (bottom, at_row(last), at_row(last - 1)),
            (
                (cells[2], cells[3]),
                (spot(left, last), spot(right, last)),
                (spot(left, last - 1), spot(right, last - 1)),
            ),
            lambda a, s: 3 * (2 - a) + s,
        ),
        (
            (left, at_col(0), at_col(1)),
            ((cells[0], cells[2]), (spot(top, 0), spot(bottom, 0)), (spot(top, 1), spot(bottom, 1))),
            lambda a, s: 3 * s + a,
        ),
        (
            (right, at_col(last), at_col(last - 1)),
            (
                (cells[1], cells[3]),
                (spot(top, last), spot(bottom, last)),
                (spot(top, last - 1), spot(bottom, last - 1)),
            ),
            lambda a, s: 3 * s + 2 - a,
        ),
    ]
    windows = [[None] * 9 for _ in range(4)]
    rows = []
    for n, (lines, ends, tap) in enumerate(bands):
        acc = jnp.zeros((S, C), F32) + bias_ref[...]
        for a in range(3):
            before = jnp.where(place == 0, ends[a][0], pltpu.roll(lines[a], 1, 0))
            after = jnp.where(place == last, ends[a][1], pltpu.roll(lines[a], last, 0))
            for s, window in enumerate((before, lines[a], after)):
                k = tap(a, s)
                windows[n][k] = window
                acc = acc + window * flat(k)
        rows.append(acc)
    field_rows = jnp.concatenate([lines[1] for lines, _, _ in bands], axis=0)
    wide_ref[...] = cot_ref[...].astype(F32)
    once = (place > 0) & (place < last)
    cot_rows = jnp.concatenate(
        [at_row(0), at_row(last)]
        + [jnp.where(once, at_col(0), 0.0), jnp.where(once, at_col(last), 0.0)],
        axis=0,
    ).astype(BF)

    gain = gain_ref[...]
    waits[11]()
    waits[13]()
    xhat, istd = norm_rows(jnp.concatenate(rows, axis=0))
    normed = (xhat * gain + shift_ref[...]).astype(BF)
    kept = []
    out, dconv, sums = mlp_rows(
        normed,
        cot_rows,
        field_rows + b_out_ref[...],
        (gain, xhat, istd),
        w_in_ref,
        b_in_ref,
        w_out_ref,
        lambda n, act, dhid: kept.append((act, dhid)),
    )
    *g_bin, g_gain, g_shift = sums
    d_lines = [dconv[S * n : S * n + S] for n in range(4)]

    def spread(line, taps):
        back = jnp.where(place == last, 0.0, pltpu.roll(line, last, 0))
        ahead = jnp.where(place == 0, 0.0, pltpu.roll(line, 1, 0))
        return back * flat(taps[0]) + line * flat(taps[1]) + ahead * flat(taps[2])

    def whole(line, at):
        line = jnp.where(place == 0, spot(d_lines[0], at), line)
        return jnp.where(place == last, spot(d_lines[1], at), line)

    row_taps = lambda u: (3 * u, 3 * u + 1, 3 * u + 2)
    col_taps = lambda v: (v, 3 + v, 6 + v)
    rim = [
        spread(d_lines[0], row_taps(0)),
        spread(d_lines[1], row_taps(2)),
        spread(whole(d_lines[2], 0), col_taps(0)),
        spread(whole(d_lines[3], last), col_taps(2)),
    ]
    corners = [
        spot(d_lines[0], 0) * flat(0),
        spot(d_lines[0], last) * flat(2),
        spot(d_lines[1], 0) * flat(6),
        spot(d_lines[1], last) * flat(8),
    ]
    put_edges(rim_ref, rim, corners)
    lines_ref[0] = spread(d_lines[0], row_taps(1))
    lines_ref[1] = spread(d_lines[0], row_taps(2))
    lines_ref[2] = spread(d_lines[1], row_taps(0))
    lines_ref[3] = spread(d_lines[1], row_taps(1))
    lines_ref[4] = spread(d_lines[2], col_taps(1))
    lines_ref[5] = spread(d_lines[2], col_taps(2))
    lines_ref[6] = spread(d_lines[3], col_taps(0))
    lines_ref[7] = spread(d_lines[3], col_taps(1))

    waits[15]()
    def put_rows(first, value):
        mine = core == first // 16
        base = first % 16
        value = value.reshape(4, 64, C) + grad_ref[first : first + 4, pl.ds(0, 64), :]

        @pl.when(mine)
        def _():
            own_ref[pl.ds(base, 4), pl.ds(0, 64), :] = value

        @pl.when(jnp.logical_not(mine))
        def _():
            send_ref[pl.ds(base, 4), pl.ds(0, 64), :] = value.astype(BF)

    for n in range(4):
        act, dhid = kept[n]
        put_rows(4 * n, lax.dot_general(normed, dhid, OVER_ROWS, preferred_element_type=F32))
        put_rows(16 + 4 * n, lax.dot_general(act, cot_rows, OVER_ROWS, preferred_element_type=F32))

    g_kernel = []
    for k in range(9):
        acc = sum(windows[n][k] * d_lines[n] for n in range(4))
        g_kernel.append(jnp.sum(acc, axis=0, keepdims=True))
    zero = jnp.zeros((1, C), F32)
    g_bias = jnp.sum(dconv, axis=0, keepdims=True)
    small = g_kernel + [g_bias, g_gain, g_shift, zero] + g_bin + [zero] * 15
    row8 = lax.broadcasted_iota(jnp.int32, (CHUNK - 64, C), 0)
    for j in range(32):
        row = jnp.where(row8 == 0, small[j], 0.0) + grad_ref[j, pl.ds(64, CHUNK - 64), :]

        @pl.when(core == j // 16)
        def _(row=row, j=j):
            own_ref[j % 16, pl.ds(64, CHUNK - 64), :] = row

        @pl.when(core != j // 16)
        def _(row=row, j=j):
            send_ref[j % 16, pl.ds(64, CHUNK - 64), :] = row.astype(BF)

    waits[14]()
    wide_ref[...] = part_ref[...].astype(F32)
    out = out.astype(F32)
    wide_ref[:, 0, :] = out[2 * S : 3 * S]
    wide_ref[:, last, :] = out[3 * S : 4 * S]
    wide_ref[0] = out[0:S]
    wide_ref[last] = out[S : 2 * S]
    blocks_ref[...] = wide_ref[...].astype(BF)


def join_kernel(
    waits, pos_ref, seam_ref, corner_ref, base_ref, lines_ref, recv_ref, out_ref, acc_ref
):
    strips, cells = take_slots(recv_ref, pos_ref[0], seam_ref, corner_ref)
    last = S - 1
    acc_ref[...] = base_ref[...]
    for i, add in (
        (0, strips[0] + lines_ref[0]),
        (1, lines_ref[1]),
        (last - 1, lines_ref[2]),
        (last, strips[1] + lines_ref[3]),
    ):
        acc_ref[i] = acc_ref[i] + add
    for j, add in (
        (0, strips[2] + lines_ref[4]),
        (1, lines_ref[5]),
        (last - 1, lines_ref[6]),
        (last, strips[3] + lines_ref[7]),
    ):
        acc_ref[:, j, :] = acc_ref[:, j, :] + add
    for n, (i, j) in enumerate(((0, 0), (0, last), (last, 0), (last, last))):
        acc_ref[i, pl.ds(j, 1), :] = acc_ref[i, pl.ds(j, 1), :] + cells[n]
    out_ref[...] = acc_ref[...].astype(BF)


def scale_kernel(
    waits, at_ref, own_ref, other_ref, kern_ref, chan_ref, w_in_ref, b_in_ref, w_out_ref, entries
):
    core = at_ref[0] % 2
    halves = (own_ref, other_ref)
    sums = []
    for half in range(2):
        def one_half(j, acc, half=half):
            v = jnp.where(core == half, own_ref[j].astype(F32), other_ref[j].astype(F32))
            return acc + jnp.sum((v * v).reshape(CHUNK // 8, 8, C), axis=0)

        sums.append(lax.fori_loop(0, 16, one_half, jnp.zeros((8, C), F32)))
    total = jnp.sum(jnp.sum(sums[0] + sums[1], axis=0, keepdims=True), axis=1, keepdims=True)
    scale = 1.0 / jnp.sqrt(total / entries + 1e-06)

    for j in range(32):
        c, k = j // 16, j % 16

        def emit(ref, j=j, k=k):
            rows = ref[k, pl.ds(0, 64), :].astype(F32) * scale
            if j < 16:
                w_in_ref[64 * (j % 4) : 64 * (j % 4) + 64, 256 * (j // 4) : 256 * (j // 4) + 256] = rows
            else:
                w_out_ref[64 * (j - 16) : 64 * (j - 16) + 64, :] = rows
            row = ref[k, pl.ds(64, 8), :].astype(F32)[0:1] * scale
            if j < 9:
                kern_ref[j : j + 1, :] = row
            elif j < 13:
                chan_ref[j - 9 : j - 8, :] = row
            elif j < 17:
                b_in_ref[:, 256 * (j - 13) : 256 * (j - 13) + 256] = row

        for near in range(2):

            @pl.when((core == c) == (near == 1))
            def _(emit=emit, near=near):
                emit(halves[1 - near])


def at(y, x, h, c):
    return ((y * 4 + x) * 2 + h) * 2 + c


def moves(axis, d):
    pairs = []
    for y in range(4):
        for x in range(4):
            for h in range(2):
                for c in range(2):
                    to = {
                        "y": ((y + d) % 4, x, h, c),
                        "x": (y, (x + d) % 4, h, c),
                        "h": (y, x, 1 - h, c),
                        "c": (y, x, h, 1 - c),
                    }[axis]
                    pairs.append((at(y, x, h, c), at(*to)))
    return pairs


def exchange(slots):
    halves = [[at(p // 8, p // 2 % 4, h, p % 2) for p in range(32)] for h in range(2)]
    return lax.all_to_all(slots, "space", 0, 0, axis_index_groups=halves, tiled=True)


def plane(slots):
    planes = [
        [at(p % 4, p // 4, h, c) for p in range(16)] for h in range(2) for c in range(2)
    ]
    return lax.all_to_all(slots, "space", 0, 0, axis_index_groups=planes, tiled=True)


def sum_over_devices(own, send, slots):
    rest = own + lax.ppermute(send, "space", moves("c", 1)).astype(F32)
    parts = plane(rest.astype(BF))
    piece = jnp.sum(parts.astype(F32), axis=0)
    piece, slots = lax.optimization_barrier((piece, slots))
    back = exchange(slots)
    mine = piece.astype(BF)
    piece = mine.astype(F32) + lax.ppermute(mine, "space", moves("h", 1)).astype(F32)
    turn = lambda d: [(i, (i + d) % 4) for i in range(4)]
    mine = piece.astype(BF)
    got = [mine] + [lax.ppermute(mine, "batch", turn(d)) for d in (1, 2, 3)]
    got = [g.astype(F32) for g in got]
    piece = (got[0] + got[2]) + (got[1] + got[3])
    piece, back = lax.optimization_barrier((piece.astype(BF), back))
    full = plane(jnp.broadcast_to(piece[None], (16, CHUNK, C)))
    return full, lax.ppermute(full, "space", moves("c", 1)), back


def shards(
    fields,
    cotangent,
    dw_kernel,
    dw_bias,
    ln_gain,
    ln_shift,
    w_in,
    b_in,
    w_out,
    b_out,
    seam_links,
    corner_links,
):
    here = lax.axis_index("space").reshape(1)
    links, diagonals = seam_links.T, corner_links.T
    field = fields[0, 0]
    cot = cotangent[0, 0]
    sds = jax.ShapeDtypeStruct
    edges = sds((EDGE, C), BF)
    wide = pltpu.VMEM((S, S, C), F32)

    def to_slots(mine):
        other = lax.ppermute(mine, "space", moves("h", 1))
        return staged_call(
            slot_kernel,
            [(here, "smem", 0), (links, "smem", 0), (mine, "vmem", 0), (other, "vmem", 0)],
            [(sds((32, SLOT, C), BF), True)],
            [],
            63,
            "slots",
        )[0]

    (field_edges,) = staged_call(
        edge_kernel, [(field, "vmem", 0)], [(edges, True)], [wide], 63, "edges"
    )
    halo = exchange(to_slots(field_edges))

    cells = S * S
    row = lambda v: (v.reshape(1, -1), "vmem", 0)
    weights = [
        (dw_kernel, "vmem", 0),
        row(dw_bias),
        row(ln_gain),
        row(ln_shift),
        row(b_out),
        (w_in, "vmem", 1),
        row(b_in),
        (w_out, "vmem", 1),
    ]
    part, base, grads = staged_call(
        inside_kernel,
        [(field, "vmem", 0), (cot.reshape(cells, C), "vmem", 0)] + weights,
        [
            (sds((cells, C), BF), True),
            (sds((S, S, C), F32), True),
            (sds((32, CHUNK, C), F32), True),
        ],
        [
            pltpu.VMEM((3, S + 2, S, C), F32),
            pltpu.VMEM((cells, C), F32),
            pltpu.VMEM((cells, 128), F32),
            pltpu.VMEM((cells, C), BF),
            pltpu.VMEM((cells, H), BF),
            pltpu.VMEM((cells, H), BF),
            pltpu.VMEM((cells, C), BF),
            wide,
        ],
        63,
        "inside",
        pl.CostEstimate(
            flops=12 * cells * C * H, bytes_accessed=8 << 20, transcendentals=cells * H
        ),
    )
    where = [(here, "smem", 0), (links, "smem", 0), (diagonals, "smem", 0)]
    blocks, lines, rim, own, send = staged_call(
        border_kernel,
        where
        + [(field, "vmem", 0), (cot, "vmem", 0), (halo, "vmem", 0)]
        + weights
        + [(part.reshape(S, S, C), "vmem", 1), (grads, "vmem", 1)],
        [
            (sds((S, S, C), BF), True),
            (sds((8, S, C), F32), True),
            (edges, True),
            (sds((16, CHUNK, C), F32), True),
            (sds((16, CHUNK, C), BF), True),
        ],
        [wide],
        63,
        "border",
    )
    near, far, back = sum_over_devices(own, send, to_slots(rim))
    (grad_tile,) = staged_call(
        join_kernel,
        where + [(base, "vmem", 0), (lines, "vmem", 0), (back, "here", 0)],
        [(sds((S, S, C), BF), True)],
        [wide],
        10,
        "join",
    )
    entries = 13 * C + 2 * C * H + H
    grad_kernel, grad_channels, grad_w_in, grad_b_in, grad_w_out = staged_call(
        functools.partial(scale_kernel, entries=entries),
        [(here, "smem", 0), (near, "here", 0), (far, "here", 0)],
        [
            (sds((9, C), F32), True),
            (sds((4, C), F32), True),
            (sds((C, H), F32), True),
            (sds((1, H), F32), True),
            (sds((H, C), F32), True),
        ],
        [],
        10,
        "scale",
    )
    return (
        blocks[None, None],
        grad_tile[None, None],
        grad_kernel,
        grad_channels,
        grad_w_in,
        grad_b_in.reshape(H),
        grad_w_out,
    )


def solution(mesh):
    tile = P("batch", "space", None, None, None)
    return jax.shard_map(
        shards,
        mesh=mesh,
        in_specs=(tile, tile) + (P(),) * 10,
        out_specs=(tile, tile) + (P(),) * 5,
        check_vma=False,
    )
```

```python
import functools

import jax
import jax.numpy as jnp
from jax import lax
from jax.experimental import pallas as pl
from jax.experimental.pallas import tpu as pltpu
from jax.sharding import PartitionSpec as P


S = 32
C = 256
H = 1024
SLOT = 72
EDGE = 136
CHUNK = 72
BF = jnp.bfloat16
F32 = jnp.float32
GELU_C = 0.7978845608028654
VMEM = functools.partial(pl.BlockSpec, memory_space=pltpu.VMEM)


def staged_call(kernel, ins, outs, scratch, mib, cost=None):
    n_in, n_out = len(ins), len(outs)
    space = {"vmem": pltpu.VMEM, "smem": pltpu.SMEM}
    in_bufs = [space[w](a.shape, a.dtype) for a, w, _ in ins if w != "here"]
    out_bufs = [pltpu.VMEM(o.shape, o.dtype) for o, to_hbm in outs if to_hbm]
    hbm = pl.BlockSpec(memory_space=pltpu.HBM)

    def body(*refs):
        given, results = refs[:n_in], refs[n_in : n_in + n_out]
        rest = list(refs[n_in + n_out :])
        sems = rest.pop(0)
        stages = [rest.pop(0) for _ in in_bufs]
        drains = [rest.pop(0) for _ in out_bufs]
        args, waits, soon, n = [], {}, [], 0
        for i, (ref, (_, where, late)) in enumerate(zip(given, ins)):
            if where == "here":
                args.append(ref)
                continue
            copy = pltpu.make_async_copy(ref, stages[n], sems.at[n])
            copy.start()
            args.append(stages[n])
            n += 1
            if late:
                waits[i] = copy.wait
            else:
                soon.append(copy)
        for copy in soon:
            copy.wait()
        writes = []
        for ref, (_, to_hbm) in zip(results, outs):
            if to_hbm:
                drain = drains.pop(0)
                writes.append(pltpu.make_async_copy(drain, ref, sems.at[n]))
                args.append(drain)
                n += 1
            else:
                args.append(ref)
        kernel(waits, *args, *rest)
        for copy in writes:
            copy.start()
        for copy in writes:
            copy.wait()

    return pl.pallas_call(
        body,
        out_shape=tuple(o for o, _ in outs),
        in_specs=[VMEM() if w == "here" else hbm for _, w, _ in ins],
        out_specs=tuple(hbm if to_hbm else VMEM() for _, to_hbm in outs),
        scratch_shapes=[pltpu.SemaphoreType.DMA((len(in_bufs) + len(out_bufs) + 1,))]
        + in_bufs
        + out_bufs
        + scratch,
        compiler_params=pltpu.CompilerParams(vmem_limit_bytes=mib * 1024 * 1024),
        cost_estimate=cost,
    )(*(a for a, _, _ in ins))


def put_edges(out_ref, strips, cells):
    for e in range(4):
        out_ref[pl.ds(S * e, S), :] = strips[e].astype(BF)
    cells8 = jnp.concatenate([c.reshape(1, C) for c in cells] + [jnp.zeros((4, C), F32)], axis=0)
    out_ref[pl.ds(4 * S, 8), :] = cells8.astype(BF)


def half_of(tile):
    return (tile // 2) % 2


def place_of(tile):
    return (tile // 4) * 2 + tile % 2


def take_slots(recv_ref, pos, seam_ref, corner_ref):
    rows = lax.broadcasted_iota(jnp.int32, (S, S), 0)
    cols = lax.broadcasted_iota(jnp.int32, (S, S), 1)
    strips = []
    for e in range(4):
        code = seam_ref[e, pos]
        tile = code // 8
        target = jnp.where(code % 2 == 1, S - 1 - rows, rows)
        turn = (cols == target).astype(F32).astype(BF)
        strip = recv_ref[place_of(tile), pl.ds(pl.multiple_of(S * half_of(tile), S), S), :]
        strips.append(jnp.dot(turn, strip, preferred_element_type=F32))
    cells = []
    row8 = lax.broadcasted_iota(jnp.int32, (SLOT - 2 * S, C), 0)
    for k in range(4):
        code = corner_ref[k, pos]
        tile = code // 4
        block = recv_ref[place_of(tile), pl.ds(2 * S, SLOT - 2 * S), :].astype(F32)
        row = 4 * half_of(tile) + code % 4
        cells.append(jnp.sum(jnp.where(row8 == row, block, 0.0), axis=0, keepdims=True))
    return strips, cells


def edge_kernel(waits, field_ref, out_ref, wide_ref):
    wide_ref[...] = field_ref[...].astype(F32)
    strips = [wide_ref[0], wide_ref[S - 1], wide_ref[:, 0, :], wide_ref[:, S - 1, :]]
    cells = [wide_ref[i, pl.ds(j, 1), :] for i in (0, S - 1) for j in (0, S - 1)]
    put_edges(out_ref, strips, cells)


def slot_kernel(waits, pos_ref, seam_ref, own_ref, other_ref, out_ref):
    pos = pos_ref[0]
    half = half_of(pos)
    mine = own_ref[pl.ds(4 * S, 8), :].astype(F32)
    other = other_ref[pl.ds(4 * S, 8), :].astype(F32)
    row8 = lax.broadcasted_iota(jnp.int32, (8, C), 0)
    first = jnp.where(half == 0, mine, other)
    second = jnp.where(half == 0, other, mine)
    cells8 = jnp.where(row8 < 4, first, pltpu.roll(second, 4, 0)).astype(BF)

    def put(p, carry):
        out_ref[p, pl.ds(2 * S, SLOT - 2 * S), :] = cells8
        return carry

    lax.fori_loop(0, 32, put, 0)
    for source, edges, at_half in ((pos, own_ref, half), (pos ^ 2, other_ref, 1 - half)):
        for e in range(4):
            tile = seam_ref[e, source] // 8

            @pl.when(half_of(tile) == half)
            def _(tile=tile, edges=edges, at_half=at_half, e=e):
                rows = pl.ds(pl.multiple_of(S * at_half, S), S)
                out_ref[place_of(tile), rows, :] = edges[pl.ds(S * e, S), :]


def mlp_rows(normed, cot, out, gain_parts, w_in_ref, b_in_ref, w_out_ref, keep):
    gain, xhat, istd = gain_parts
    dnorm = jnp.zeros(out.shape, F32)
    sums = []
    for n in range(4):
        h = slice(256 * n, 256 * n + 256)
        z = jnp.dot(normed, w_in_ref[:, h], preferred_element_type=F32) + b_in_ref[:, h]
        dact = lax.dot_general(
            cot, w_out_ref[h, :], (((1,), (1,)), ((), ())), preferred_element_type=F32
        )
        z2 = z * z
        half = 0.5 + 0.5 * jnp.tanh(z * (GELU_C + (GELU_C * 0.044715) * z2))
        act = z * half
        slope = half + act * (1.0 - half) * (2 * GELU_C + (6 * GELU_C * 0.044715) * z2)
        act = act.astype(BF)
        dhid = (dact * slope).astype(BF)
        keep(n, act, dhid)
        sums.append(jnp.sum(dhid.astype(F32), axis=0, keepdims=True))
        out = out + jnp.dot(act, w_out_ref[h, :], preferred_element_type=F32)
        dnorm = dnorm + lax.dot_general(
            dhid, w_in_ref[:, h], (((1,), (1,)), ((), ())), preferred_element_type=F32
        )
    dunit = dnorm * gain
    dconv = istd * (
        dunit
        - jnp.mean(dunit, axis=1, keepdims=True)
        - xhat * jnp.mean(dunit * xhat, axis=1, keepdims=True)
    )
    sums.append(jnp.sum(dnorm * xhat, axis=0, keepdims=True))
    sums.append(jnp.sum(dnorm, axis=0, keepdims=True))
    return out.astype(BF), dconv.astype(BF).astype(F32), sums


def norm_rows(rows):
    centred = rows - jnp.mean(rows, axis=1, keepdims=True)
    istd = 1.0 / jnp.sqrt(jnp.mean(centred * centred, axis=1, keepdims=True) + 1e-06)
    return centred * istd, istd


OVER_ROWS = (((0,), (0,)), ((), ()))


def inside_kernel(
    waits,
    field_ref,
    cot_ref,
    kern_ref,
    bias_ref,
    gain_ref,
    shift_ref,
    b_out_ref,
    w_in_ref,
    b_in_ref,
    w_out_ref,
    blocks_ref,
    base_ref,
    grad_ref,
    pad_ref,
    xhat_ref,
    istd_ref,
    normed_ref,
    active_ref,
    dhid_ref,
    keep_ref,
    dconv_ref,
):
    center = field_ref[...].astype(F32)
    pad_ref[:, 0] = jnp.zeros((3, S, C), F32)
    pad_ref[:, S + 1] = jnp.zeros((3, S, C), F32)
    pad_ref[1, pl.ds(1, S)] = center
    pad_ref[0, pl.ds(1, S)] = pltpu.roll(center, 1, 1)
    pad_ref[2, pl.ds(1, S)] = pltpu.roll(center, S - 1, 1)

    bias = bias_ref[...]
    gain = gain_ref[...]
    shift = shift_ref[...]
    b_out = b_out_ref[...]
    rowid = lax.broadcasted_iota(jnp.int32, (256, C), 0)
    col = rowid & (S - 1)

    def forward_rows(b, carry):
        r0 = b * 8
        acc = jnp.zeros((8, S, C), F32) + bias.reshape(1, 1, C)
        for u in range(3):
            for v in range(3):
                k = 3 * u + v
                acc = acc + pad_ref[v, pl.ds(r0 + u, 8)] * kern_ref[k : k + 1, :].reshape(1, 1, C)
        xhat, istd = norm_rows(acc.reshape(8 * S, C))
        q = pl.ds(pl.multiple_of(b * 256, 256), 256)
        xhat_ref[q, :] = xhat
        istd_ref[q, :] = jnp.broadcast_to(istd, (256, 128))
        normed_ref[q, :] = (xhat * gain + shift).astype(BF)
        row = r0 + (rowid >> 5)
        kept = (col > 0) & (col < S - 1) & (row > 0) & (row < S - 1)
        keep_ref[q, :] = jnp.where(kept, cot_ref[q, :].astype(F32), 0.0).astype(BF)
        return carry

    lax.fori_loop(0, 4, forward_rows, 0)
    waits[7]()
    waits[9]()

    def block_rows(b, carry):
        q = pl.ds(pl.multiple_of(b * 256, 256), 256)

        def keep(n, act, dhid):
            active_ref[q, 256 * n : 256 * n + 256] = act
            dhid_ref[q, 256 * n : 256 * n + 256] = dhid

        out = field_ref[pl.ds(b * 8, 8)].reshape(256, C).astype(F32) + b_out
        parts = (gain, xhat_ref[q, :], istd_ref[q, 0:1])
        out, dconv, sums = mlp_rows(
            normed_ref[q, :], keep_ref[q, :], out, parts, w_in_ref, b_in_ref, w_out_ref, keep
        )
        blocks_ref[q, :] = out
        dconv_ref[pl.ds(b * 8, 8)] = dconv.reshape(8, S, C)
        sums.append(jnp.sum(cot_ref[q, :].astype(F32), axis=0, keepdims=True))
        return tuple(a + x for a, x in zip(carry, sums))

    zero = jnp.zeros((1, C), F32)
    *g_bin, g_gain, g_shift, g_bout = lax.fori_loop(0, 4, block_rows, (zero,) * 7)

    for n in range(4):
        h = slice(256 * n, 256 * n + 256)
        dot = functools.partial(lax.dot_general, dimension_numbers=OVER_ROWS, preferred_element_type=F32)
        g = dot(normed_ref[...], dhid_ref[:, h])
        grad_ref[4 * n : 4 * n + 4, pl.ds(0, 64), :] = g.reshape(4, 64, C)
        g = dot(active_ref[:, h], keep_ref[...])
        grad_ref[16 + 4 * n : 20 + 4 * n, pl.ds(0, 64), :] = g.reshape(4, 64, C)

    g_kernel = []
    for u in range(3):
        for v in range(3):

            def tap_rows(b, acc, u=u, v=v):
                part = pad_ref[v, pl.ds(b * 4 + u, 4)] * dconv_ref[pl.ds(b * 4, 4)]
                return acc + jnp.sum(part.reshape(4 * S // 8, 8, C), axis=0)

            acc = lax.fori_loop(0, 8, tap_rows, jnp.zeros((8, C), F32))
            g_kernel.append(jnp.sum(acc, axis=0, keepdims=True))

    def bias_rows(b, acc):
        return acc + jnp.sum(dconv_ref[pl.ds(b * 4, 4)].reshape(4 * S // 8, 8, C), axis=0)

    g_bias = jnp.sum(lax.fori_loop(0, 8, bias_rows, jnp.zeros((8, C), F32)), axis=0, keepdims=True)

    small = g_kernel + [g_bias, g_gain, g_shift, g_bout] + g_bin + [zero] * 15
    row8 = lax.broadcasted_iota(jnp.int32, (CHUNK - 64, C), 0)
    for j in range(32):
        grad_ref[j, pl.ds(64, CHUNK - 64), :] = jnp.where(row8 == 0, small[j], 0.0)

    def shift_rows(i, carry):
        row = dconv_ref[i]
        pad_ref[1, i + 1] = row
        pad_ref[0, i + 1] = pltpu.roll(row, S - 1, 0)
        pad_ref[2, i + 1] = pltpu.roll(row, 1, 0)
        return carry

    lax.fori_loop(0, S, shift_rows, 0)
    taps = [kern_ref[k : k + 1, :].reshape(1, 1, C) for k in range(9)]

    def inner_rows(b, carry):
        q = pl.ds(pl.multiple_of(b * 4 * S, 4 * S), 4 * S)
        acc = cot_ref[q, :].astype(F32).reshape(4, S, C)
        for u in range(3):
            for v in range(3):
                acc = acc + pad_ref[v, pl.ds(b * 4 + 2 - u, 4)] * taps[3 * u + v]
        base_ref[pl.ds(b * 4, 4)] = acc
        return carry

    lax.fori_loop(0, 8, inner_rows, 0)


def border_kernel(
    waits,
    pos_ref,
    seam_ref,
    corner_ref,
    field_ref,
    cot_ref,
    recv_ref,
    kern_ref,
    bias_ref,
    gain_ref,
    shift_ref,
    b_out_ref,
    w_in_ref,
    b_in_ref,
    w_out_ref,
    grad_ref,
    rows_ref,
    lines_ref,
    rim_ref,
    own_ref,
    send_ref,
    wide_ref,
):
    pos = pos_ref[0]
    core = pos % 2
    strips, cells = take_slots(recv_ref, pos, seam_ref, corner_ref)
    top, bottom, left, right = strips
    last = S - 1
    wide_ref[...] = field_ref[...].astype(F32)
    at_row = lambda i: wide_ref[i]
    at_col = lambda j: wide_ref[:, j, :]
    spot = lambda line, i: line[i : i + 1]
    place = lax.broadcasted_iota(jnp.int32, (S, C), 0)
    flat = lambda k: kern_ref[k : k + 1, :]

    bands = [
        (
            (top, at_row(0), at_row(1)),
            ((cells[0], cells[1]), (spot(left, 0), spot(right, 0)), (spot(left, 1), spot(right, 1))),
            lambda a, s: 3 * a + s,
        ),
        (
            (bottom, at_row(last), at_row(last - 1)),
            (
                (cells[2], cells[3]),
                (spot(left, last), spot(right, last)),
                (spot(left, last - 1), spot(right, last - 1)),
            ),
            lambda a, s: 3 * (2 - a) + s,
        ),
        (
            (left, at_col(0), at_col(1)),
            ((cells[0], cells[2]), (spot(top, 0), spot(bottom, 0)), (spot(top, 1), spot(bottom, 1))),
            lambda a, s: 3 * s + a,
        ),
        (
            (right, at_col(last), at_col(last - 1)),
            (
                (cells[1], cells[3]),
                (spot(top, last), spot(bottom, last)),
                (spot(top, last - 1), spot(bottom, last - 1)),
            ),
            lambda a, s: 3 * s + 2 - a,
        ),
    ]
    windows = [[None] * 9 for _ in range(4)]
    rows = []
    for n, (lines, ends, tap) in enumerate(bands):
        acc = jnp.zeros((S, C), F32) + bias_ref[...]
        for a in range(3):
            before = jnp.where(place == 0, ends[a][0], pltpu.roll(lines[a], 1, 0))
            after = jnp.where(place == last, ends[a][1], pltpu.roll(lines[a], last, 0))
            for s, window in enumerate((before, lines[a], after)):
                k = tap(a, s)
                windows[n][k] = window
                acc = acc + window * flat(k)
        rows.append(acc)
    field_rows = jnp.concatenate([lines[1] for lines, _, _ in bands], axis=0)
    wide_ref[...] = cot_ref[...].astype(F32)
    once = (place > 0) & (place < last)
    cot_rows = jnp.concatenate(
        [at_row(0), at_row(last)]
        + [jnp.where(once, at_col(0), 0.0), jnp.where(once, at_col(last), 0.0)],
        axis=0,
    ).astype(BF)

    gain = gain_ref[...]
    waits[11]()
    waits[13]()
    xhat, istd = norm_rows(jnp.concatenate(rows, axis=0))
    normed = (xhat * gain + shift_ref[...]).astype(BF)
    kept = []
    out, dconv, sums = mlp_rows(
        normed,
        cot_rows,
        field_rows + b_out_ref[...],
        (gain, xhat, istd),
        w_in_ref,
        b_in_ref,
        w_out_ref,
        lambda n, act, dhid: kept.append((act, dhid)),
    )
    rows_ref[...] = out
    *g_bin, g_gain, g_shift = sums
    d_lines = [dconv[S * n : S * n + S] for n in range(4)]

    def spread(line, taps):
        back = jnp.where(place == last, 0.0, pltpu.roll(line, last, 0))
        ahead = jnp.where(place == 0, 0.0, pltpu.roll(line, 1, 0))
        return back * flat(taps[0]) + line * flat(taps[1]) + ahead * flat(taps[2])

    def whole(line, at):
        line = jnp.where(place == 0, spot(d_lines[0], at), line)
        return jnp.where(place == last, spot(d_lines[1], at), line)

    row_taps = lambda u: (3 * u, 3 * u + 1, 3 * u + 2)
    col_taps = lambda v: (v, 3 + v, 6 + v)
    rim = [
        spread(d_lines[0], row_taps(0)),
        spread(d_lines[1], row_taps(2)),
        spread(whole(d_lines[2], 0), col_taps(0)),
        spread(whole(d_lines[3], last), col_taps(2)),
    ]
    corners = [
        spot(d_lines[0], 0) * flat(0),
        spot(d_lines[0], last) * flat(2),
        spot(d_lines[1], 0) * flat(6),
        spot(d_lines[1], last) * flat(8),
    ]
    put_edges(rim_ref, rim, corners)
    lines_ref[0] = spread(d_lines[0], row_taps(1))
    lines_ref[1] = spread(d_lines[0], row_taps(2))
    lines_ref[2] = spread(d_lines[1], row_taps(0))
    lines_ref[3] = spread(d_lines[1], row_taps(1))
    lines_ref[4] = spread(d_lines[2], col_taps(1))
    lines_ref[5] = spread(d_lines[2], col_taps(2))
    lines_ref[6] = spread(d_lines[3], col_taps(0))
    lines_ref[7] = spread(d_lines[3], col_taps(1))

    waits[14]()

    def put_rows(first, value):
        mine = core == first // 16
        base = first % 16
        value = value.reshape(4, 64, C) + grad_ref[first : first + 4, pl.ds(0, 64), :]

        @pl.when(mine)
        def _():
            own_ref[pl.ds(base, 4), pl.ds(0, 64), :] = value.astype(BF)

        @pl.when(jnp.logical_not(mine))
        def _():
            send_ref[pl.ds(base, 4), pl.ds(0, 64), :] = value.astype(BF)

    for n in range(4):
        act, dhid = kept[n]
        put_rows(4 * n, lax.dot_general(normed, dhid, OVER_ROWS, preferred_element_type=F32))
        put_rows(16 + 4 * n, lax.dot_general(act, cot_rows, OVER_ROWS, preferred_element_type=F32))

    g_kernel = []
    for k in range(9):
        acc = sum(windows[n][k] * d_lines[n] for n in range(4))
        g_kernel.append(jnp.sum(acc, axis=0, keepdims=True))
    zero = jnp.zeros((1, C), F32)
    g_bias = jnp.sum(dconv, axis=0, keepdims=True)
    small = g_kernel + [g_bias, g_gain, g_shift, zero] + g_bin + [zero] * 15
    row8 = lax.broadcasted_iota(jnp.int32, (CHUNK - 64, C), 0)
    for j in range(32):
        row = jnp.where(row8 == 0, small[j], 0.0) + grad_ref[j, pl.ds(64, CHUNK - 64), :]

        @pl.when(core == j // 16)
        def _(row=row, j=j):
            own_ref[j % 16, pl.ds(64, CHUNK - 64), :] = row.astype(BF)

        @pl.when(core != j // 16)
        def _(row=row, j=j):
            send_ref[j % 16, pl.ds(64, CHUNK - 64), :] = row.astype(BF)


def patch_kernel(waits, part_ref, rows_ref, blocks_ref, wide_ref):
    last = S - 1
    wide_ref[...] = part_ref[...].astype(F32)
    rows = rows_ref[...].astype(F32)
    wide_ref[:, 0, :] = rows[2 * S : 3 * S]
    wide_ref[:, last, :] = rows[3 * S : 4 * S]
    wide_ref[0] = rows[0:S]
    wide_ref[last] = rows[S : 2 * S]
    blocks_ref[...] = wide_ref[...].astype(BF)


def join_kernel(
    waits, pos_ref, seam_ref, corner_ref, base_ref, lines_ref, recv_ref, out_ref, acc_ref
):
    strips, cells = take_slots(recv_ref, pos_ref[0], seam_ref, corner_ref)
    last = S - 1
    acc_ref[...] = base_ref[...]
    for i, add in (
        (0, strips[0] + lines_ref[0]),
        (1, lines_ref[1]),
        (last - 1, lines_ref[2]),
        (last, strips[1] + lines_ref[3]),
    ):
        acc_ref[i] = acc_ref[i] + add
    for j, add in (
        (0, strips[2] + lines_ref[4]),
        (1, lines_ref[5]),
        (last - 1, lines_ref[6]),
        (last, strips[3] + lines_ref[7]),
    ):
        acc_ref[:, j, :] = acc_ref[:, j, :] + add
    for n, (i, j) in enumerate(((0, 0), (0, last), (last, 0), (last, last))):
        acc_ref[i, pl.ds(j, 1), :] = acc_ref[i, pl.ds(j, 1), :] + cells[n]
    out_ref[...] = acc_ref[...].astype(BF)


def scale_kernel(
    waits, at_ref, own_ref, other_ref, kern_ref, chan_ref, w_in_ref, b_in_ref, w_out_ref, entries
):
    core = at_ref[0] % 2
    halves = (own_ref, other_ref)
    sums = []
    for half in range(2):
        def one_half(j, acc, half=half):
            v = jnp.where(core == half, own_ref[j].astype(F32), other_ref[j].astype(F32))
            return acc + jnp.sum((v * v).reshape(CHUNK // 8, 8, C), axis=0)

        sums.append(lax.fori_loop(0, 16, one_half, jnp.zeros((8, C), F32)))
    total = jnp.sum(jnp.sum(sums[0] + sums[1], axis=0, keepdims=True), axis=1, keepdims=True)
    scale = 1.0 / jnp.sqrt(total / entries + 1e-06)

    for j in range(32):
        c, k = j // 16, j % 16

        def emit(ref, j=j, k=k):
            rows = ref[k, pl.ds(0, 64), :].astype(F32) * scale
            if j < 16:
                w_in_ref[64 * (j % 4) : 64 * (j % 4) + 64, 256 * (j // 4) : 256 * (j // 4) + 256] = rows
            else:
                w_out_ref[64 * (j - 16) : 64 * (j - 16) + 64, :] = rows
            row = ref[k, pl.ds(64, 8), :].astype(F32)[0:1] * scale
            if j < 9:
                kern_ref[j : j + 1, :] = row
            elif j < 13:
                chan_ref[j - 9 : j - 8, :] = row
            elif j < 17:
                b_in_ref[:, 256 * (j - 13) : 256 * (j - 13) + 256] = row

        for near in range(2):

            @pl.when((core == c) == (near == 1))
            def _(emit=emit, near=near):
                emit(halves[1 - near])


def at(y, x, h, c):
    return ((y * 4 + x) * 2 + h) * 2 + c


def moves(axis, d):
    pairs = []
    for y in range(4):
        for x in range(4):
            for h in range(2):
                for c in range(2):
                    to = {
                        "y": ((y + d) % 4, x, h, c),
                        "x": (y, (x + d) % 4, h, c),
                        "h": (y, x, 1 - h, c),
                        "c": (y, x, h, 1 - c),
                    }[axis]
                    pairs.append((at(y, x, h, c), at(*to)))
    return pairs


def exchange(slots):
    halves = [[at(p // 8, p // 2 % 4, h, p % 2) for p in range(32)] for h in range(2)]
    return lax.all_to_all(slots, "space", 0, 0, axis_index_groups=halves, tiled=True)


def plane(slots):
    planes = [
        [at(p % 4, p // 4, h, c) for p in range(16)] for h in range(2) for c in range(2)
    ]
    return lax.all_to_all(slots, "space", 0, 0, axis_index_groups=planes, tiled=True)


def sum_over_devices(own, send, slots):
    rest = own.astype(F32) + lax.ppermute(send, "space", moves("c", 1)).astype(F32)
    parts = plane(rest.astype(BF))
    piece = jnp.sum(parts.astype(F32), axis=0)
    piece, slots = lax.optimization_barrier((piece, slots))
    back = exchange(slots)
    mine = piece.astype(BF)
    other = lax.ppermute(mine, "space", moves("h", 1))
    piece = mine.astype(F32) + other.astype(F32)
    turn = lambda d: [(i, (i + d) % 4) for i in range(4)]
    mine = piece.astype(BF)
    got = [mine] + [lax.ppermute(mine, "batch", turn(d)) for d in (1, 2, 3)]
    got = [g.astype(F32) for g in got]
    piece = (got[0] + got[2]) + (got[1] + got[3])
    piece, back = lax.optimization_barrier((piece.astype(BF), back))
    full = plane(jnp.broadcast_to(piece[None], (16, CHUNK, C)))
    return full, lax.ppermute(full, "space", moves("c", 1)), back


def shards(
    fields,
    cotangent,
    dw_kernel,
    dw_bias,
    ln_gain,
    ln_shift,
    w_in,
    b_in,
    w_out,
    b_out,
    seam_links,
    corner_links,
):
    here = lax.axis_index("space").reshape(1)
    links, diagonals = seam_links.T, corner_links.T
    field = fields[0, 0]
    cot = cotangent[0, 0]
    sds = jax.ShapeDtypeStruct
    edges = sds((EDGE, C), BF)
    wide = pltpu.VMEM((S, S, C), F32)

    def to_slots(mine):
        other = lax.ppermute(mine, "space", moves("h", 1))
        return staged_call(
            slot_kernel,
            [(here, "smem", 0), (links, "smem", 0), (mine, "vmem", 0), (other, "vmem", 0)],
            [(sds((32, SLOT, C), BF), True)],
            [],
            63,
        )[0]

    (field_edges,) = staged_call(edge_kernel, [(field, "vmem", 0)], [(edges, True)], [wide], 63)
    halo = exchange(to_slots(field_edges))

    cells = S * S
    row = lambda v: (v.reshape(1, -1), "vmem", 0)
    weights = [
        (dw_kernel, "vmem", 0),
        row(dw_bias),
        row(ln_gain),
        row(ln_shift),
        row(b_out),
        (w_in, "vmem", 1),
        row(b_in),
        (w_out, "vmem", 1),
    ]
    part, base, grads = staged_call(
        inside_kernel,
        [(field, "vmem", 0), (cot.reshape(cells, C), "vmem", 0)] + weights,
        [
            (sds((cells, C), BF), True),
            (sds((S, S, C), F32), True),
            (sds((32, CHUNK, C), F32), True),
        ],
        [
            pltpu.VMEM((3, S + 2, S, C), F32),
            pltpu.VMEM((cells, C), F32),
            pltpu.VMEM((cells, 128), F32),
            pltpu.VMEM((cells, C), BF),
            pltpu.VMEM((cells, H), BF),
            pltpu.VMEM((cells, H), BF),
            pltpu.VMEM((cells, C), BF),
            wide,
        ],
        63,
        pl.CostEstimate(
            flops=12 * cells * C * H, bytes_accessed=8 << 20, transcendentals=cells * H
        ),
    )
    where = [(here, "smem", 0), (links, "smem", 0), (diagonals, "smem", 0)]
    border_rows, lines, rim, own, send = staged_call(
        border_kernel,
        where
        + [(field, "vmem", 0), (cot, "vmem", 0), (halo, "vmem", 0)]
        + weights
        + [(grads, "vmem", 1)],
        [
            (sds((4 * S, C), BF), True),
            (sds((8, S, C), F32), True),
            (edges, True),
            (sds((16, CHUNK, C), BF), True),
            (sds((16, CHUNK, C), BF), True),
        ],
        [wide],
        63,
    )
    (blocks,) = staged_call(
        patch_kernel,
        [(part.reshape(S, S, C), "vmem", 0), (border_rows, "vmem", 0)],
        [(sds((S, S, C), BF), True)],
        [wide],
        63,
    )
    near, far, back = sum_over_devices(own, send, to_slots(rim))
    (grad_tile,) = staged_call(
        join_kernel,
        where + [(base, "vmem", 0), (lines, "vmem", 0), (back, "here", 0)],
        [(sds((S, S, C), BF), True)],
        [wide],
        10,
    )
    entries = 13 * C + 2 * C * H + H
    grad_kernel, grad_channels, grad_w_in, grad_b_in, grad_w_out = staged_call(
        functools.partial(scale_kernel, entries=entries),
        [(here, "smem", 0), (near, "here", 0), (far, "here", 0)],
        [
            (sds((9, C), F32), True),
            (sds((4, C), F32), True),
            (sds((C, H), F32), True),
            (sds((1, H), F32), True),
            (sds((H, C), F32), True),
        ],
        [],
        10,
    )
    return (
        blocks[None, None],
        grad_tile[None, None],
        grad_kernel,
        grad_channels,
        grad_w_in,
        grad_b_in.reshape(H),
        grad_w_out,
    )


def solution(mesh):
    tile = P("batch", "space", None, None, None)

    return jax.shard_map(
        shards,
        mesh=mesh,
        in_specs=(tile, tile) + (P(),) * 10,
        out_specs=(tile, tile) + (P(),) * 5,
        check_vma=False,
    )
```

```python
import functools

import jax
import jax.numpy as jnp
from jax import lax
from jax.experimental import pallas as pl
from jax.experimental.pallas import tpu as pltpu
from jax.sharding import PartitionSpec as P


S = 32
C = 256
H = 1024
SLOT = 72
EDGE = 136
CHUNK = 72
BF = jnp.bfloat16
F32 = jnp.float32
GELU_C = 0.7978845608028654
VMEM = functools.partial(pl.BlockSpec, memory_space=pltpu.VMEM)


def staged_call(kernel, ins, outs, scratch, mib, cost=None):
    n_in, n_out = len(ins), len(outs)
    space = {"vmem": pltpu.VMEM, "smem": pltpu.SMEM}
    in_bufs = [space[w](a.shape, a.dtype) for a, w, _ in ins if w != "here"]
    out_bufs = [pltpu.VMEM(o.shape, o.dtype) for o, to_hbm in outs if to_hbm]
    hbm = pl.BlockSpec(memory_space=pltpu.HBM)

    def body(*refs):
        given, results = refs[:n_in], refs[n_in : n_in + n_out]
        rest = list(refs[n_in + n_out :])
        sems = rest.pop(0)
        stages = [rest.pop(0) for _ in in_bufs]
        drains = [rest.pop(0) for _ in out_bufs]
        args, waits, soon, n = [], {}, [], 0
        for i, (ref, (_, where, late)) in enumerate(zip(given, ins)):
            if where == "here":
                args.append(ref)
                continue
            copy = pltpu.make_async_copy(ref, stages[n], sems.at[n])
            copy.start()
            args.append(stages[n])
            n += 1
            if late:
                waits[i] = copy.wait
            else:
                soon.append(copy)
        for copy in soon:
            copy.wait()
        writes = []
        for ref, (_, to_hbm) in zip(results, outs):
            if to_hbm:
                drain = drains.pop(0)
                writes.append(pltpu.make_async_copy(drain, ref, sems.at[n]))
                args.append(drain)
                n += 1
            else:
                args.append(ref)
        started = []

        def flush(i):
            writes[i].start()
            started.append(i)

        waits["flush"] = flush
        kernel(waits, *args, *rest)
        for i, copy in enumerate(writes):
            if i not in started:
                copy.start()
        for copy in writes:
            copy.wait()

    return pl.pallas_call(
        body,
        out_shape=tuple(o for o, _ in outs),
        in_specs=[VMEM() if w == "here" else hbm for _, w, _ in ins],
        out_specs=tuple(hbm if to_hbm else VMEM() for _, to_hbm in outs),
        scratch_shapes=[pltpu.SemaphoreType.DMA((len(in_bufs) + len(out_bufs) + 1,))]
        + in_bufs
        + out_bufs
        + scratch,
        compiler_params=pltpu.CompilerParams(vmem_limit_bytes=mib * 1024 * 1024),
        cost_estimate=cost,
    )(*(a for a, _, _ in ins))


def put_edges(out_ref, strips, cells):
    for e in range(4):
        out_ref[pl.ds(S * e, S), :] = strips[e].astype(BF)
    cells8 = jnp.concatenate([c.reshape(1, C) for c in cells] + [jnp.zeros((4, C), F32)], axis=0)
    out_ref[pl.ds(4 * S, 8), :] = cells8.astype(BF)


def half_of(tile):
    return (tile // 2) % 2


def place_of(tile):
    return (tile // 4) * 2 + tile % 2


def take_slots(recv_ref, pos, seam_ref, corner_ref):
    rows = lax.broadcasted_iota(jnp.int32, (S, S), 0)
    cols = lax.broadcasted_iota(jnp.int32, (S, S), 1)
    strips = []
    for e in range(4):
        code = seam_ref[e, pos]
        tile = code // 8
        target = jnp.where(code % 2 == 1, S - 1 - rows, rows)
        turn = (cols == target).astype(F32).astype(BF)
        strip = recv_ref[place_of(tile), pl.ds(pl.multiple_of(S * half_of(tile), S), S), :]
        strips.append(jnp.dot(turn, strip, preferred_element_type=F32))
    cells = []
    row8 = lax.broadcasted_iota(jnp.int32, (SLOT - 2 * S, C), 0)
    for k in range(4):
        code = corner_ref[k, pos]
        tile = code // 4
        block = recv_ref[place_of(tile), pl.ds(2 * S, SLOT - 2 * S), :].astype(F32)
        row = 4 * half_of(tile) + code % 4
        cells.append(jnp.sum(jnp.where(row8 == row, block, 0.0), axis=0, keepdims=True))
    return strips, cells


def edge_kernel(waits, field_ref, out_ref, wide_ref):
    wide_ref[...] = field_ref[...].astype(F32)
    strips = [wide_ref[0], wide_ref[S - 1], wide_ref[:, 0, :], wide_ref[:, S - 1, :]]
    cells = [wide_ref[i, pl.ds(j, 1), :] for i in (0, S - 1) for j in (0, S - 1)]
    put_edges(out_ref, strips, cells)


def slot_kernel(waits, pos_ref, seam_ref, own_ref, other_ref, out_ref):
    pos = pos_ref[0]
    half = half_of(pos)
    mine = own_ref[pl.ds(4 * S, 8), :].astype(F32)
    other = other_ref[pl.ds(4 * S, 8), :].astype(F32)
    row8 = lax.broadcasted_iota(jnp.int32, (8, C), 0)
    first = jnp.where(half == 0, mine, other)
    second = jnp.where(half == 0, other, mine)
    cells8 = jnp.where(row8 < 4, first, pltpu.roll(second, 4, 0)).astype(BF)

    def put(p, carry):
        out_ref[p, pl.ds(2 * S, SLOT - 2 * S), :] = cells8
        return carry

    lax.fori_loop(0, 32, put, 0)
    for source, edges, at_half in ((pos, own_ref, half), (pos ^ 2, other_ref, 1 - half)):
        for e in range(4):
            tile = seam_ref[e, source] // 8

            @pl.when(half_of(tile) == half)
            def _(tile=tile, edges=edges, at_half=at_half, e=e):
                rows = pl.ds(pl.multiple_of(S * at_half, S), S)
                out_ref[place_of(tile), rows, :] = edges[pl.ds(S * e, S), :]


def mlp_rows(normed, cot, out, gain_parts, w_in_ref, b_in_ref, w_out_ref, keep):
    gain, xhat, istd = gain_parts
    dnorm = jnp.zeros(out.shape, F32)
    sums = []
    for n in range(4):
        h = slice(256 * n, 256 * n + 256)
        z = jnp.dot(normed, w_in_ref[:, h], preferred_element_type=F32) + b_in_ref[:, h]
        dact = lax.dot_general(
            cot, w_out_ref[h, :], (((1,), (1,)), ((), ())), preferred_element_type=F32
        )
        z2 = z * z
        half = 0.5 + 0.5 * jnp.tanh(z * (GELU_C + (GELU_C * 0.044715) * z2))
        act = z * half
        slope = half + act * (1.0 - half) * (2 * GELU_C + (6 * GELU_C * 0.044715) * z2)
        act = act.astype(BF)
        dhid = (dact * slope).astype(BF)
        keep(n, act, dhid)
        sums.append(jnp.sum(dhid.astype(F32), axis=0, keepdims=True))
        out = out + jnp.dot(act, w_out_ref[h, :], preferred_element_type=F32)
        dnorm = dnorm + lax.dot_general(
            dhid, w_in_ref[:, h], (((1,), (1,)), ((), ())), preferred_element_type=F32
        )
    dunit = dnorm * gain
    dconv = istd * (
        dunit
        - jnp.mean(dunit, axis=1, keepdims=True)
        - xhat * jnp.mean(dunit * xhat, axis=1, keepdims=True)
    )
    sums.append(jnp.sum(dnorm * xhat, axis=0, keepdims=True))
    sums.append(jnp.sum(dnorm, axis=0, keepdims=True))
    return out.astype(BF), dconv.astype(BF).astype(F32), sums


def norm_rows(rows):
    centred = rows - jnp.mean(rows, axis=1, keepdims=True)
    istd = 1.0 / jnp.sqrt(jnp.mean(centred * centred, axis=1, keepdims=True) + 1e-06)
    return centred * istd, istd


OVER_ROWS = (((0,), (0,)), ((), ()))


def inside_kernel(
    waits,
    field_ref,
    cot_ref,
    kern_ref,
    bias_ref,
    gain_ref,
    shift_ref,
    b_out_ref,
    w_in_ref,
    b_in_ref,
    w_out_ref,
    blocks_ref,
    base_ref,
    grad_ref,
    pad_ref,
    xhat_ref,
    istd_ref,
    normed_ref,
    active_ref,
    dhid_ref,
    keep_ref,
    dconv_ref,
):
    center = field_ref[...].astype(F32)
    pad_ref[:, 0] = jnp.zeros((3, S, C), F32)
    pad_ref[:, S + 1] = jnp.zeros((3, S, C), F32)
    pad_ref[1, pl.ds(1, S)] = center
    pad_ref[0, pl.ds(1, S)] = pltpu.roll(center, 1, 1)
    pad_ref[2, pl.ds(1, S)] = pltpu.roll(center, S - 1, 1)

    bias = bias_ref[...]
    gain = gain_ref[...]
    shift = shift_ref[...]
    b_out = b_out_ref[...]
    rowid = lax.broadcasted_iota(jnp.int32, (256, C), 0)
    col = rowid & (S - 1)

    def forward_rows(b, carry):
        r0 = b * 8
        acc = jnp.zeros((8, S, C), F32) + bias.reshape(1, 1, C)
        for u in range(3):
            for v in range(3):
                k = 3 * u + v
                acc = acc + pad_ref[v, pl.ds(r0 + u, 8)] * kern_ref[k : k + 1, :].reshape(1, 1, C)
        xhat, istd = norm_rows(acc.reshape(8 * S, C))
        q = pl.ds(pl.multiple_of(b * 256, 256), 256)
        xhat_ref[q, :] = xhat
        istd_ref[q, :] = jnp.broadcast_to(istd, (256, 128))
        normed_ref[q, :] = (xhat * gain + shift).astype(BF)
        row = r0 + (rowid >> 5)
        kept = (col > 0) & (col < S - 1) & (row > 0) & (row < S - 1)
        keep_ref[q, :] = jnp.where(kept, cot_ref[q, :].astype(F32), 0.0).astype(BF)
        return carry

    lax.fori_loop(0, 4, forward_rows, 0)
    waits[7]()
    waits[9]()

    def block_rows(b, carry):
        q = pl.ds(pl.multiple_of(b * 256, 256), 256)

        def keep(n, act, dhid):
            active_ref[q, 256 * n : 256 * n + 256] = act
            dhid_ref[q, 256 * n : 256 * n + 256] = dhid

        out = field_ref[pl.ds(b * 8, 8)].reshape(256, C).astype(F32) + b_out
        parts = (gain, xhat_ref[q, :], istd_ref[q, 0:1])
        out, dconv, sums = mlp_rows(
            normed_ref[q, :], keep_ref[q, :], out, parts, w_in_ref, b_in_ref, w_out_ref, keep
        )
        blocks_ref[q, :] = out
        dconv_ref[pl.ds(b * 8, 8)] = dconv.reshape(8, S, C)
        sums.append(jnp.sum(cot_ref[q, :].astype(F32), axis=0, keepdims=True))
        return tuple(a + x for a, x in zip(carry, sums))

    zero = jnp.zeros((1, C), F32)
    *g_bin, g_gain, g_shift, g_bout = lax.fori_loop(0, 4, block_rows, (zero,) * 7)

    for n in range(4):
        h = slice(256 * n, 256 * n + 256)
        dot = functools.partial(lax.dot_general, dimension_numbers=OVER_ROWS, preferred_element_type=F32)
        g = dot(normed_ref[...], dhid_ref[:, h])
        grad_ref[4 * n : 4 * n + 4, pl.ds(0, 64), :] = g.reshape(4, 64, C)
        g = dot(active_ref[:, h], keep_ref[...])
        grad_ref[16 + 4 * n : 20 + 4 * n, pl.ds(0, 64), :] = g.reshape(4, 64, C)

    g_kernel = []
    for u in range(3):
        for v in range(3):

            def tap_rows(b, acc, u=u, v=v):
                part = pad_ref[v, pl.ds(b * 4 + u, 4)] * dconv_ref[pl.ds(b * 4, 4)]
                return acc + jnp.sum(part.reshape(4 * S // 8, 8, C), axis=0)

            acc = lax.fori_loop(0, 8, tap_rows, jnp.zeros((8, C), F32))
            g_kernel.append(jnp.sum(acc, axis=0, keepdims=True))

    def bias_rows(b, acc):
        return acc + jnp.sum(dconv_ref[pl.ds(b * 4, 4)].reshape(4 * S // 8, 8, C), axis=0)

    g_bias = jnp.sum(lax.fori_loop(0, 8, bias_rows, jnp.zeros((8, C), F32)), axis=0, keepdims=True)

    small = g_kernel + [g_bias, g_gain, g_shift, g_bout] + g_bin + [zero] * 15
    row8 = lax.broadcasted_iota(jnp.int32, (CHUNK - 64, C), 0)
    for j in range(32):
        grad_ref[j, pl.ds(64, CHUNK - 64), :] = jnp.where(row8 == 0, small[j], 0.0)

    def shift_rows(i, carry):
        row = dconv_ref[i]
        pad_ref[1, i + 1] = row
        pad_ref[0, i + 1] = pltpu.roll(row, S - 1, 0)
        pad_ref[2, i + 1] = pltpu.roll(row, 1, 0)
        return carry

    lax.fori_loop(0, S, shift_rows, 0)
    taps = [kern_ref[k : k + 1, :].reshape(1, 1, C) for k in range(9)]

    def inner_rows(b, carry):
        q = pl.ds(pl.multiple_of(b * 4 * S, 4 * S), 4 * S)
        acc = cot_ref[q, :].astype(F32).reshape(4, S, C)
        for u in range(3):
            for v in range(3):
                acc = acc + pad_ref[v, pl.ds(b * 4 + 2 - u, 4)] * taps[3 * u + v]
        base_ref[pl.ds(b * 4, 4)] = acc
        return carry

    lax.fori_loop(0, 8, inner_rows, 0)


def border_kernel(
    waits,
    pos_ref,
    seam_ref,
    corner_ref,
    field_ref,
    cot_ref,
    recv_ref,
    kern_ref,
    bias_ref,
    gain_ref,
    shift_ref,
    b_out_ref,
    w_in_ref,
    b_in_ref,
    w_out_ref,
    grad_ref,
    rows_ref,
    dconv_ref,
    own_ref,
    send_ref,
    wide_ref,
):
    pos = pos_ref[0]
    core = pos % 2
    strips, cells = take_slots(recv_ref, pos, seam_ref, corner_ref)
    top, bottom, left, right = strips
    last = S - 1
    wide_ref[...] = field_ref[...].astype(F32)
    at_row = lambda i: wide_ref[i]
    at_col = lambda j: wide_ref[:, j, :]
    spot = lambda line, i: line[i : i + 1]
    place = lax.broadcasted_iota(jnp.int32, (S, C), 0)
    flat = lambda k: kern_ref[k : k + 1, :]

    bands = [
        (
            (top, at_row(0), at_row(1)),
            ((cells[0], cells[1]), (spot(left, 0), spot(right, 0)), (spot(left, 1), spot(right, 1))),
            lambda a, s: 3 * a + s,
        ),
        (
            (bottom, at_row(last), at_row(last - 1)),
            (
                (cells[2], cells[3]),
                (spot(left, last), spot(right, last)),
                (spot(left, last - 1), spot(right, last - 1)),
            ),
            lambda a, s: 3 * (2 - a) + s,
        ),
        (
            (left, at_col(0), at_col(1)),
            ((cells[0], cells[2]), (spot(top, 0), spot(bottom, 0)), (spot(top, 1), spot(bottom, 1))),
            lambda a, s: 3 * s + a,
        ),
        (
            (right, at_col(last), at_col(last - 1)),
            (
                (cells[1], cells[3]),
                (spot(top, last), spot(bottom, last)),
                (spot(top, last - 1), spot(bottom, last - 1)),
            ),
            lambda a, s: 3 * s + 2 - a,
        ),
    ]
    windows = [[None] * 9 for _ in range(4)]
    rows = []
    for n, (lines, ends, tap) in enumerate(bands):
        acc = jnp.zeros((S, C), F32) + bias_ref[...]
        for a in range(3):
            before = jnp.where(place == 0, ends[a][0], pltpu.roll(lines[a], 1, 0))
            after = jnp.where(place == last, ends[a][1], pltpu.roll(lines[a], last, 0))
            for s, window in enumerate((before, lines[a], after)):
                k = tap(a, s)
                windows[n][k] = window
                acc = acc + window * flat(k)
        rows.append(acc)
    field_rows = jnp.concatenate([lines[1] for lines, _, _ in bands], axis=0)
    wide_ref[...] = cot_ref[...].astype(F32)
    once = (place > 0) & (place < last)
    cot_rows = jnp.concatenate(
        [at_row(0), at_row(last)]
        + [jnp.where(once, at_col(0), 0.0), jnp.where(once, at_col(last), 0.0)],
        axis=0,
    ).astype(BF)

    gain = gain_ref[...]
    waits[11]()
    waits[13]()
    xhat, istd = norm_rows(jnp.concatenate(rows, axis=0))
    normed = (xhat * gain + shift_ref[...]).astype(BF)
    kept = []
    out, dconv, sums = mlp_rows(
        normed,
        cot_rows,
        field_rows + b_out_ref[...],
        (gain, xhat, istd),
        w_in_ref,
        b_in_ref,
        w_out_ref,
        lambda n, act, dhid: kept.append((act, dhid)),
    )
    rows_ref[...] = out
    *g_bin, g_gain, g_shift = sums
    d_lines = [dconv[S * n : S * n + S] for n in range(4)]

    dconv_ref[...] = dconv

    waits[14]()

    def put_rows(first, value):
        mine = core == first // 16
        base = first % 16
        value = value.reshape(4, 64, C) + grad_ref[first : first + 4, pl.ds(0, 64), :]

        @pl.when(mine)
        def _():
            own_ref[pl.ds(base, 4), pl.ds(0, 64), :] = value

        @pl.when(jnp.logical_not(mine))
        def _():
            send_ref[pl.ds(base, 4), pl.ds(0, 64), :] = value.astype(BF)

    for n in range(4):
        act, dhid = kept[n]
        put_rows(4 * n, lax.dot_general(normed, dhid, OVER_ROWS, preferred_element_type=F32))
        put_rows(16 + 4 * n, lax.dot_general(act, cot_rows, OVER_ROWS, preferred_element_type=F32))

    g_kernel = []
    for k in range(9):
        acc = sum(windows[n][k] * d_lines[n] for n in range(4))
        g_kernel.append(jnp.sum(acc, axis=0, keepdims=True))
    zero = jnp.zeros((1, C), F32)
    g_bias = jnp.sum(dconv, axis=0, keepdims=True)
    small = g_kernel + [g_bias, g_gain, g_shift, zero] + g_bin + [zero] * 15
    row8 = lax.broadcasted_iota(jnp.int32, (CHUNK - 64, C), 0)
    for j in range(32):
        row = jnp.where(row8 == 0, small[j], 0.0) + grad_ref[j, pl.ds(64, CHUNK - 64), :]

        @pl.when(core == j // 16)
        def _(row=row, j=j):
            own_ref[j % 16, pl.ds(64, CHUNK - 64), :] = row

        @pl.when(core != j // 16)
        def _(row=row, j=j):
            send_ref[j % 16, pl.ds(64, CHUNK - 64), :] = row.astype(BF)


def rim_kernel(waits, dconv_ref, kern_ref, lines_ref, rim_ref):
    last = S - 1
    spot = lambda line, i: line[i : i + 1]
    place = lax.broadcasted_iota(jnp.int32, (S, C), 0)
    flat = lambda k: kern_ref[k : k + 1, :]
    d_lines = [dconv_ref[S * n : S * n + S] for n in range(4)]

    def spread(line, taps):
        back = jnp.where(place == last, 0.0, pltpu.roll(line, last, 0))
        ahead = jnp.where(place == 0, 0.0, pltpu.roll(line, 1, 0))
        return back * flat(taps[0]) + line * flat(taps[1]) + ahead * flat(taps[2])

    def whole(line, at):
        line = jnp.where(place == 0, spot(d_lines[0], at), line)
        return jnp.where(place == last, spot(d_lines[1], at), line)

    row_taps = lambda u: (3 * u, 3 * u + 1, 3 * u + 2)
    col_taps = lambda v: (v, 3 + v, 6 + v)
    rim = [
        spread(d_lines[0], row_taps(0)),
        spread(d_lines[1], row_taps(2)),
        spread(whole(d_lines[2], 0), col_taps(0)),
        spread(whole(d_lines[3], last), col_taps(2)),
    ]
    corners = [
        spot(d_lines[0], 0) * flat(0),
        spot(d_lines[0], last) * flat(2),
        spot(d_lines[1], 0) * flat(6),
        spot(d_lines[1], last) * flat(8),
    ]
    put_edges(rim_ref, rim, corners)
    lines_ref[0] = spread(d_lines[0], row_taps(1))
    lines_ref[1] = spread(d_lines[0], row_taps(2))
    lines_ref[2] = spread(d_lines[1], row_taps(0))
    lines_ref[3] = spread(d_lines[1], row_taps(1))
    lines_ref[4] = spread(d_lines[2], col_taps(1))
    lines_ref[5] = spread(d_lines[2], col_taps(2))
    lines_ref[6] = spread(d_lines[3], col_taps(0))
    lines_ref[7] = spread(d_lines[3], col_taps(1))


def patch_kernel(waits, part_ref, rows_ref, blocks_ref, wide_ref):
    last = S - 1
    wide_ref[...] = part_ref[...].astype(F32)
    rows = rows_ref[...].astype(F32)
    wide_ref[:, 0, :] = rows[2 * S : 3 * S]
    wide_ref[:, last, :] = rows[3 * S : 4 * S]
    wide_ref[0] = rows[0:S]
    wide_ref[last] = rows[S : 2 * S]
    blocks_ref[...] = wide_ref[...].astype(BF)


def join_kernel(
    waits, pos_ref, seam_ref, corner_ref, base_ref, lines_ref, recv_ref, out_ref, acc_ref
):
    strips, cells = take_slots(recv_ref, pos_ref[0], seam_ref, corner_ref)
    last = S - 1
    acc_ref[...] = base_ref[...]
    for i, add in (
        (0, strips[0] + lines_ref[0]),
        (1, lines_ref[1]),
        (last - 1, lines_ref[2]),
        (last, strips[1] + lines_ref[3]),
    ):
        acc_ref[i] = acc_ref[i] + add
    for j, add in (
        (0, strips[2] + lines_ref[4]),
        (1, lines_ref[5]),
        (last - 1, lines_ref[6]),
        (last, strips[3] + lines_ref[7]),
    ):
        acc_ref[:, j, :] = acc_ref[:, j, :] + add
    for n, (i, j) in enumerate(((0, 0), (0, last), (last, 0), (last, last))):
        acc_ref[i, pl.ds(j, 1), :] = acc_ref[i, pl.ds(j, 1), :] + cells[n]
    out_ref[...] = acc_ref[...].astype(BF)


def scale_kernel(
    waits, at_ref, own_ref, other_ref, kern_ref, chan_ref, w_in_ref, b_in_ref, w_out_ref, entries
):
    core = at_ref[0] % 2
    halves = (own_ref, other_ref)
    sums = []
    for half in range(2):
        def one_half(j, acc, half=half):
            v = jnp.where(core == half, own_ref[j].astype(F32), other_ref[j].astype(F32))
            return acc + jnp.sum((v * v).reshape(CHUNK // 8, 8, C), axis=0)

        sums.append(lax.fori_loop(0, 16, one_half, jnp.zeros((8, C), F32)))
    total = jnp.sum(jnp.sum(sums[0] + sums[1], axis=0, keepdims=True), axis=1, keepdims=True)
    scale = 1.0 / jnp.sqrt(total / entries + 1e-06)

    for j in range(32):
        c, k = j // 16, j % 16
        if j == 16:
            waits["flush"](2)

        def emit(ref, j=j, k=k):
            rows = ref[k, pl.ds(0, 64), :].astype(F32) * scale
            if j < 16:
                w_in_ref[64 * (j % 4) : 64 * (j % 4) + 64, 256 * (j // 4) : 256 * (j // 4) + 256] = rows
            else:
                w_out_ref[64 * (j - 16) : 64 * (j - 16) + 64, :] = rows
            row = ref[k, pl.ds(64, 8), :].astype(F32)[0:1] * scale
            if j < 9:
                kern_ref[j : j + 1, :] = row
            elif j < 13:
                chan_ref[j - 9 : j - 8, :] = row
            elif j < 17:
                b_in_ref[:, 256 * (j - 13) : 256 * (j - 13) + 256] = row

        for near in range(2):

            @pl.when((core == c) == (near == 1))
            def _(emit=emit, near=near):
                emit(halves[1 - near])


def at(y, x, h, c):
    return ((y * 4 + x) * 2 + h) * 2 + c


def moves(axis, d):
    pairs = []
    for y in range(4):
        for x in range(4):
            for h in range(2):
                for c in range(2):
                    to = {
                        "y": ((y + d) % 4, x, h, c),
                        "x": (y, (x + d) % 4, h, c),
                        "h": (y, x, 1 - h, c),
                        "c": (y, x, h, 1 - c),
                    }[axis]
                    pairs.append((at(y, x, h, c), at(*to)))
    return pairs


def exchange(slots):
    halves = [[at(p // 8, p // 2 % 4, h, p % 2) for p in range(32)] for h in range(2)]
    return lax.all_to_all(slots, "space", 0, 0, axis_index_groups=halves, tiled=True)


def plane(slots):
    planes = [
        [at(p % 4, p // 4, h, c) for p in range(16)] for h in range(2) for c in range(2)
    ]
    return lax.all_to_all(slots, "space", 0, 0, axis_index_groups=planes, tiled=True)


def sum_over_devices(own, send, slots):
    other = lax.ppermute(send, "space", moves("c", 1))
    rest = (own + other.astype(F32)).astype(BF)
    parts = plane(rest)
    piece = lax.optimization_barrier(jnp.sum(parts.astype(F32), axis=0))
    back = exchange(slots)
    mine = piece.astype(BF)
    other = lax.ppermute(mine, "space", moves("h", 1))
    piece = mine.astype(F32) + other.astype(F32)
    turn = lambda d: [(i, (i + d) % 4) for i in range(4)]
    mine = piece.astype(BF)
    got = [mine] + [lax.ppermute(mine, "batch", turn(d)) for d in (1, 2, 3)]
    got = [g.astype(F32) for g in got]
    piece = (got[0] + got[2]) + (got[1] + got[3])
    piece, back = lax.optimization_barrier((piece.astype(BF), back))
    full = plane(jnp.broadcast_to(piece[None], (16, CHUNK, C)))
    return full, lax.ppermute(full, "space", moves("c", 1)), back


def shards(
    fields,
    cotangent,
    dw_kernel,
    dw_bias,
    ln_gain,
    ln_shift,
    w_in,
    b_in,
    w_out,
    b_out,
    seam_links,
    corner_links,
):
    here = lax.axis_index("space").reshape(1)
    links, diagonals = seam_links.T, corner_links.T
    field = fields[0, 0]
    cot = cotangent[0, 0]
    sds = jax.ShapeDtypeStruct
    edges = sds((EDGE, C), BF)
    wide = pltpu.VMEM((S, S, C), F32)

    def to_slots(mine):
        other = lax.ppermute(mine, "space", moves("h", 1))
        return staged_call(
            slot_kernel,
            [(here, "smem", 0), (links, "smem", 0), (mine, "vmem", 0), (other, "vmem", 0)],
            [(sds((32, SLOT, C), BF), True)],
            [],
            63,
        )[0]

    (field_edges,) = staged_call(edge_kernel, [(field, "vmem", 0)], [(edges, True)], [wide], 63)
    halo = exchange(to_slots(field_edges))

    cells = S * S
    row = lambda v: (v.reshape(1, -1), "vmem", 0)
    weights = [
        (dw_kernel, "vmem", 0),
        row(dw_bias),
        row(ln_gain),
        row(ln_shift),
        row(b_out),
        (w_in, "vmem", 1),
        row(b_in),
        (w_out, "vmem", 1),
    ]
    part, base, grads = staged_call(
        inside_kernel,
        [(field, "vmem", 0), (cot.reshape(cells, C), "vmem", 0)] + weights,
        [
            (sds((cells, C), BF), True),
            (sds((S, S, C), F32), True),
            (sds((32, CHUNK, C), F32), True),
        ],
        [
            pltpu.VMEM((3, S + 2, S, C), F32),
            pltpu.VMEM((cells, C), F32),
            pltpu.VMEM((cells, 128), F32),
            pltpu.VMEM((cells, C), BF),
            pltpu.VMEM((cells, H), BF),
            pltpu.VMEM((cells, H), BF),
            pltpu.VMEM((cells, C), BF),
            wide,
        ],
        63,
        pl.CostEstimate(
            flops=12 * cells * C * H, bytes_accessed=8 << 20, transcendentals=cells * H
        ),
    )
    where = [(here, "smem", 0), (links, "smem", 0), (diagonals, "smem", 0)]
    border_rows, dconv, own, send = staged_call(
        border_kernel,
        where
        + [(field, "vmem", 0), (cot, "vmem", 0), (halo, "vmem", 0)]
        + weights
        + [(grads, "vmem", 1)],
        [
            (sds((4 * S, C), BF), True),
            (sds((4 * S, C), F32), True),
            (sds((16, CHUNK, C), F32), True),
            (sds((16, CHUNK, C), BF), True),
        ],
        [wide],
        63,
    )
    lines, rim = staged_call(
        rim_kernel,
        [(dconv, "vmem", 0), (dw_kernel, "vmem", 0)],
        [(sds((8, S, C), F32), True), (edges, True)],
        [],
        63,
    )
    (blocks,) = staged_call(
        patch_kernel,
        [(part.reshape(S, S, C), "vmem", 0), (border_rows, "vmem", 0)],
        [(sds((S, S, C), BF), True)],
        [wide],
        63,
    )
    near, far, back = sum_over_devices(own, send, to_slots(rim))
    (grad_tile,) = staged_call(
        join_kernel,
        where + [(base, "vmem", 0), (lines, "vmem", 0), (back, "here", 0)],
        [(sds((S, S, C), BF), True)],
        [wide],
        10,
    )
    entries = 13 * C + 2 * C * H + H
    grad_kernel, grad_channels, grad_w_in, grad_b_in, grad_w_out = staged_call(
        functools.partial(scale_kernel, entries=entries),
        [(here, "smem", 0), (near, "here", 0), (far, "here", 0)],
        [
            (sds((9, C), F32), True),
            (sds((4, C), F32), True),
            (sds((C, H), F32), True),
            (sds((1, H), F32), True),
            (sds((H, C), F32), True),
        ],
        [],
        10,
    )
    return (
        blocks[None, None],
        grad_tile[None, None],
        grad_kernel,
        grad_channels,
        grad_w_in,
        grad_b_in.reshape(H),
        grad_w_out,
    )


def solution(mesh):
    tile = P("batch", "space", None, None, None)

    return jax.shard_map(
        shards,
        mesh=mesh,
        in_specs=(tile, tile) + (P(),) * 10,
        out_specs=(tile, tile) + (P(),) * 5,
        check_vma=False,
    )
```

```python
import functools

import jax
import jax.numpy as jnp
from jax import lax
from jax.experimental import pallas as pl
from jax.experimental.pallas import tpu as pltpu
from jax.sharding import PartitionSpec as P


S = 32
C = 256
H = 1024
SLOT = 72
EDGE = 136
CHUNK = 72
BF = jnp.bfloat16
F32 = jnp.float32
GELU_C = 0.7978845608028654
VMEM = functools.partial(pl.BlockSpec, memory_space=pltpu.VMEM)


def staged_call(kernel, ins, outs, scratch, mib, cost=None):
    n_in, n_out = len(ins), len(outs)
    space = {"vmem": pltpu.VMEM, "smem": pltpu.SMEM}
    in_bufs = [space[w](a.shape, a.dtype) for a, w, _ in ins if w != "here"]
    out_bufs = [pltpu.VMEM(o.shape, o.dtype) for o, to_hbm in outs if to_hbm]
    hbm = pl.BlockSpec(memory_space=pltpu.HBM)

    def body(*refs):
        given, results = refs[:n_in], refs[n_in : n_in + n_out]
        rest = list(refs[n_in + n_out :])
        sems = rest.pop(0)
        stages = [rest.pop(0) for _ in in_bufs]
        drains = [rest.pop(0) for _ in out_bufs]
        args, waits, soon, n = [], {}, [], 0
        for i, (ref, (_, where, late)) in enumerate(zip(given, ins)):
            if where == "here":
                args.append(ref)
                continue
            copy = pltpu.make_async_copy(ref, stages[n], sems.at[n])
            copy.start()
            args.append(stages[n])
            n += 1
            if late:
                waits[i] = copy.wait
            else:
                soon.append(copy)
        for copy in soon:
            copy.wait()
        writes = []
        for ref, (_, to_hbm) in zip(results, outs):
            if to_hbm:
                drain = drains.pop(0)
                writes.append(pltpu.make_async_copy(drain, ref, sems.at[n]))
                args.append(drain)
                n += 1
            else:
                args.append(ref)
        started = []

        def flush(i):
            writes[i].start()
            started.append(i)

        waits["flush"] = flush
        kernel(waits, *args, *rest)
        for i, copy in enumerate(writes):
            if i not in started:
                copy.start()
        for copy in writes:
            copy.wait()

    return pl.pallas_call(
        body,
        out_shape=tuple(o for o, _ in outs),
        in_specs=[VMEM() if w == "here" else hbm for _, w, _ in ins],
        out_specs=tuple(hbm if to_hbm else VMEM() for _, to_hbm in outs),
        scratch_shapes=[pltpu.SemaphoreType.DMA((len(in_bufs) + len(out_bufs) + 1,))]
        + in_bufs
        + out_bufs
        + scratch,
        compiler_params=pltpu.CompilerParams(vmem_limit_bytes=mib * 1024 * 1024),
        cost_estimate=cost,
    )(*(a for a, _, _ in ins))


def put_edges(out_ref, strips, cells):
    for e in range(4):
        out_ref[pl.ds(S * e, S), :] = strips[e].astype(BF)
    cells8 = jnp.concatenate([c.reshape(1, C) for c in cells] + [jnp.zeros((4, C), F32)], axis=0)
    out_ref[pl.ds(4 * S, 8), :] = cells8.astype(BF)


def half_of(tile):
    return (tile // 2) % 2


def place_of(tile):
    return (tile // 4) * 2 + tile % 2


def take_slots(recv_ref, pos, seam_ref, corner_ref):
    rows = lax.broadcasted_iota(jnp.int32, (S, S), 0)
    cols = lax.broadcasted_iota(jnp.int32, (S, S), 1)
    strips = []
    for e in range(4):
        code = seam_ref[e, pos]
        tile = code // 8
        target = jnp.where(code % 2 == 1, S - 1 - rows, rows)
        turn = (cols == target).astype(F32).astype(BF)
        strip = recv_ref[place_of(tile), pl.ds(pl.multiple_of(S * half_of(tile), S), S), :]
        strips.append(jnp.dot(turn, strip, preferred_element_type=F32))
    cells = []
    row8 = lax.broadcasted_iota(jnp.int32, (SLOT - 2 * S, C), 0)
    for k in range(4):
        code = corner_ref[k, pos]
        tile = code // 4
        block = recv_ref[place_of(tile), pl.ds(2 * S, SLOT - 2 * S), :].astype(F32)
        row = 4 * half_of(tile) + code % 4
        cells.append(jnp.sum(jnp.where(row8 == row, block, 0.0), axis=0, keepdims=True))
    return strips, cells


def edge_kernel(waits, field_ref, out_ref, wide_ref):
    wide_ref[...] = field_ref[...].astype(F32)
    strips = [wide_ref[0], wide_ref[S - 1], wide_ref[:, 0, :], wide_ref[:, S - 1, :]]
    cells = [wide_ref[i, pl.ds(j, 1), :] for i in (0, S - 1) for j in (0, S - 1)]
    put_edges(out_ref, strips, cells)


def slot_kernel(waits, pos_ref, seam_ref, own_ref, other_ref, out_ref):
    pos = pos_ref[0]
    half = half_of(pos)
    mine = own_ref[pl.ds(4 * S, 8), :].astype(F32)
    other = other_ref[pl.ds(4 * S, 8), :].astype(F32)
    row8 = lax.broadcasted_iota(jnp.int32, (8, C), 0)
    first = jnp.where(half == 0, mine, other)
    second = jnp.where(half == 0, other, mine)
    cells8 = jnp.where(row8 < 4, first, pltpu.roll(second, 4, 0)).astype(BF)

    def put(p, carry):
        out_ref[p, pl.ds(2 * S, SLOT - 2 * S), :] = cells8
        return carry

    lax.fori_loop(0, 32, put, 0)
    for source, edges, at_half in ((pos, own_ref, half), (pos ^ 2, other_ref, 1 - half)):
        for e in range(4):
            tile = seam_ref[e, source] // 8

            @pl.when(half_of(tile) == half)
            def _(tile=tile, edges=edges, at_half=at_half, e=e):
                rows = pl.ds(pl.multiple_of(S * at_half, S), S)
                out_ref[place_of(tile), rows, :] = edges[pl.ds(S * e, S), :]


def mlp_rows(normed, cot, out, gain_parts, w_in_ref, b_in_ref, w_out_ref, keep):
    gain, xhat, istd = gain_parts
    dnorm = jnp.zeros(out.shape, F32)
    sums = []
    for n in range(4):
        h = slice(256 * n, 256 * n + 256)
        z = jnp.dot(normed, w_in_ref[:, h], preferred_element_type=F32) + b_in_ref[:, h]
        dact = lax.dot_general(
            cot, w_out_ref[h, :], (((1,), (1,)), ((), ())), preferred_element_type=F32
        )
        z2 = z * z
        half = 0.5 + 0.5 * jnp.tanh(z * (GELU_C + (GELU_C * 0.044715) * z2))
        act = z * half
        slope = half + act * (1.0 - half) * (2 * GELU_C + (6 * GELU_C * 0.044715) * z2)
        act = act.astype(BF)
        dhid = (dact * slope).astype(BF)
        keep(n, act, dhid)
        sums.append(jnp.sum(dhid.astype(F32), axis=0, keepdims=True))
        out = out + jnp.dot(act, w_out_ref[h, :], preferred_element_type=F32)
        dnorm = dnorm + lax.dot_general(
            dhid, w_in_ref[:, h], (((1,), (1,)), ((), ())), preferred_element_type=F32
        )
    dunit = dnorm * gain
    dconv = istd * (
        dunit
        - jnp.mean(dunit, axis=1, keepdims=True)
        - xhat * jnp.mean(dunit * xhat, axis=1, keepdims=True)
    )
    sums.append(jnp.sum(dnorm * xhat, axis=0, keepdims=True))
    sums.append(jnp.sum(dnorm, axis=0, keepdims=True))
    return out.astype(BF), dconv.astype(BF).astype(F32), sums


def norm_rows(rows):
    centred = rows - jnp.mean(rows, axis=1, keepdims=True)
    istd = 1.0 / jnp.sqrt(jnp.mean(centred * centred, axis=1, keepdims=True) + 1e-06)
    return centred * istd, istd


OVER_ROWS = (((0,), (0,)), ((), ()))


def inside_kernel(
    waits,
    field_ref,
    cot_ref,
    kern_ref,
    bias_ref,
    gain_ref,
    shift_ref,
    b_out_ref,
    w_in_ref,
    b_in_ref,
    w_out_ref,
    blocks_ref,
    base_ref,
    grad_ref,
    edge_ref,
    pad_ref,
    xhat_ref,
    istd_ref,
    normed_ref,
    active_ref,
    dhid_ref,
    keep_ref,
    dconv_ref,
):
    center = field_ref[...].astype(F32)
    pad_ref[:, 0] = jnp.zeros((3, S, C), F32)
    pad_ref[:, S + 1] = jnp.zeros((3, S, C), F32)
    pad_ref[1, pl.ds(1, S)] = center
    pad_ref[0, pl.ds(1, S)] = pltpu.roll(center, 1, 1)
    pad_ref[2, pl.ds(1, S)] = pltpu.roll(center, S - 1, 1)

    last = S - 1
    for n, i in enumerate((0, 1, last - 1, last)):
        edge_ref[n] = pad_ref[1, i + 1].astype(BF)
        edge_ref[4 + n] = pad_ref[1, pl.ds(1, S), i, :].astype(BF)
    dconv_ref[...] = cot_ref[...].astype(F32).reshape(S, S, C)
    for n, i in enumerate((0, last)):
        edge_ref[8 + n] = dconv_ref[i].astype(BF)
        edge_ref[10 + n] = dconv_ref[:, i, :].astype(BF)

    bias = bias_ref[...]
    gain = gain_ref[...]
    shift = shift_ref[...]
    b_out = b_out_ref[...]
    rowid = lax.broadcasted_iota(jnp.int32, (256, C), 0)
    col = rowid & (S - 1)

    def forward_rows(b, carry):
        r0 = b * 8
        acc = jnp.zeros((8, S, C), F32) + bias.reshape(1, 1, C)
        for u in range(3):
            for v in range(3):
                k = 3 * u + v
                acc = acc + pad_ref[v, pl.ds(r0 + u, 8)] * kern_ref[k : k + 1, :].reshape(1, 1, C)
        xhat, istd = norm_rows(acc.reshape(8 * S, C))
        q = pl.ds(pl.multiple_of(b * 256, 256), 256)
        xhat_ref[q, :] = xhat
        istd_ref[q, :] = jnp.broadcast_to(istd, (256, 128))
        normed_ref[q, :] = (xhat * gain + shift).astype(BF)
        row = r0 + (rowid >> 5)
        kept = (col > 0) & (col < S - 1) & (row > 0) & (row < S - 1)
        keep_ref[q, :] = jnp.where(kept, cot_ref[q, :].astype(F32), 0.0).astype(BF)
        return carry

    lax.fori_loop(0, 4, forward_rows, 0)
    waits[7]()
    waits[9]()

    def block_rows(b, carry):
        q = pl.ds(pl.multiple_of(b * 256, 256), 256)

        def keep(n, act, dhid):
            active_ref[q, 256 * n : 256 * n + 256] = act
            dhid_ref[q, 256 * n : 256 * n + 256] = dhid

        out = field_ref[pl.ds(b * 8, 8)].reshape(256, C).astype(F32) + b_out
        parts = (gain, xhat_ref[q, :], istd_ref[q, 0:1])
        out, dconv, sums = mlp_rows(
            normed_ref[q, :], keep_ref[q, :], out, parts, w_in_ref, b_in_ref, w_out_ref, keep
        )
        blocks_ref[q, :] = out
        dconv_ref[pl.ds(b * 8, 8)] = dconv.reshape(8, S, C)
        sums.append(jnp.sum(cot_ref[q, :].astype(F32), axis=0, keepdims=True))
        return tuple(a + x for a, x in zip(carry, sums))

    zero = jnp.zeros((1, C), F32)
    *g_bin, g_gain, g_shift, g_bout = lax.fori_loop(0, 4, block_rows, (zero,) * 7)

    for n in range(4):
        h = slice(256 * n, 256 * n + 256)
        dot = functools.partial(lax.dot_general, dimension_numbers=OVER_ROWS, preferred_element_type=F32)
        g = dot(normed_ref[...], dhid_ref[:, h])
        grad_ref[4 * n : 4 * n + 4, pl.ds(0, 64), :] = g.reshape(4, 64, C)
        g = dot(active_ref[:, h], keep_ref[...])
        grad_ref[16 + 4 * n : 20 + 4 * n, pl.ds(0, 64), :] = g.reshape(4, 64, C)

    g_kernel = []
    for u in range(3):
        for v in range(3):

            def tap_rows(b, acc, u=u, v=v):
                part = pad_ref[v, pl.ds(b * 4 + u, 4)] * dconv_ref[pl.ds(b * 4, 4)]
                return acc + jnp.sum(part.reshape(4 * S // 8, 8, C), axis=0)

            acc = lax.fori_loop(0, 8, tap_rows, jnp.zeros((8, C), F32))
            g_kernel.append(jnp.sum(acc, axis=0, keepdims=True))

    def bias_rows(b, acc):
        return acc + jnp.sum(dconv_ref[pl.ds(b * 4, 4)].reshape(4 * S // 8, 8, C), axis=0)

    g_bias = jnp.sum(lax.fori_loop(0, 8, bias_rows, jnp.zeros((8, C), F32)), axis=0, keepdims=True)

    small = g_kernel + [g_bias, g_gain, g_shift, g_bout] + g_bin + [zero] * 15
    row8 = lax.broadcasted_iota(jnp.int32, (CHUNK - 64, C), 0)
    for j in range(32):
        grad_ref[j, pl.ds(64, CHUNK - 64), :] = jnp.where(row8 == 0, small[j], 0.0)

    def shift_rows(i, carry):
        row = dconv_ref[i]
        pad_ref[1, i + 1] = row
        pad_ref[0, i + 1] = pltpu.roll(row, S - 1, 0)
        pad_ref[2, i + 1] = pltpu.roll(row, 1, 0)
        return carry

    lax.fori_loop(0, S, shift_rows, 0)
    taps = [kern_ref[k : k + 1, :].reshape(1, 1, C) for k in range(9)]

    def inner_rows(b, carry):
        q = pl.ds(pl.multiple_of(b * 4 * S, 4 * S), 4 * S)
        acc = cot_ref[q, :].astype(F32).reshape(4, S, C)
        for u in range(3):
            for v in range(3):
                acc = acc + pad_ref[v, pl.ds(b * 4 + 2 - u, 4)] * taps[3 * u + v]
        base_ref[pl.ds(b * 4, 4)] = acc
        return carry

    lax.fori_loop(0, 8, inner_rows, 0)


def border_kernel(
    waits,
    pos_ref,
    seam_ref,
    corner_ref,
    edge_ref,
    recv_ref,
    kern_ref,
    bias_ref,
    gain_ref,
    shift_ref,
    b_out_ref,
    w_in_ref,
    b_in_ref,
    w_out_ref,
    grad_ref,
    rows_ref,
    dconv_ref,
    own_ref,
    send_ref,
):
    pos = pos_ref[0]
    core = pos % 2
    strips, cells = take_slots(recv_ref, pos, seam_ref, corner_ref)
    top, bottom, left, right = strips
    last = S - 1
    order = {0: 0, 1: 1, last - 1: 2, last: 3}
    at_row = lambda i: edge_ref[order[i]].astype(F32)
    at_col = lambda j: edge_ref[4 + order[j]].astype(F32)
    spot = lambda line, i: line[i : i + 1]
    place = lax.broadcasted_iota(jnp.int32, (S, C), 0)
    flat = lambda k: kern_ref[k : k + 1, :]

    bands = [
        (
            (top, at_row(0), at_row(1)),
            ((cells[0], cells[1]), (spot(left, 0), spot(right, 0)), (spot(left, 1), spot(right, 1))),
            lambda a, s: 3 * a + s,
        ),
        (
            (bottom, at_row(last), at_row(last - 1)),
            (
                (cells[2], cells[3]),
                (spot(left, last), spot(right, last)),
                (spot(left, last - 1), spot(right, last - 1)),
            ),
            lambda a, s: 3 * (2 - a) + s,
        ),
        (
            (left, at_col(0), at_col(1)),
            ((cells[0], cells[2]), (spot(top, 0), spot(bottom, 0)), (spot(top, 1), spot(bottom, 1))),
            lambda a, s: 3 * s + a,
        ),
        (
            (right, at_col(last), at_col(last - 1)),
            (
                (cells[1], cells[3]),
                (spot(top, last), spot(bottom, last)),
                (spot(top, last - 1), spot(bottom, last - 1)),
            ),
            lambda a, s: 3 * s + 2 - a,
        ),
    ]
    windows = [[None] * 9 for _ in range(4)]
    rows = []
    for n, (lines, ends, tap) in enumerate(bands):
        acc = jnp.zeros((S, C), F32) + bias_ref[...]
        for a in range(3):
            before = jnp.where(place == 0, ends[a][0], pltpu.roll(lines[a], 1, 0))
            after = jnp.where(place == last, ends[a][1], pltpu.roll(lines[a], last, 0))
            for s, window in enumerate((before, lines[a], after)):
                k = tap(a, s)
                windows[n][k] = window
                acc = acc + window * flat(k)
        rows.append(acc)
    field_rows = jnp.concatenate([lines[1] for lines, _, _ in bands], axis=0)
    once = (place > 0) & (place < last)
    cot_rows = jnp.concatenate(
        [edge_ref[8].astype(F32), edge_ref[9].astype(F32)]
        + [jnp.where(once, edge_ref[n].astype(F32), 0.0) for n in (10, 11)],
        axis=0,
    ).astype(BF)

    gain = gain_ref[...]
    waits[10]()
    waits[12]()
    xhat, istd = norm_rows(jnp.concatenate(rows, axis=0))
    normed = (xhat * gain + shift_ref[...]).astype(BF)
    kept = []
    out, dconv, sums = mlp_rows(
        normed,
        cot_rows,
        field_rows + b_out_ref[...],
        (gain, xhat, istd),
        w_in_ref,
        b_in_ref,
        w_out_ref,
        lambda n, act, dhid: kept.append((act, dhid)),
    )
    rows_ref[...] = out
    *g_bin, g_gain, g_shift = sums
    d_lines = [dconv[S * n : S * n + S] for n in range(4)]

    dconv_ref[...] = dconv

    waits[13]()

    def put_rows(first, value):
        mine = core == first // 16
        base = first % 16
        value = value.reshape(4, 64, C) + grad_ref[first : first + 4, pl.ds(0, 64), :]

        @pl.when(mine)
        def _():
            own_ref[pl.ds(base, 4), pl.ds(0, 64), :] = value

        @pl.when(jnp.logical_not(mine))
        def _():
            send_ref[pl.ds(base, 4), pl.ds(0, 64), :] = value.astype(BF)

    for n in range(4):
        act, dhid = kept[n]
        put_rows(4 * n, lax.dot_general(normed, dhid, OVER_ROWS, preferred_element_type=F32))
        put_rows(16 + 4 * n, lax.dot_general(act, cot_rows, OVER_ROWS, preferred_element_type=F32))

    g_kernel = []
    for k in range(9):
        acc = sum(windows[n][k] * d_lines[n] for n in range(4))
        g_kernel.append(jnp.sum(acc, axis=0, keepdims=True))
    zero = jnp.zeros((1, C), F32)
    g_bias = jnp.sum(dconv, axis=0, keepdims=True)
    small = g_kernel + [g_bias, g_gain, g_shift, zero] + g_bin + [zero] * 15
    row8 = lax.broadcasted_iota(jnp.int32, (CHUNK - 64, C), 0)
    for j in range(32):
        row = jnp.where(row8 == 0, small[j], 0.0) + grad_ref[j, pl.ds(64, CHUNK - 64), :]

        @pl.when(core == j // 16)
        def _(row=row, j=j):
            own_ref[j % 16, pl.ds(64, CHUNK - 64), :] = row

        @pl.when(core != j // 16)
        def _(row=row, j=j):
            send_ref[j % 16, pl.ds(64, CHUNK - 64), :] = row.astype(BF)


def rim_kernel(waits, dconv_ref, kern_ref, lines_ref, rim_ref):
    last = S - 1
    spot = lambda line, i: line[i : i + 1]
    place = lax.broadcasted_iota(jnp.int32, (S, C), 0)
    flat = lambda k: kern_ref[k : k + 1, :]
    d_lines = [dconv_ref[S * n : S * n + S] for n in range(4)]

    def spread(line, taps):
        back = jnp.where(place == last, 0.0, pltpu.roll(line, last, 0))
        ahead = jnp.where(place == 0, 0.0, pltpu.roll(line, 1, 0))
        return back * flat(taps[0]) + line * flat(taps[1]) + ahead * flat(taps[2])

    def whole(line, at):
        line = jnp.where(place == 0, spot(d_lines[0], at), line)
        return jnp.where(place == last, spot(d_lines[1], at), line)

    row_taps = lambda u: (3 * u, 3 * u + 1, 3 * u + 2)
    col_taps = lambda v: (v, 3 + v, 6 + v)
    rim = [
        spread(d_lines[0], row_taps(0)),
        spread(d_lines[1], row_taps(2)),
        spread(whole(d_lines[2], 0), col_taps(0)),
        spread(whole(d_lines[3], last), col_taps(2)),
    ]
    corners = [
        spot(d_lines[0], 0) * flat(0),
        spot(d_lines[0], last) * flat(2),
        spot(d_lines[1], 0) * flat(6),
        spot(d_lines[1], last) * flat(8),
    ]
    put_edges(rim_ref, rim, corners)
    lines_ref[0] = spread(d_lines[0], row_taps(1))
    lines_ref[1] = spread(d_lines[0], row_taps(2))
    lines_ref[2] = spread(d_lines[1], row_taps(0))
    lines_ref[3] = spread(d_lines[1], row_taps(1))
    lines_ref[4] = spread(d_lines[2], col_taps(1))
    lines_ref[5] = spread(d_lines[2], col_taps(2))
    lines_ref[6] = spread(d_lines[3], col_taps(0))
    lines_ref[7] = spread(d_lines[3], col_taps(1))


def patch_kernel(waits, part_ref, rows_ref, blocks_ref, wide_ref):
    last = S - 1
    wide_ref[...] = part_ref[...].astype(F32)
    rows = rows_ref[...].astype(F32)
    wide_ref[:, 0, :] = rows[2 * S : 3 * S]
    wide_ref[:, last, :] = rows[3 * S : 4 * S]
    wide_ref[0] = rows[0:S]
    wide_ref[last] = rows[S : 2 * S]
    blocks_ref[...] = wide_ref[...].astype(BF)


def join_kernel(
    waits, pos_ref, seam_ref, corner_ref, base_ref, lines_ref, recv_ref, out_ref, acc_ref
):
    strips, cells = take_slots(recv_ref, pos_ref[0], seam_ref, corner_ref)
    last = S - 1
    acc_ref[...] = base_ref[...]
    for i, add in (
        (0, strips[0] + lines_ref[0]),
        (1, lines_ref[1]),
        (last - 1, lines_ref[2]),
        (last, strips[1] + lines_ref[3]),
    ):
        acc_ref[i] = acc_ref[i] + add
    for j, add in (
        (0, strips[2] + lines_ref[4]),
        (1, lines_ref[5]),
        (last - 1, lines_ref[6]),
        (last, strips[3] + lines_ref[7]),
    ):
        acc_ref[:, j, :] = acc_ref[:, j, :] + add
    for n, (i, j) in enumerate(((0, 0), (0, last), (last, 0), (last, last))):
        acc_ref[i, pl.ds(j, 1), :] = acc_ref[i, pl.ds(j, 1), :] + cells[n]
    out_ref[...] = acc_ref[...].astype(BF)


def scale_kernel(
    waits, at_ref, own_ref, other_ref, kern_ref, chan_ref, w_in_ref, b_in_ref, w_out_ref, entries
):
    core = at_ref[0] % 2
    halves = (own_ref, other_ref)
    sums = []
    for half in range(2):
        def one_half(j, acc, half=half):
            v = jnp.where(core == half, own_ref[j].astype(F32), other_ref[j].astype(F32))
            return acc + jnp.sum((v * v).reshape(CHUNK // 8, 8, C), axis=0)

        sums.append(lax.fori_loop(0, 16, one_half, jnp.zeros((8, C), F32)))
    total = jnp.sum(jnp.sum(sums[0] + sums[1], axis=0, keepdims=True), axis=1, keepdims=True)
    scale = 1.0 / jnp.sqrt(total / entries + 1e-06)

    for j in range(32):
        c, k = j // 16, j % 16
        if j == 16:
            waits["flush"](2)

        def emit(ref, j=j, k=k):
            rows = ref[k, pl.ds(0, 64), :].astype(F32) * scale
            if j < 16:
                w_in_ref[64 * (j % 4) : 64 * (j % 4) + 64, 256 * (j // 4) : 256 * (j // 4) + 256] = rows
            else:
                w_out_ref[64 * (j - 16) : 64 * (j - 16) + 64, :] = rows
            row = ref[k, pl.ds(64, 8), :].astype(F32)[0:1] * scale
            if j < 9:
                kern_ref[j : j + 1, :] = row
            elif j < 13:
                chan_ref[j - 9 : j - 8, :] = row
            elif j < 17:
                b_in_ref[:, 256 * (j - 13) : 256 * (j - 13) + 256] = row

        for near in range(2):

            @pl.when((core == c) == (near == 1))
            def _(emit=emit, near=near):
                emit(halves[1 - near])


def at(y, x, h, c):
    return ((y * 4 + x) * 2 + h) * 2 + c


def moves(axis, d):
    pairs = []
    for y in range(4):
        for x in range(4):
            for h in range(2):
                for c in range(2):
                    to = {
                        "y": ((y + d) % 4, x, h, c),
                        "x": (y, (x + d) % 4, h, c),
                        "h": (y, x, 1 - h, c),
                        "c": (y, x, h, 1 - c),
                    }[axis]
                    pairs.append((at(y, x, h, c), at(*to)))
    return pairs


def exchange(slots):
    halves = [[at(p // 8, p // 2 % 4, h, p % 2) for p in range(32)] for h in range(2)]
    return lax.all_to_all(slots, "space", 0, 0, axis_index_groups=halves, tiled=True)


def plane(slots):
    planes = [
        [at(p % 4, p // 4, h, c) for p in range(16)] for h in range(2) for c in range(2)
    ]
    return lax.all_to_all(slots, "space", 0, 0, axis_index_groups=planes, tiled=True)


def sum_over_devices(own, send, slots):
    other = lax.ppermute(send, "space", moves("c", 1))
    rest = (own + other.astype(F32)).astype(BF)
    parts = plane(rest)
    piece = lax.optimization_barrier(jnp.sum(parts.astype(F32), axis=0))
    back = exchange(slots)
    mine = piece.astype(BF)
    other = lax.ppermute(mine, "space", moves("h", 1))
    piece = mine.astype(F32) + other.astype(F32)
    turn = lambda d: [(i, (i + d) % 4) for i in range(4)]
    mine = piece.astype(BF)
    got = [mine] + [lax.ppermute(mine, "batch", turn(d)) for d in (1, 2, 3)]
    got = [g.astype(F32) for g in got]
    piece = (got[0] + got[2]) + (got[1] + got[3])
    spread = jnp.broadcast_to(piece.astype(BF)[None], (16, CHUNK, C))
    spread, back = lax.optimization_barrier((spread, back))
    full = plane(spread)
    return full, lax.ppermute(full, "space", moves("c", 1)), back


def shards(
    fields,
    cotangent,
    dw_kernel,
    dw_bias,
    ln_gain,
    ln_shift,
    w_in,
    b_in,
    w_out,
    b_out,
    seam_links,
    corner_links,
):
    here = lax.axis_index("space").reshape(1)
    links, diagonals = seam_links.T, corner_links.T
    field = fields[0, 0]
    cot = cotangent[0, 0]
    sds = jax.ShapeDtypeStruct
    edges = sds((EDGE, C), BF)
    wide = pltpu.VMEM((S, S, C), F32)

    def to_slots(mine):
        other = lax.ppermute(mine, "space", moves("h", 1))
        return staged_call(
            slot_kernel,
            [(here, "smem", 0), (links, "smem", 0), (mine, "vmem", 0), (other, "vmem", 0)],
            [(sds((32, SLOT, C), BF), True)],
            [],
            63,
        )[0]

    (field_edges,) = staged_call(edge_kernel, [(field, "vmem", 0)], [(edges, True)], [wide], 63)
    halo = exchange(to_slots(field_edges))

    cells = S * S
    row = lambda v: (v.reshape(1, -1), "vmem", 0)
    weights = [
        (dw_kernel, "vmem", 0),
        row(dw_bias),
        row(ln_gain),
        row(ln_shift),
        row(b_out),
        (w_in, "vmem", 1),
        row(b_in),
        (w_out, "vmem", 1),
    ]
    part, base, grads, border_lines = staged_call(
        inside_kernel,
        [(field, "vmem", 0), (cot.reshape(cells, C), "vmem", 0)] + weights,
        [
            (sds((cells, C), BF), True),
            (sds((S, S, C), F32), True),
            (sds((32, CHUNK, C), F32), True),
            (sds((12, S, C), BF), True),
        ],
        [
            pltpu.VMEM((3, S + 2, S, C), F32),
            pltpu.VMEM((cells, C), F32),
            pltpu.VMEM((cells, 128), F32),
            pltpu.VMEM((cells, C), BF),
            pltpu.VMEM((cells, H), BF),
            pltpu.VMEM((cells, H), BF),
            pltpu.VMEM((cells, C), BF),
            wide,
        ],
        63,
        pl.CostEstimate(
            flops=12 * cells * C * H, bytes_accessed=8 << 20, transcendentals=cells * H
        ),
    )
    where = [(here, "smem", 0), (links, "smem", 0), (diagonals, "smem", 0)]
    border_rows, dconv, own, send = staged_call(
        border_kernel,
        where
        + [(border_lines, "vmem", 0), (halo, "vmem", 0)]
        + weights
        + [(grads, "vmem", 1)],
        [
            (sds((4 * S, C), BF), True),
            (sds((4 * S, C), F32), True),
            (sds((16, CHUNK, C), F32), True),
            (sds((16, CHUNK, C), BF), True),
        ],
        [],
        63,
    )
    lines, rim = staged_call(
        rim_kernel,
        [(dconv, "vmem", 0), (dw_kernel, "vmem", 0)],
        [(sds((8, S, C), F32), True), (edges, True)],
        [],
        63,
    )
    (blocks,) = staged_call(
        patch_kernel,
        [(part.reshape(S, S, C), "vmem", 0), (border_rows, "vmem", 0)],
        [(sds((S, S, C), BF), True)],
        [wide],
        63,
    )
    near, far, back = sum_over_devices(own, send, to_slots(rim))
    (grad_tile,) = staged_call(
        join_kernel,
        where + [(base, "vmem", 0), (lines, "vmem", 0), (back, "here", 0)],
        [(sds((S, S, C), BF), True)],
        [wide],
        10,
    )
    entries = 13 * C + 2 * C * H + H
    grad_kernel, grad_channels, grad_w_in, grad_b_in, grad_w_out = staged_call(
        functools.partial(scale_kernel, entries=entries),
        [(here, "smem", 0), (near, "here", 0), (far, "here", 0)],
        [
            (sds((9, C), F32), True),
            (sds((4, C), F32), True),
            (sds((C, H), F32), True),
            (sds((1, H), F32), True),
            (sds((H, C), F32), True),
        ],
        [],
        10,
    )
    return (
        blocks[None, None],
        grad_tile[None, None],
        grad_kernel,
        grad_channels,
        grad_w_in,
        grad_b_in.reshape(H),
        grad_w_out,
    )


def solution(mesh):
    tile = P("batch", "space", None, None, None)

    return jax.shard_map(
        shards,
        mesh=mesh,
        in_specs=(tile, tile) + (P(),) * 10,
        out_specs=(tile, tile) + (P(),) * 5,
        check_vma=False,
    )
```

```python
import functools

import jax
import jax.numpy as jnp
from jax import lax
from jax.experimental import pallas as pl
from jax.experimental.pallas import tpu as pltpu
from jax.sharding import PartitionSpec as P


S = 32
C = 256
H = 1024
SLOT = 72
EDGE = 136
CHUNK = 72
BF = jnp.bfloat16
F32 = jnp.float32
GELU_C = 0.7978845608028654
VMEM = functools.partial(pl.BlockSpec, memory_space=pltpu.VMEM)


def staged_call(kernel, ins, outs, scratch, mib, cost=None):
    n_in, n_out = len(ins), len(outs)
    space = {"vmem": pltpu.VMEM, "smem": pltpu.SMEM}
    in_bufs = [space[w](a.shape, a.dtype) for a, w, _ in ins if w != "here"]
    out_bufs = [pltpu.VMEM(o.shape, o.dtype) for o, to_hbm in outs if to_hbm]
    hbm = pl.BlockSpec(memory_space=pltpu.HBM)

    def body(*refs):
        given, results = refs[:n_in], refs[n_in : n_in + n_out]
        rest = list(refs[n_in + n_out :])
        sems = rest.pop(0)
        stages = [rest.pop(0) for _ in in_bufs]
        drains = [rest.pop(0) for _ in out_bufs]
        args, waits, soon, n = [], {}, [], 0
        for i, (ref, (_, where, late)) in enumerate(zip(given, ins)):
            if where == "here":
                args.append(ref)
                continue
            copy = pltpu.make_async_copy(ref, stages[n], sems.at[n])
            copy.start()
            args.append(stages[n])
            n += 1
            if late:
                waits[i] = copy.wait
            else:
                soon.append(copy)
        for copy in soon:
            copy.wait()
        writes = []
        for ref, (_, to_hbm) in zip(results, outs):
            if to_hbm:
                drain = drains.pop(0)
                writes.append(pltpu.make_async_copy(drain, ref, sems.at[n]))
                args.append(drain)
                n += 1
            else:
                args.append(ref)
        started = []

        def flush(i):
            writes[i].start()
            started.append(i)

        waits["flush"] = flush
        kernel(waits, *args, *rest)
        for i, copy in enumerate(writes):
            if i not in started:
                copy.start()
        for copy in writes:
            copy.wait()

    return pl.pallas_call(
        body,
        out_shape=tuple(o for o, _ in outs),
        in_specs=[VMEM() if w == "here" else hbm for _, w, _ in ins],
        out_specs=tuple(hbm if to_hbm else VMEM() for _, to_hbm in outs),
        scratch_shapes=[pltpu.SemaphoreType.DMA((len(in_bufs) + len(out_bufs) + 1,))]
        + in_bufs
        + out_bufs
        + scratch,
        compiler_params=pltpu.CompilerParams(vmem_limit_bytes=mib * 1024 * 1024),
        cost_estimate=cost,
    )(*(a for a, _, _ in ins))


def put_edges(out_ref, strips, cells):
    for e in range(4):
        out_ref[pl.ds(S * e, S), :] = strips[e].astype(BF)
    cells8 = jnp.concatenate([c.reshape(1, C) for c in cells] + [jnp.zeros((4, C), F32)], axis=0)
    out_ref[pl.ds(4 * S, 8), :] = cells8.astype(BF)


def half_of(tile):
    return (tile // 2) % 2


def place_of(tile):
    return (tile // 4) * 2 + tile % 2


def take_slots(recv_ref, pos, seam_ref, corner_ref):
    rows = lax.broadcasted_iota(jnp.int32, (S, S), 0)
    cols = lax.broadcasted_iota(jnp.int32, (S, S), 1)
    strips = []
    for e in range(4):
        code = seam_ref[e, pos]
        tile = code // 8
        target = jnp.where(code % 2 == 1, S - 1 - rows, rows)
        turn = (cols == target).astype(F32).astype(BF)
        strip = recv_ref[place_of(tile), pl.ds(pl.multiple_of(S * half_of(tile), S), S), :]
        strips.append(jnp.dot(turn, strip, preferred_element_type=F32))
    cells = []
    row8 = lax.broadcasted_iota(jnp.int32, (SLOT - 2 * S, C), 0)
    for k in range(4):
        code = corner_ref[k, pos]
        tile = code // 4
        block = recv_ref[place_of(tile), pl.ds(2 * S, SLOT - 2 * S), :].astype(F32)
        row = 4 * half_of(tile) + code % 4
        cells.append(jnp.sum(jnp.where(row8 == row, block, 0.0), axis=0, keepdims=True))
    return strips, cells


def edge_kernel(waits, field_ref, out_ref, wide_ref):
    wide_ref[...] = field_ref[...].astype(F32)
    strips = [wide_ref[0], wide_ref[S - 1], wide_ref[:, 0, :], wide_ref[:, S - 1, :]]
    cells = [wide_ref[i, pl.ds(j, 1), :] for i in (0, S - 1) for j in (0, S - 1)]
    put_edges(out_ref, strips, cells)


def slot_kernel(waits, pos_ref, seam_ref, own_ref, other_ref, out_ref):
    pos = pos_ref[0]
    half = half_of(pos)
    mine = own_ref[pl.ds(4 * S, 8), :].astype(F32)
    other = other_ref[pl.ds(4 * S, 8), :].astype(F32)
    row8 = lax.broadcasted_iota(jnp.int32, (8, C), 0)
    first = jnp.where(half == 0, mine, other)
    second = jnp.where(half == 0, other, mine)
    cells8 = jnp.where(row8 < 4, first, pltpu.roll(second, 4, 0)).astype(BF)

    def put(p, carry):
        out_ref[p, pl.ds(2 * S, SLOT - 2 * S), :] = cells8
        return carry

    lax.fori_loop(0, 32, put, 0)
    for source, edges, at_half in ((pos, own_ref, half), (pos ^ 2, other_ref, 1 - half)):
        for e in range(4):
            tile = seam_ref[e, source] // 8

            @pl.when(half_of(tile) == half)
            def _(tile=tile, edges=edges, at_half=at_half, e=e):
                rows = pl.ds(pl.multiple_of(S * at_half, S), S)
                out_ref[place_of(tile), rows, :] = edges[pl.ds(S * e, S), :]


def mlp_rows(normed, cot, out, gain_parts, w_in_ref, b_in_ref, w_out_ref, keep):
    gain, xhat, istd = gain_parts
    dnorm = jnp.zeros(out.shape, F32)
    sums = []
    for n in range(4):
        h = slice(256 * n, 256 * n + 256)
        z = jnp.dot(normed, w_in_ref[:, h], preferred_element_type=F32) + b_in_ref[:, h]
        dact = lax.dot_general(
            cot, w_out_ref[h, :], (((1,), (1,)), ((), ())), preferred_element_type=F32
        )
        z2 = z * z
        half = 0.5 + 0.5 * jnp.tanh(z * (GELU_C + (GELU_C * 0.044715) * z2))
        act = z * half
        slope = half + act * (1.0 - half) * (2 * GELU_C + (6 * GELU_C * 0.044715) * z2)
        act = act.astype(BF)
        dhid = (dact * slope).astype(BF)
        keep(n, act, dhid)
        sums.append(jnp.sum(dhid.astype(F32), axis=0, keepdims=True))
        out = out + jnp.dot(act, w_out_ref[h, :], preferred_element_type=F32)
        dnorm = dnorm + lax.dot_general(
            dhid, w_in_ref[:, h], (((1,), (1,)), ((), ())), preferred_element_type=F32
        )
    dunit = dnorm * gain
    dconv = istd * (
        dunit
        - jnp.mean(dunit, axis=1, keepdims=True)
        - xhat * jnp.mean(dunit * xhat, axis=1, keepdims=True)
    )
    sums.append(jnp.sum(dnorm * xhat, axis=0, keepdims=True))
    sums.append(jnp.sum(dnorm, axis=0, keepdims=True))
    return out.astype(BF), dconv.astype(BF).astype(F32), sums


def norm_rows(rows):
    centred = rows - jnp.mean(rows, axis=1, keepdims=True)
    istd = 1.0 / jnp.sqrt(jnp.mean(centred * centred, axis=1, keepdims=True) + 1e-06)
    return centred * istd, istd


OVER_ROWS = (((0,), (0,)), ((), ()))


def inside_kernel(
    waits,
    field_ref,
    cot_ref,
    kern_ref,
    bias_ref,
    gain_ref,
    shift_ref,
    b_out_ref,
    w_in_ref,
    b_in_ref,
    w_out_ref,
    blocks_ref,
    base_ref,
    grad_ref,
    edge_ref,
    pad_ref,
    xhat_ref,
    istd_ref,
    normed_ref,
    active_ref,
    dhid_ref,
    keep_ref,
    dconv_ref,
):
    center = field_ref[...].astype(F32)
    pad_ref[:, 0] = jnp.zeros((3, S, C), F32)
    pad_ref[:, S + 1] = jnp.zeros((3, S, C), F32)
    pad_ref[1, pl.ds(1, S)] = center
    pad_ref[0, pl.ds(1, S)] = pltpu.roll(center, 1, 1)
    pad_ref[2, pl.ds(1, S)] = pltpu.roll(center, S - 1, 1)

    last = S - 1
    for n, i in enumerate((0, 1, last - 1, last)):
        edge_ref[n] = pad_ref[1, i + 1].astype(BF)
        edge_ref[4 + n] = pad_ref[1, pl.ds(1, S), i, :].astype(BF)
    dconv_ref[...] = cot_ref[...].astype(F32).reshape(S, S, C)
    for n, i in enumerate((0, last)):
        edge_ref[8 + n] = dconv_ref[i].astype(BF)
        edge_ref[10 + n] = dconv_ref[:, i, :].astype(BF)

    bias = bias_ref[...]
    gain = gain_ref[...]
    shift = shift_ref[...]
    b_out = b_out_ref[...]
    rowid = lax.broadcasted_iota(jnp.int32, (256, C), 0)
    col = rowid & (S - 1)

    def forward_rows(b, carry):
        r0 = b * 8
        acc = jnp.zeros((8, S, C), F32) + bias.reshape(1, 1, C)
        for u in range(3):
            for v in range(3):
                k = 3 * u + v
                acc = acc + pad_ref[v, pl.ds(r0 + u, 8)] * kern_ref[k : k + 1, :].reshape(1, 1, C)
        xhat, istd = norm_rows(acc.reshape(8 * S, C))
        q = pl.ds(pl.multiple_of(b * 256, 256), 256)
        xhat_ref[q, :] = xhat
        istd_ref[q, :] = jnp.broadcast_to(istd, (256, 128))
        normed_ref[q, :] = (xhat * gain + shift).astype(BF)
        row = r0 + (rowid >> 5)
        kept = (col > 0) & (col < S - 1) & (row > 0) & (row < S - 1)
        keep_ref[q, :] = jnp.where(kept, cot_ref[q, :].astype(F32), 0.0).astype(BF)
        return carry

    lax.fori_loop(0, 4, forward_rows, 0)
    waits[7]()
    waits[9]()

    def block_rows(b, carry):
        q = pl.ds(pl.multiple_of(b * 256, 256), 256)

        def keep(n, act, dhid):
            active_ref[q, 256 * n : 256 * n + 256] = act
            dhid_ref[q, 256 * n : 256 * n + 256] = dhid

        out = field_ref[pl.ds(b * 8, 8)].reshape(256, C).astype(F32) + b_out
        parts = (gain, xhat_ref[q, :], istd_ref[q, 0:1])
        out, dconv, sums = mlp_rows(
            normed_ref[q, :], keep_ref[q, :], out, parts, w_in_ref, b_in_ref, w_out_ref, keep
        )
        blocks_ref[q, :] = out
        dconv_ref[pl.ds(b * 8, 8)] = dconv.reshape(8, S, C)
        sums.append(jnp.sum(cot_ref[q, :].astype(F32), axis=0, keepdims=True))
        return tuple(a + x for a, x in zip(carry, sums))

    zero = jnp.zeros((1, C), F32)
    *g_bin, g_gain, g_shift, g_bout = lax.fori_loop(0, 4, block_rows, (zero,) * 7)

    for n in range(4):
        h = slice(256 * n, 256 * n + 256)
        dot = functools.partial(lax.dot_general, dimension_numbers=OVER_ROWS, preferred_element_type=F32)
        g = dot(normed_ref[...], dhid_ref[:, h])
        grad_ref[4 * n : 4 * n + 4, pl.ds(0, 64), :] = g.reshape(4, 64, C)
        g = dot(active_ref[:, h], keep_ref[...])
        grad_ref[16 + 4 * n : 20 + 4 * n, pl.ds(0, 64), :] = g.reshape(4, 64, C)

    g_kernel = []
    for u in range(3):
        for v in range(3):

            def tap_rows(b, acc, u=u, v=v):
                part = pad_ref[v, pl.ds(b * 4 + u, 4)] * dconv_ref[pl.ds(b * 4, 4)]
                return acc + jnp.sum(part.reshape(4 * S // 8, 8, C), axis=0)

            acc = lax.fori_loop(0, 8, tap_rows, jnp.zeros((8, C), F32))
            g_kernel.append(jnp.sum(acc, axis=0, keepdims=True))

    def bias_rows(b, acc):
        return acc + jnp.sum(dconv_ref[pl.ds(b * 4, 4)].reshape(4 * S // 8, 8, C), axis=0)

    g_bias = jnp.sum(lax.fori_loop(0, 8, bias_rows, jnp.zeros((8, C), F32)), axis=0, keepdims=True)

    small = g_kernel + [g_bias, g_gain, g_shift, g_bout] + g_bin + [zero] * 15
    row8 = lax.broadcasted_iota(jnp.int32, (CHUNK - 64, C), 0)
    for j in range(32):
        grad_ref[j, pl.ds(64, CHUNK - 64), :] = jnp.where(row8 == 0, small[j], 0.0)

    def shift_rows(i, carry):
        row = dconv_ref[i]
        pad_ref[1, i + 1] = row
        pad_ref[0, i + 1] = pltpu.roll(row, S - 1, 0)
        pad_ref[2, i + 1] = pltpu.roll(row, 1, 0)
        return carry

    lax.fori_loop(0, S, shift_rows, 0)
    taps = [kern_ref[k : k + 1, :].reshape(1, 1, C) for k in range(9)]

    def inner_rows(b, carry):
        q = pl.ds(pl.multiple_of(b * 4 * S, 4 * S), 4 * S)
        acc = cot_ref[q, :].astype(F32).reshape(4, S, C)
        for u in range(3):
            for v in range(3):
                acc = acc + pad_ref[v, pl.ds(b * 4 + 2 - u, 4)] * taps[3 * u + v]
        base_ref[pl.ds(b * 4, 4)] = acc
        return carry

    lax.fori_loop(0, 8, inner_rows, 0)


def put_rim(d_lines, kern_ref, lines_ref, rim_ref):
    last = S - 1
    spot = lambda line, i: line[i : i + 1]
    place = lax.broadcasted_iota(jnp.int32, (S, C), 0)
    flat = lambda k: kern_ref[k : k + 1, :]

    def spread(line, taps):
        back = jnp.where(place == last, 0.0, pltpu.roll(line, last, 0))
        ahead = jnp.where(place == 0, 0.0, pltpu.roll(line, 1, 0))
        return back * flat(taps[0]) + line * flat(taps[1]) + ahead * flat(taps[2])

    def whole(line, at):
        line = jnp.where(place == 0, spot(d_lines[0], at), line)
        return jnp.where(place == last, spot(d_lines[1], at), line)

    row_taps = lambda u: (3 * u, 3 * u + 1, 3 * u + 2)
    col_taps = lambda v: (v, 3 + v, 6 + v)
    rim = [
        spread(d_lines[0], row_taps(0)),
        spread(d_lines[1], row_taps(2)),
        spread(whole(d_lines[2], 0), col_taps(0)),
        spread(whole(d_lines[3], last), col_taps(2)),
    ]
    corners = [
        spot(d_lines[0], 0) * flat(0),
        spot(d_lines[0], last) * flat(2),
        spot(d_lines[1], 0) * flat(6),
        spot(d_lines[1], last) * flat(8),
    ]
    put_edges(rim_ref, rim, corners)
    lines_ref[0] = spread(d_lines[0], row_taps(1))
    lines_ref[1] = spread(d_lines[0], row_taps(2))
    lines_ref[2] = spread(d_lines[1], row_taps(0))
    lines_ref[3] = spread(d_lines[1], row_taps(1))
    lines_ref[4] = spread(d_lines[2], col_taps(1))
    lines_ref[5] = spread(d_lines[2], col_taps(2))
    lines_ref[6] = spread(d_lines[3], col_taps(0))
    lines_ref[7] = spread(d_lines[3], col_taps(1))


def border_kernel(
    waits,
    pos_ref,
    seam_ref,
    corner_ref,
    edge_ref,
    recv_ref,
    kern_ref,
    bias_ref,
    gain_ref,
    shift_ref,
    b_out_ref,
    w_in_ref,
    b_in_ref,
    w_out_ref,
    grad_ref,
    rows_ref,
    lines_ref,
    rim_ref,
    own_ref,
    send_ref,
):
    pos = pos_ref[0]
    core = pos % 2
    strips, cells = take_slots(recv_ref, pos, seam_ref, corner_ref)
    top, bottom, left, right = strips
    last = S - 1
    order = {0: 0, 1: 1, last - 1: 2, last: 3}
    at_row = lambda i: edge_ref[order[i]].astype(F32)
    at_col = lambda j: edge_ref[4 + order[j]].astype(F32)
    spot = lambda line, i: line[i : i + 1]
    place = lax.broadcasted_iota(jnp.int32, (S, C), 0)
    flat = lambda k: kern_ref[k : k + 1, :]

    bands = [
        (
            (top, at_row(0), at_row(1)),
            ((cells[0], cells[1]), (spot(left, 0), spot(right, 0)), (spot(left, 1), spot(right, 1))),
            lambda a, s: 3 * a + s,
        ),
        (
            (bottom, at_row(last), at_row(last - 1)),
            (
                (cells[2], cells[3]),
                (spot(left, last), spot(right, last)),
                (spot(left, last - 1), spot(right, last - 1)),
            ),
            lambda a, s: 3 * (2 - a) + s,
        ),
        (
            (left, at_col(0), at_col(1)),
            ((cells[0], cells[2]), (spot(top, 0), spot(bottom, 0)), (spot(top, 1), spot(bottom, 1))),
            lambda a, s: 3 * s + a,
        ),
        (
            (right, at_col(last), at_col(last - 1)),
            (
                (cells[1], cells[3]),
                (spot(top, last), spot(bottom, last)),
                (spot(top, last - 1), spot(bottom, last - 1)),
            ),
            lambda a, s: 3 * s + 2 - a,
        ),
    ]
    windows = [[None] * 9 for _ in range(4)]
    rows = []
    for n, (lines, ends, tap) in enumerate(bands):
        acc = jnp.zeros((S, C), F32) + bias_ref[...]
        for a in range(3):
            before = jnp.where(place == 0, ends[a][0], pltpu.roll(lines[a], 1, 0))
            after = jnp.where(place == last, ends[a][1], pltpu.roll(lines[a], last, 0))
            for s, window in enumerate((before, lines[a], after)):
                k = tap(a, s)
                windows[n][k] = window
                acc = acc + window * flat(k)
        rows.append(acc)
    field_rows = jnp.concatenate([lines[1] for lines, _, _ in bands], axis=0)
    once = (place > 0) & (place < last)
    cot_rows = jnp.concatenate(
        [edge_ref[8].astype(F32), edge_ref[9].astype(F32)]
        + [jnp.where(once, edge_ref[n].astype(F32), 0.0) for n in (10, 11)],
        axis=0,
    ).astype(BF)

    gain = gain_ref[...]
    waits[10]()
    waits[12]()
    xhat, istd = norm_rows(jnp.concatenate(rows, axis=0))
    normed = (xhat * gain + shift_ref[...]).astype(BF)
    kept = []
    out, dconv, sums = mlp_rows(
        normed,
        cot_rows,
        field_rows + b_out_ref[...],
        (gain, xhat, istd),
        w_in_ref,
        b_in_ref,
        w_out_ref,
        lambda n, act, dhid: kept.append((act, dhid)),
    )
    rows_ref[...] = out
    *g_bin, g_gain, g_shift = sums
    d_lines = [dconv[S * n : S * n + S] for n in range(4)]

    put_rim(d_lines, kern_ref, lines_ref, rim_ref)

    waits[13]()

    def put_rows(first, value):
        mine = core == first // 16
        base = first % 16
        value = value.reshape(4, 64, C) + grad_ref[first : first + 4, pl.ds(0, 64), :]

        @pl.when(mine)
        def _():
            own_ref[pl.ds(base, 4), pl.ds(0, 64), :] = value

        @pl.when(jnp.logical_not(mine))
        def _():
            send_ref[pl.ds(base, 4), pl.ds(0, 64), :] = value.astype(BF)

    for n in range(4):
        act, dhid = kept[n]
        put_rows(4 * n, lax.dot_general(normed, dhid, OVER_ROWS, preferred_element_type=F32))
        put_rows(16 + 4 * n, lax.dot_general(act, cot_rows, OVER_ROWS, preferred_element_type=F32))

    g_kernel = []
    for k in range(9):
        acc = sum(windows[n][k] * d_lines[n] for n in range(4))
        g_kernel.append(jnp.sum(acc, axis=0, keepdims=True))
    zero = jnp.zeros((1, C), F32)
    g_bias = jnp.sum(dconv, axis=0, keepdims=True)
    small = g_kernel + [g_bias, g_gain, g_shift, zero] + g_bin + [zero] * 15
    row8 = lax.broadcasted_iota(jnp.int32, (CHUNK - 64, C), 0)
    for j in range(32):
        row = jnp.where(row8 == 0, small[j], 0.0) + grad_ref[j, pl.ds(64, CHUNK - 64), :]

        @pl.when(core == j // 16)
        def _(row=row, j=j):
            own_ref[j % 16, pl.ds(64, CHUNK - 64), :] = row

        @pl.when(core != j // 16)
        def _(row=row, j=j):
            send_ref[j % 16, pl.ds(64, CHUNK - 64), :] = row.astype(BF)


def patch_kernel(waits, part_ref, rows_ref, blocks_ref, wide_ref):
    last = S - 1
    wide_ref[...] = part_ref[...].astype(F32)
    rows = rows_ref[...].astype(F32)
    wide_ref[:, 0, :] = rows[2 * S : 3 * S]
    wide_ref[:, last, :] = rows[3 * S : 4 * S]
    wide_ref[0] = rows[0:S]
    wide_ref[last] = rows[S : 2 * S]
    blocks_ref[...] = wide_ref[...].astype(BF)


def join_kernel(
    waits, pos_ref, seam_ref, corner_ref, base_ref, lines_ref, recv_ref, out_ref, acc_ref
):
    strips, cells = take_slots(recv_ref, pos_ref[0], seam_ref, corner_ref)
    last = S - 1
    acc_ref[...] = base_ref[...]
    for i, add in (
        (0, strips[0] + lines_ref[0]),
        (1, lines_ref[1]),
        (last - 1, lines_ref[2]),
        (last, strips[1] + lines_ref[3]),
    ):
        acc_ref[i] = acc_ref[i] + add
    for j, add in (
        (0, strips[2] + lines_ref[4]),
        (1, lines_ref[5]),
        (last - 1, lines_ref[6]),
        (last, strips[3] + lines_ref[7]),
    ):
        acc_ref[:, j, :] = acc_ref[:, j, :] + add
    for n, (i, j) in enumerate(((0, 0), (0, last), (last, 0), (last, last))):
        acc_ref[i, pl.ds(j, 1), :] = acc_ref[i, pl.ds(j, 1), :] + cells[n]
    out_ref[...] = acc_ref[...].astype(BF)


def scale_kernel(
    waits, at_ref, own_ref, other_ref, kern_ref, chan_ref, w_in_ref, b_in_ref, w_out_ref, entries
):
    core = at_ref[0] % 2
    halves = (own_ref, other_ref)
    sums = []
    for half in range(2):
        def one_half(j, acc, half=half):
            v = jnp.where(core == half, own_ref[j].astype(F32), other_ref[j].astype(F32))
            return acc + jnp.sum((v * v).reshape(CHUNK // 8, 8, C), axis=0)

        sums.append(lax.fori_loop(0, 16, one_half, jnp.zeros((8, C), F32)))
    total = jnp.sum(jnp.sum(sums[0] + sums[1], axis=0, keepdims=True), axis=1, keepdims=True)
    scale = 1.0 / jnp.sqrt(total / entries + 1e-06)

    for j in range(32):
        c, k = j // 16, j % 16
        if j == 16:
            waits["flush"](2)

        def emit(ref, j=j, k=k):
            rows = ref[k, pl.ds(0, 64), :].astype(F32) * scale
            if j < 16:
                w_in_ref[64 * (j % 4) : 64 * (j % 4) + 64, 256 * (j // 4) : 256 * (j // 4) + 256] = rows
            else:
                w_out_ref[64 * (j - 16) : 64 * (j - 16) + 64, :] = rows
            row = ref[k, pl.ds(64, 8), :].astype(F32)[0:1] * scale
            if j < 9:
                kern_ref[j : j + 1, :] = row
            elif j < 13:
                chan_ref[j - 9 : j - 8, :] = row
            elif j < 17:
                b_in_ref[:, 256 * (j - 13) : 256 * (j - 13) + 256] = row

        for near in range(2):

            @pl.when((core == c) == (near == 1))
            def _(emit=emit, near=near):
                emit(halves[1 - near])


def at(y, x, h, c):
    return ((y * 4 + x) * 2 + h) * 2 + c


def moves(axis, d):
    pairs = []
    for y in range(4):
        for x in range(4):
            for h in range(2):
                for c in range(2):
                    to = {
                        "y": ((y + d) % 4, x, h, c),
                        "x": (y, (x + d) % 4, h, c),
                        "h": (y, x, 1 - h, c),
                        "c": (y, x, h, 1 - c),
                    }[axis]
                    pairs.append((at(y, x, h, c), at(*to)))
    return pairs


def exchange(slots):
    halves = [[at(p // 8, p // 2 % 4, h, p % 2) for p in range(32)] for h in range(2)]
    return lax.all_to_all(slots, "space", 0, 0, axis_index_groups=halves, tiled=True)


def plane(slots):
    planes = [
        [at(p % 4, p // 4, h, c) for p in range(16)] for h in range(2) for c in range(2)
    ]
    return lax.all_to_all(slots, "space", 0, 0, axis_index_groups=planes, tiled=True)


def sum_over_devices(own, send, slots):
    other = lax.ppermute(send, "space", moves("c", 1))
    rest = (own + other.astype(F32)).astype(BF)
    parts = plane(rest)
    piece = lax.optimization_barrier(jnp.sum(parts.astype(F32), axis=0))
    back = exchange(slots)
    mine = piece.astype(BF)
    other = lax.ppermute(mine, "space", moves("h", 1))
    piece = mine.astype(F32) + other.astype(F32)
    turn = lambda d: [(i, (i + d) % 4) for i in range(4)]
    mine = piece.astype(BF)
    got = [mine] + [lax.ppermute(mine, "batch", turn(d)) for d in (1, 2, 3)]
    got = [g.astype(F32) for g in got]
    piece = (got[0] + got[2]) + (got[1] + got[3])
    spread = jnp.broadcast_to(piece.astype(BF)[None], (16, CHUNK, C))
    spread, back = lax.optimization_barrier((spread, back))
    full = plane(spread)
    return full, lax.ppermute(full, "space", moves("c", 1)), back


def shards(
    fields,
    cotangent,
    dw_kernel,
    dw_bias,
    ln_gain,
    ln_shift,
    w_in,
    b_in,
    w_out,
    b_out,
    seam_links,
    corner_links,
):
    here = lax.axis_index("space").reshape(1)
    links, diagonals = seam_links.T, corner_links.T
    field = fields[0, 0]
    cot = cotangent[0, 0]
    sds = jax.ShapeDtypeStruct
    edges = sds((EDGE, C), BF)
    wide = pltpu.VMEM((S, S, C), F32)

    def to_slots(mine):
        other = lax.ppermute(mine, "space", moves("h", 1))
        return staged_call(
            slot_kernel,
            [(here, "smem", 0), (links, "smem", 0), (mine, "vmem", 0), (other, "vmem", 0)],
            [(sds((32, SLOT, C), BF), True)],
            [],
            63,
        )[0]

    (field_edges,) = staged_call(edge_kernel, [(field, "vmem", 0)], [(edges, True)], [wide], 63)
    halo = exchange(to_slots(field_edges))

    cells = S * S
    row = lambda v: (v.reshape(1, -1), "vmem", 0)
    weights = [
        (dw_kernel, "vmem", 0),
        row(dw_bias),
        row(ln_gain),
        row(ln_shift),
        row(b_out),
        (w_in, "vmem", 1),
        row(b_in),
        (w_out, "vmem", 1),
    ]
    part, base, grads, border_lines = staged_call(
        inside_kernel,
        [(field, "vmem", 0), (cot.reshape(cells, C), "vmem", 0)] + weights,
        [
            (sds((cells, C), BF), True),
            (sds((S, S, C), F32), True),
            (sds((32, CHUNK, C), F32), True),
            (sds((12, S, C), BF), True),
        ],
        [
            pltpu.VMEM((3, S + 2, S, C), F32),
            pltpu.VMEM((cells, C), F32),
            pltpu.VMEM((cells, 128), F32),
            pltpu.VMEM((cells, C), BF),
            pltpu.VMEM((cells, H), BF),
            pltpu.VMEM((cells, H), BF),
            pltpu.VMEM((cells, C), BF),
            wide,
        ],
        63,
        pl.CostEstimate(
            flops=12 * cells * C * H, bytes_accessed=8 << 20, transcendentals=cells * H
        ),
    )
    where = [(here, "smem", 0), (links, "smem", 0), (diagonals, "smem", 0)]
    border_rows, lines, rim, own, send = staged_call(
        border_kernel,
        where
        + [(border_lines, "vmem", 0), (halo, "vmem", 0)]
        + weights
        + [(grads, "vmem", 1)],
        [
            (sds((4 * S, C), BF), True),
            (sds((8, S, C), F32), True),
            (edges, True),
            (sds((16, CHUNK, C), F32), True),
            (sds((16, CHUNK, C), BF), True),
        ],
        [],
        63,
    )
    (blocks,) = staged_call(
        patch_kernel,
        [(part.reshape(S, S, C), "vmem", 0), (border_rows, "vmem", 0)],
        [(sds((S, S, C), BF), True)],
        [wide],
        63,
    )
    near, far, back = sum_over_devices(own, send, to_slots(rim))
    (grad_tile,) = staged_call(
        join_kernel,
        where + [(base, "vmem", 0), (lines, "vmem", 0), (back, "here", 0)],
        [(sds((S, S, C), BF), True)],
        [wide],
        10,
    )
    entries = 13 * C + 2 * C * H + H
    grad_kernel, grad_channels, grad_w_in, grad_b_in, grad_w_out = staged_call(
        functools.partial(scale_kernel, entries=entries),
        [(here, "smem", 0), (near, "here", 0), (far, "here", 0)],
        [
            (sds((9, C), F32), True),
            (sds((4, C), F32), True),
            (sds((C, H), F32), True),
            (sds((1, H), F32), True),
            (sds((H, C), F32), True),
        ],
        [],
        10,
    )
    return (
        blocks[None, None],
        grad_tile[None, None],
        grad_kernel,
        grad_channels,
        grad_w_in,
        grad_b_in.reshape(H),
        grad_w_out,
    )


def solution(mesh):
    tile = P("batch", "space", None, None, None)

    return jax.shard_map(
        shards,
        mesh=mesh,
        in_specs=(tile, tile) + (P(),) * 10,
        out_specs=(tile, tile) + (P(),) * 5,
        check_vma=False,
    )
```
